32 devices in a mesh: energy: 8 (over z, x), slab: 2 (over core), rep: 2 (over y).
Axes of the slice: x: 2, y: 2, z: 4, core: 2. Of those that a mesh axis runs over, the one named last changes fastest.
Arguments:
- green_blocks: bfloat16 [8, 2, 512, 512], P('energy', 'slab', 'rep'), may hold values from -1 to 1
- occupation: float32 [8], P('energy'), may hold values from 0.1 to 1
- offsets: int32 [2], replicated, may hold values from 1 to 4, as said below
- coulomb: float32 [2, 512, 512], P('slab', 'rep'), may hold values from -0.9 to 0.9
- hamiltonian: float32 [2, 512, 512], P('slab', 'rep'), may hold values from -0.25 to 0.25
- onsite_level: float32 [8], P('energy'), may hold values from 2 to 3
- green_steps: int32 [8], P('energy'), may hold values from 1 to 2, as said below
- screen_steps: int32 [2], replicated, may hold values from 0 to 2, as said below
Outputs:
- green_next: float32 [8, 2, 512, 512], P('energy', 'slab', 'rep')
- screened: bfloat16 [2, 2, 512, 512], P(None, 'slab', 'rep')
The draws below stay inside these ranges and needn't reach their ends.
Inputs may be any that keep to these rules, and one draw needn't show every extreme that they name: `offsets`: some frequency has offset 4; every other frequency has a smaller one. `green_steps`: some energy takes 2 turns. `screen_steps`: some frequency takes 2 turns; every other frequency takes fewer.
All inputs are finite; a program needn't handle non-finite values.
Results may differ from the reference program's by a relative error of at most 0.0004.
Values may be sent and summed in bfloat16 or wider, within the bound.
No kernel may reach another device: no remote copies, remote signals or barrier semaphores. Data moves between devices by JAX's collectives and lax.ppermute only.
A program may use at most 64 MiB of HBM per device.

```python
import math
import jax
import jax.numpy as jnp
from jax import lax

B = 512
SHIFTS = 4
FREQS = 2
NG = 2
NW = 2
E = 8
S = 2


def draw_offsets(key, part):
    own_key = jax.random.fold_in(key, 101)
    values = jax.random.randint(own_key, (FREQS,), 1, SHIFTS)
    place = jax.random.randint(jax.random.fold_in(own_key, 1), (), 0, FREQS)
    return values.at[place].set(SHIFTS).astype(jnp.int32)


def draw_green_steps(key, part):
    own_key = jax.random.fold_in(key, 202)
    values = jax.random.randint(own_key, (E,), 1, NG + 1)
    place = jax.random.randint(jax.random.fold_in(own_key, 1), (), 0, E)
    return values.at[place].set(NG).astype(jnp.int32)


def draw_screen_steps(key, part):
    own_key = jax.random.fold_in(key, 303)
    values = jax.random.randint(own_key, (FREQS,), 0, NW)
    place = jax.random.randint(jax.random.fold_in(own_key, 1), (), 0, FREQS)
    return values.at[place].set(NW).astype(jnp.int32)


def levels(key, shape, pieces, smallest, largest):
    def one(dim, blocks):
        steps = jax.random.uniform(jax.random.fold_in(jax.random.fold_in(key, 6), dim), (blocks,), jnp.float32, smallest / len(pieces), largest / len(pieces))
        return jnp.repeat(jnp.exp(steps), shape[dim] // blocks).reshape((-1,) + (1,) * (len(shape) - dim - 1))

    loudness = one(*pieces[0])
    for cut in pieces[1:]:
        loudness = loudness * one(*cut)
    return loudness


def noise(stream_key, extent, width, bound, split=(), kind=jnp.bfloat16):
    level = levels(stream_key, extent, split, -0.22, 0.18) if split else 1.0
    array = jax.random.normal(stream_key, extent, jnp.float32) * width * level
    return jnp.minimum(jnp.maximum(array, -bound), bound).astype(kind)


def setup_inputs(seed: int = 0) -> dict:
    key_of = jax.random.split(jax.random.key(seed), 9)
    green_blocks = jnp.clip(jax.random.uniform(key_of[0], (E, S, B, B), jnp.float32, -1.0, 1.0) * levels(key_of[0], (E, S, B, B), ((0, 8), (1, 2), (2, 2)), -0.4, 0.0), -1.0, 1.0).astype(jnp.bfloat16)
    occupation = jnp.clip(jnp.exp(math.log(1.0) - 2.3025851 * jax.random.uniform(key_of[1], (E,), jnp.float32) ** levels(key_of[1], (E,), ((0, 8),), -0.2, 0.2)), 0.1, 1.0)
    offsets = draw_offsets(jax.random.fold_in(key_of[8], 71), 0)
    coulomb = jnp.clip(jax.random.uniform(key_of[3], (S, B, B), jnp.float32, -0.9, 0.9) * levels(key_of[3], (S, B, B), ((0, 2), (1, 2)), -0.4, 0.0), -0.9, 0.9)
    hamiltonian = noise(key_of[4], (S, B, B), B ** -0.5, 0.25, ((0, 2), (1, 2)), jnp.float32)
    onsite_level = jnp.clip(2.0 + 1.0 * jax.random.uniform(key_of[5], (E,), jnp.float32) ** levels(key_of[5], (E,), ((0, 8),), -0.2, 0.2), 2.0, 3.0)
    green_steps = draw_green_steps(jax.random.fold_in(key_of[8], 71), 0)
    screen_steps = draw_screen_steps(jax.random.fold_in(key_of[8], 71), 0)
    return dict(green_blocks=green_blocks, occupation=occupation, offsets=offsets, coulomb=coulomb, hamiltonian=hamiltonian, onsite_level=onsite_level, green_steps=green_steps, screen_steps=screen_steps)


precise = lax.Precision.HIGHEST


def newton_solve(operator, initial, count, turn_total):
    iterate = initial
    for turn_index in range(turn_total):
        applied = jnp.matmul(operator, iterate, precision=precise)
        composed = jnp.matmul(iterate, applied, precision=precise)
        iterate = jnp.where(turn_index < count, 2.0 * iterate - composed, iterate)
    return iterate


def reference(green_blocks, occupation, offsets, coulomb, hamiltonian, onsite_level, green_steps, screen_steps):
    energies = green_blocks.shape[0]
    front = jnp.zeros((SHIFTS,) + green_blocks.shape[1:], green_blocks.dtype)
    padded = jnp.concatenate([front, green_blocks], axis=0)
    slab_padded = jnp.pad(green_blocks, ((0, 0), (1, 1), (0, 0), (0, 0)))
    identity = jnp.eye(B, dtype=jnp.float32)
    entry_scale = B ** -0.5

    def lowered_at(energy):
        blocks = [lax.dynamic_index_in_dim(padded, energy + SHIFTS - offsets[index], 0, keepdims=False) for index in range(FREQS)]
        return jnp.stack(blocks).astype(jnp.float32)

    def accumulate(total, energy):
        current = lax.dynamic_index_in_dim(green_blocks, energy, 0, keepdims=False).astype(jnp.float32)
        weighted = occupation[energy] * current
        return total + weighted[None] * lowered_at(energy), None

    zeros_total = jnp.zeros((FREQS,) + green_blocks.shape[1:], jnp.float32)
    polarization, _ = lax.scan(accumulate, zeros_total, jnp.arange(energies, dtype=jnp.int32))
    polarization = polarization * (energies ** -0.5)

    def screen_one(polar_slabs, count):
        operator = identity + entry_scale * coulomb * polar_slabs
        initial = jnp.broadcast_to(identity, operator.shape)
        inverse = newton_solve(operator, initial, count, NW)
        return jnp.matmul(coulomb, inverse, precision=precise).astype(jnp.bfloat16)

    screened = jnp.stack([screen_one(polarization[index], screen_steps[index]) for index in range(FREQS)])

    def solve_energy(energy):
        lowered = lowered_at(energy)
        self_energy = jnp.sum(lowered * screened.astype(jnp.float32), axis=0) * entry_scale
        beside_all = lax.dynamic_index_in_dim(slab_padded, energy, 0, keepdims=False)
        contact = (beside_all[:-2].astype(jnp.float32) + beside_all[2:].astype(jnp.float32)) * (0.5 * entry_scale)
        dyson = onsite_level[energy] * identity + hamiltonian - self_energy - contact
        diagonal = jnp.diagonal(dyson, axis1=1, axis2=2)
        initial = identity[None] * (1.0 / diagonal)[:, None, :]
        return newton_solve(dyson, initial, green_steps[energy], NG)

    green_next = lax.map(solve_energy, jnp.arange(energies, dtype=jnp.int32))
    return green_next, screened
```

```python
import jax
import jax.numpy as jnp
from jax import lax
from jax.sharding import PartitionSpec as P

SHIFTS = 4
FREQS = 2

coded = jnp.float16
near = lax.Precision.HIGH


def shifted(block, axis, distance):
    count = lax.axis_size(axis)
    route = [(i, i + distance) for i in range(count - distance)]
    return lax.ppermute(block, axis, route)


def product(first, second):
    return lax.dot_general(
        first, second, (((1,), (0,)), ((), ())), precision=near,
        preferred_element_type=jnp.float32,
    )


def lowered_blocks(block, offsets):
    two = shifted(block, "energy", 2)
    four = shifted(two, "energy", 2)
    other = jnp.min(offsets)
    odd = shifted(jnp.where(other == 3, two, block), "energy", 1)
    less = jnp.where(other == 2, two, odd)
    return [jnp.where(offsets[f] == SHIFTS, four, less) for f in range(FREQS)]


def split3(value):
    high = lax.reduce_precision(value, 8, 7)
    middle = lax.reduce_precision(value - high, 8, 7)
    return high, middle, value - high - middle


def every_energy(block, weight):
    energies = lax.axis_size("energy")
    rows, width = block.shape
    share = rows // energies
    parts = jnp.stack([w.astype(block.dtype) for w in split3(weight)])
    extra = jnp.zeros((energies, 8, width), block.dtype).at[:, :3, :].set(
        jnp.broadcast_to(parts[None, :, None], (energies, 3, width))
    )
    sent = jnp.concatenate([block.reshape(energies, share, width), extra], axis=1)
    got = lax.all_to_all(sent, "energy", 0, 0, tiled=True)
    tail = got[:, share:share + 3, :].astype(jnp.float32)
    return got[:, :share, :], tail[:, 0:1] + tail[:, 1:2] + tail[:, 2:3]


def gather_energy(chunk):
    energies = lax.axis_size("energy")
    if energies % 2 or energies > 16:
        return lax.all_gather(chunk, "energy", axis=0)
    outer = energies // 2
    here = lax.axis_index("energy") // 2
    whole = jnp.zeros((outer,) + chunk.shape, chunk.dtype)
    whole = lax.dynamic_update_index_in_dim(whole, chunk, here, 0)
    for k in range(1, outer):
        route = [(z * 2 + x, (z + k) % outer * 2 + x) for z in range(outer) for x in range(2)]
        got = lax.ppermute(chunk, "energy", route)
        whole = lax.dynamic_update_index_in_dim(whole, got, (here - k) % outer, 0)
    return whole


def gather_square(part):
    energies = lax.axis_size("energy")
    swap = [(e, e ^ 1) for e in range(energies)]
    turn = [(0, 1), (1, 0)]
    cross = [(e * 2 + r, (e ^ 1) * 2 + 1 - r) for e in range(energies) for r in range(2)]
    beside = lax.ppermute(part, "energy", swap)
    above = lax.ppermute(part, "rep", turn)
    apart = lax.ppermute(part, ("energy", "rep"), cross)
    first_x = lax.axis_index("energy") % 2 == 0
    first_y = lax.axis_index("rep") == 0

    def paired(own, other):
        return jnp.stack([jnp.where(first_x, own, other), jnp.where(first_x, other, own)], axis=1)

    mine = paired(part, beside)
    theirs = paired(above, apart)
    return jnp.stack([jnp.where(first_y, mine, theirs), jnp.where(first_y, theirs, mine)])


def gather_rows(chunk):
    energies = lax.axis_size("energy")
    freqs, share, width = chunk.shape
    if energies % 2 or energies > 16 or lax.axis_size("rep") != 2:
        whole = lax.all_gather(chunk, ("rep", "energy"), axis=1, tiled=True)
        return whole
    whole = gather_square(gather_energy(chunk))
    whole = jnp.moveaxis(whole, 3, 0)
    return whole.reshape(freqs, -1, width)


def body(
    green_blocks, occupation, offsets, coulomb, hamiltonian, onsite_level, green_steps, screen_steps
):
    green = green_blocks[0, 0]
    bare = coulomb[0]
    rows, width = green.shape
    energies = lax.axis_size("energy")
    share = rows // energies
    entry_scale = width ** (-0.5)
    place = lax.axis_index("energy")
    rep_start = lax.axis_index("rep") * rows

    everything, weights = every_energy(green, occupation[0])
    wide = everything.astype(jnp.float32)
    weighted = wide * weights
    padded = jnp.concatenate([jnp.zeros((SHIFTS,) + wide.shape[1:], wide.dtype), wide], axis=0)
    bare_share = lax.dynamic_slice_in_dim(bare, place * share, share, 0)
    chunks = []
    for f in range(FREQS):
        low = lax.dynamic_slice_in_dim(padded, SHIFTS - offsets[f], energies, 0)
        polar = jnp.sum(weighted * low, axis=0) * energies ** (-0.5)
        chunks.append(-entry_scale * bare_share * polar)
    ratio = gather_rows(jnp.stack(chunks).astype(coded)).astype(jnp.float32)

    lowered = lowered_blocks(green, offsets)
    slabs = lax.axis_size("slab")
    if slabs == 2:
        beside = lax.ppermute(green, "slab", [(0, 1), (1, 0)]).astype(jnp.float32)
    else:
        up = [(i, i + 1) for i in range(slabs - 1)]
        down = [(j, i) for i, j in up]
        beside = lax.ppermute(green, "slab", up).astype(jnp.float32) + lax.ppermute(
            green, "slab", down
        ).astype(jnp.float32)

    once = [bare + product(bare, ratio[f]) for f in range(FREQS)]
    twice_at = jnp.argmax(screen_steps)
    ratio_twice = lax.dynamic_index_in_dim(ratio, twice_at, 0, keepdims=False)
    once_twice = jnp.where(twice_at == 0, once[0], once[1])
    twice = once_twice + product(product(once_twice, ratio_twice), ratio_twice)
    screened = jnp.stack(
        [
            jnp.where(
                screen_steps[f] == 0, bare, jnp.where(screen_steps[f] == 1, once[f], twice)
            )
            for f in range(FREQS)
        ]
    ).astype(jnp.bfloat16)

    energy_terms = sum(
        lowered[f].astype(jnp.float32) * screened[f].astype(jnp.float32) for f in range(FREQS)
    )
    rest = hamiltonian[0] - entry_scale * energy_terms - (0.5 * entry_scale) * beside
    col_index = lax.broadcasted_iota(jnp.int32, (rows, width), 1)
    row_index = lax.broadcasted_iota(jnp.int32, (rows, width), 0) + rep_start
    on_diagonal = col_index == row_index
    level = onsite_level[0]
    diagonal = level + jnp.sum(jnp.where(on_diagonal, rest, 0.0), axis=1, keepdims=True)
    off = jnp.where(on_diagonal, 0.0, rest)
    largest = jnp.max(jnp.abs(off), axis=1, keepdims=True)
    largest = jnp.where(largest > 0.0, largest, 1.0)
    unit = off / largest
    factor = -largest / diagonal
    inverse = 1.0 / diagonal
    factor_row = jnp.sum(jnp.where(on_diagonal, factor, 0.0), axis=0)
    inverse_row = jnp.sum(jnp.where(on_diagonal, inverse, 0.0), axis=0)
    turn = [(0, 1), (1, 0)]
    vectors = jnp.stack([factor_row, inverse_row])
    if lax.axis_size("rep") == 2:
        vectors = vectors + lax.ppermute(vectors, "rep", turn)
        mine = unit.astype(coded)
        theirs = lax.ppermute(mine, "rep", turn)
        first = lax.axis_index("rep") == 0
        full = jnp.concatenate(
            [jnp.where(first, mine, theirs), jnp.where(first, theirs, mine)], axis=0
        ).astype(jnp.float32)
    else:
        vectors = lax.psum(vectors, "rep")
        full = lax.all_gather(unit.astype(coded), "rep", axis=0, tiled=True).astype(jnp.float32)
    factors, inverses = vectors[0:1], vectors[1:2]
    step = unit * factor
    square = product(step * factors, full)
    cube = product(square * factors, full)
    near_one = jnp.where(on_diagonal, 1.0, step)
    total = near_one + jnp.where(green_steps[0] >= 2, square + cube, 0.0)
    return (total * inverses)[None, None], screened[:, None]


def solution(mesh):
    return jax.shard_map(
        body,
        mesh=mesh,
        in_specs=(
            P("energy", "slab", "rep", None),
            P("energy"),
            P(),
            P("slab", "rep", None),
            P("slab", "rep", None),
            P("energy"),
            P("energy"),
            P(),
        ),
        out_specs=(P("energy", "slab", "rep", None), P(None, "slab", "rep", None)),
        check_vma=False,
    )
```

```python
import jax
import jax.numpy as jnp
from jax import lax
from jax.experimental import pallas as pl
from jax.experimental.pallas import tpu as pltpu
from jax.sharding import PartitionSpec as P

SHIFTS = 4
FREQS = 2
EXTRA = 8

coded = jnp.float16
VMEM = pltpu.VMEM
in_vmem = pl.BlockSpec(memory_space=pltpu.VMEM)
in_smem = pl.BlockSpec(memory_space=pltpu.SMEM)
in_place = pl.BlockSpec(memory_space=pl.ANY)


def halves(value):
    high = value.astype(jnp.bfloat16)
    return high, (value - high.astype(jnp.float32)).astype(jnp.bfloat16)


def dot(first, second):
    return jnp.dot(first, second, preferred_element_type=jnp.float32)


def product(first, high, low):
    top, rest = halves(first)
    return dot(top, high) + dot(top, low) + dot(rest, high)


def shifted(block, axis, distance):
    count = lax.axis_size(axis)
    route = [(i, i + distance) for i in range(count - distance)]
    return lax.ppermute(block, axis, route)


def prepare_kernel(weight_ref, block_ref, out_ref):
    energies, padded, width = out_ref.shape
    share = padded - EXTRA
    weight = jnp.full((EXTRA, width), weight_ref[0], jnp.float32)
    first = weight.astype(jnp.bfloat16).astype(jnp.float32)
    second = (weight - first).astype(jnp.bfloat16).astype(jnp.float32)
    third = weight - first - second
    row = lax.broadcasted_iota(jnp.int32, (EXTRA, width), 0)
    tail = jnp.where(row == 0, first, jnp.where(row == 1, second, third)).astype(jnp.bfloat16)
    for k in range(energies):
        out_ref[k, :share, :] = block_ref[k * share:(k + 1) * share, :]
        out_ref[k, share:, :] = tail


def polar_kernel(offsets_ref, got_ref, bare_ref, out_ref, padded, bare_rows, arrived):
    energies, tall, width = got_ref.shape
    share = tall - EXTRA
    place = lax.axis_index("energy")
    start = pl.multiple_of(place * share, share)
    copy = pltpu.make_async_copy(bare_ref.at[pl.ds(start, share), :], bare_rows, arrived)
    copy.start()
    padded[:SHIFTS] = jnp.zeros((SHIFTS, share, width), jnp.float32)
    for e in range(energies):
        padded[SHIFTS + e] = got_ref[e, :share, :].astype(jnp.float32)
    totals = [jnp.zeros((share, width), jnp.float32) for _ in range(FREQS)]
    for e in range(energies):
        tail = got_ref[e, share:, :].astype(jnp.float32)
        weighted = padded[SHIFTS + e] * (tail[0:1] + tail[1:2] + tail[2:3])
        for f in range(FREQS):
            totals[f] += weighted * padded[SHIFTS + e - offsets_ref[f]]
    copy.wait()
    factor = -(width ** -0.5) * energies ** -0.5
    for f in range(FREQS):
        out_ref[f] = totals[f] * (factor * bare_rows[...])


def polar_share(green, weight, offsets, bare):
    energies = lax.axis_size("energy")
    rows, width = green.shape
    share = rows // energies
    sent = pl.pallas_call(
        prepare_kernel,
        out_shape=jax.ShapeDtypeStruct((energies, share + EXTRA, width), green.dtype),
        in_specs=[in_smem, in_vmem],
        out_specs=in_vmem,
        name="prepare",
    )(weight, green)
    got = lax.all_to_all(sent, "energy", 0, 0, tiled=True)
    return pl.pallas_call(
        polar_kernel,
        out_shape=jax.ShapeDtypeStruct((FREQS, share, width), jnp.float32),
        in_specs=[in_smem, in_vmem, in_place],
        out_specs=in_vmem,
        scratch_shapes=[
            VMEM((SHIFTS + energies, share, width), jnp.float32),
            VMEM((share, width), jnp.float32),
            pltpu.SemaphoreType.DMA,
        ],
        name="polar",
    )(offsets, got, bare)


def polar_share_plain(green, weight, offsets, bare):
    energies = lax.axis_size("energy")
    rows, width = green.shape
    share = rows // energies
    weights = lax.all_gather(weight, "energy", axis=0, tiled=True)
    got = lax.all_to_all(green.reshape(energies, share, width), "energy", 0, 0, tiled=True)
    wide = got.astype(jnp.float32)
    weighted = wide * weights[:, None, None]
    padded = jnp.concatenate([jnp.zeros((SHIFTS,) + wide.shape[1:], wide.dtype), wide], axis=0)
    own = lax.dynamic_slice_in_dim(bare, lax.axis_index("energy") * share, share, 0)
    factor = -(width ** -0.5) * energies ** -0.5
    chunks = []
    for f in range(FREQS):
        low = lax.dynamic_slice_in_dim(padded, SHIFTS - offsets[f], energies, 0)
        chunks.append(factor * own * jnp.sum(weighted * low, axis=0))
    return jnp.stack(chunks)


def gather_energy(chunk):
    outer = lax.axis_size("energy") // 2
    here = lax.axis_index("energy") // 2
    whole = jnp.zeros((outer,) + chunk.shape, chunk.dtype)
    whole = lax.dynamic_update_index_in_dim(whole, chunk, here, 0)
    for k in range(1, outer):
        route = [(z * 2 + x, (z + k) % outer * 2 + x) for z in range(outer) for x in range(2)]
        got = lax.ppermute(chunk, "energy", route)
        whole = lax.dynamic_update_index_in_dim(whole, got, (here - k) % outer, 0)
    return whole


def gather_square(part):
    energies = lax.axis_size("energy")
    swap = [(e, e ^ 1) for e in range(energies)]
    turn = [(0, 1), (1, 0)]
    cross = [(e * 2 + r, (e ^ 1) * 2 + 1 - r) for e in range(energies) for r in range(2)]
    return [
        part,
        lax.ppermute(part, "energy", swap),
        lax.ppermute(part, "rep", turn),
        lax.ppermute(part, ("energy", "rep"), cross),
    ]


def gathered(chunk):
    energies = lax.axis_size("energy")
    chunk = chunk.astype(coded)
    if energies % 2 or energies > 16 or lax.axis_size("rep") != 2:
        pieces = [lax.all_gather(chunk, ("rep", "energy"), axis=1, tiled=True)]
    else:
        pieces = gather_square(gather_energy(chunk))
    return [piece.astype(jnp.float32) for piece in pieces]


def parts_of(value):
    size = jnp.abs(value)
    exponent = jnp.where(size > 0.0, jnp.floor(jnp.log2(jnp.where(size > 0.0, size, 1.0))), 0.0)
    exponent = jnp.clip(exponent, -120.0, 120.0)
    mantissa = value * jnp.exp2(-exponent)
    first = mantissa.astype(jnp.bfloat16).astype(jnp.float32)
    second = (mantissa - first).astype(jnp.bfloat16).astype(jnp.float32)
    return exponent, first, second


def whole_of(exponent, first, second):
    return (first + second) * jnp.exp2(exponent)


def dyson_kernel(pieces, offsets_ref, steps_ref, level_ref, bare_ref, hamiltonian_ref, two_ref,
                 four_ref, odd_ref, beside_refs, screened_ref, packed_ref, step_ref, own_ref,
                 high, low):
    rows, width = bare_ref.shape
    entry_scale = width ** -0.5
    energy, rep = lax.axis_index("energy"), lax.axis_index("rep")
    if len(pieces) == 1:
        for f in range(FREQS):
            high[f], low[f] = halves(pieces[0][f])
    else:
        outer, _, share, _ = pieces[0].shape
        x = energy % 2
        corners = [(x, rep), (1 - x, rep), (x, 1 - rep), (1 - x, 1 - rep)]
        for piece, (at_x, at_rep) in zip(pieces, corners):
            for z in range(outer):
                start = pl.multiple_of(at_rep * rows + z * 2 * share + at_x * share, share)
                for f in range(FREQS):
                    upper, lower = halves(piece[z, f])
                    high[f, pl.ds(start, share), :] = upper
                    low[f, pl.ds(start, share), :] = lower
    bare = bare_ref[...]
    once = [bare + product(bare, high[f], low[f]) for f in range(FREQS)]
    at = jnp.where(steps_ref[1] > steps_ref[0], 1, 0)
    last = jnp.where(at == 0, once[0], once[1])
    upper, lower = high[at], low[at]
    twice = last + product(product(last, upper, lower), upper, lower)
    other = jnp.minimum(offsets_ref[0], offsets_ref[1])
    less = jnp.where(other == 2, two_ref[...].astype(jnp.float32), odd_ref[...].astype(jnp.float32))
    four = four_ref[...].astype(jnp.float32)
    energy_terms = jnp.zeros((rows, width), jnp.float32)
    for f in range(FREQS):
        count = steps_ref[f]
        value = jnp.where(count == 0, bare, jnp.where(count == 1, once[f], twice))
        value = value.astype(jnp.bfloat16)
        screened_ref[f] = value
        lowered = jnp.where(offsets_ref[f] == SHIFTS, four, less)
        energy_terms += lowered * value.astype(jnp.float32)
    beside = sum(ref[...].astype(jnp.float32) for ref in beside_refs)
    rest = hamiltonian_ref[...] - entry_scale * energy_terms - (0.5 * entry_scale) * beside
    col = lax.broadcasted_iota(jnp.int32, (rows, width), 1)
    row = lax.broadcasted_iota(jnp.int32, (rows, width), 0) + rep * rows
    on = col == row
    diagonal = level_ref[0] + jnp.sum(jnp.where(on, rest, 0.0), axis=1, keepdims=True)
    off = jnp.where(on, 0.0, rest)
    largest = jnp.max(jnp.abs(off), axis=1, keepdims=True)
    largest = jnp.where(largest > 0.0, largest, 1.0)
    unit = off * (1.0 / largest)
    inverse = 1.0 / diagonal
    factor = -largest * inverse
    step_ref[...] = unit * factor
    factor_row = jnp.sum(jnp.where(on, factor, 0.0), axis=0, keepdims=True)
    inverse_row = jnp.sum(jnp.where(on, inverse, 0.0), axis=0, keepdims=True)
    blank = jnp.zeros((1, width), jnp.float32)
    packed_ref[:rows, :] = unit
    packed_ref[rows:, :] = jnp.concatenate(
        [*parts_of(factor_row), *parts_of(inverse_row), blank, blank], axis=0
    )
    own_ref[...] = jnp.concatenate([factor_row, inverse_row] + [blank] * 6, axis=0)


def dyson_rows(pieces, offsets, steps, level, bare, hamiltonian, two, four, odd, beside):
    rows, width = bare.shape
    count, sides = len(pieces), len(beside)

    def kernel(*refs):
        own, rest = refs[:count], refs[count:]
        named, rest = rest[:8], rest[8:]
        dyson_kernel(own, *named, rest[:sides], *rest[sides:])

    return pl.pallas_call(
        kernel,
        out_shape=(
            jax.ShapeDtypeStruct((FREQS, rows, width), jnp.bfloat16),
            jax.ShapeDtypeStruct((rows + EXTRA, width), jnp.float32),
            jax.ShapeDtypeStruct((rows, width), jnp.float32),
            jax.ShapeDtypeStruct((EXTRA, width), jnp.float32),
        ),
        in_specs=[in_vmem] * count + [in_smem] * 3 + [in_vmem] * (5 + sides),
        out_specs=(in_vmem,) * 4,
        scratch_shapes=[VMEM((FREQS, width, width), jnp.bfloat16)] * 2,
        name="dyson",
    )(*pieces, offsets, steps, level, bare, hamiltonian, two, four, odd, *beside)


def finish_kernel(steps_ref, step_ref, packed_ref, theirs_ref, own_ref, out_ref):
    rows, width = step_ref.shape
    rep = lax.axis_index("rep")
    first = rep == 0
    tail = theirs_ref[rows:, :]
    factors = own_ref[0:1] + whole_of(tail[0:1], tail[1:2], tail[2:3])
    inverses = own_ref[1:2] + whole_of(tail[3:4], tail[4:5], tail[5:6])
    mine = halves(packed_ref[:rows, :])
    theirs = halves(theirs_ref[:rows, :])

    def times_all(value):
        left, right = value[:, :rows], value[:, rows:]
        return product(jnp.where(first, left, right), *mine) + product(
            jnp.where(first, right, left), *theirs
        )

    step = step_ref[...]
    square = times_all(step * factors)
    cube = times_all(square * factors)
    col = lax.broadcasted_iota(jnp.int32, (rows, width), 1)
    row = lax.broadcasted_iota(jnp.int32, (rows, width), 0) + rep * rows
    total = jnp.where(col == row, 1.0, step)
    total = total + jnp.where(steps_ref[0] >= 2, square + cube, 0.0)
    out_ref[...] = total * inverses


def body(
    green_blocks, occupation, offsets, coulomb, hamiltonian, onsite_level, green_steps, screen_steps
):
    green = green_blocks[0, 0]
    bare = coulomb[0]
    rows, width = green.shape
    share = rows // lax.axis_size("energy")
    make = polar_share if share % 16 == 0 else polar_share_plain
    pieces = gathered(make(green, occupation, offsets, bare))

    two = shifted(green, "energy", 2)
    four = shifted(two, "energy", 2)
    odd = shifted(chosen(offsets, two, green), "energy", 1)

    slabs = lax.axis_size("slab")
    if slabs == 2:
        beside = [lax.ppermute(green, "slab", [(0, 1), (1, 0)])]
    else:
        up = [(i, i + 1) for i in range(slabs - 1)]
        down = [(j, i) for i, j in up]
        beside = [lax.ppermute(green, "slab", up), lax.ppermute(green, "slab", down)]

    screened, packed, step, own = dyson_rows(
        pieces, offsets, screen_steps, onsite_level, bare, hamiltonian[0], two, four, odd, beside
    )
    theirs = lax.ppermute(packed.astype(coded), "rep", [(0, 1), (1, 0)]).astype(jnp.float32)
    green_next = pl.pallas_call(
        finish_kernel,
        out_shape=jax.ShapeDtypeStruct((rows, width), jnp.float32),
        in_specs=[in_smem] + [in_vmem] * 4,
        out_specs=in_vmem,
        name="finish",
    )(green_steps, step, packed, theirs, own)
    return green_next[None, None], screened[:, None]


def chosen_kernel(offsets_ref, two_ref, green_ref, out_ref):
    three = jnp.minimum(offsets_ref[0], offsets_ref[1]) == 3

    @pl.when(three)
    def _():
        out_ref[...] = two_ref[...]

    @pl.when(jnp.logical_not(three))
    def _():
        out_ref[...] = green_ref[...]


def chosen(offsets, two, green):
    return pl.pallas_call(
        chosen_kernel,
        out_shape=jax.ShapeDtypeStruct(green.shape, green.dtype),
        in_specs=[in_smem, in_vmem, in_vmem],
        out_specs=in_vmem,
        name="chosen",
    )(offsets, two, green)


def solution(mesh):
    return jax.shard_map(
        body,
        mesh=mesh,
        in_specs=(
            P("energy", "slab", "rep", None),
            P("energy"),
            P(),
            P("slab", "rep", None),
            P("slab", "rep", None),
            P("energy"),
            P("energy"),
            P(),
        ),
        out_specs=(P("energy", "slab", "rep", None), P(None, "slab", "rep", None)),
        check_vma=False,
    )
```

```python
import jax
import jax.numpy as jnp
from jax import lax
from jax.experimental import pallas as pl
from jax.experimental.pallas import tpu as pltpu
from jax.sharding import PartitionSpec as P

SHIFTS = 4
FREQS = 2
EXTRA = 8

coded = jnp.float16
VMEM = pltpu.VMEM
in_vmem = pl.BlockSpec(memory_space=pltpu.VMEM)
in_smem = pl.BlockSpec(memory_space=pltpu.SMEM)
in_place = pl.BlockSpec(memory_space=pl.ANY)
small = pltpu.CompilerParams(vmem_limit_bytes=6 << 20)
large = pltpu.CompilerParams(vmem_limit_bytes=16 << 20)


def halves(value):
    high = value.astype(jnp.bfloat16)
    return high, (value - high.astype(jnp.float32)).astype(jnp.bfloat16)


def dot(first, second):
    return jnp.dot(first, second, preferred_element_type=jnp.float32)


def product(first, high, low):
    top, rest = halves(first)
    return dot(top, high) + dot(top, low) + dot(rest, high)


def shifted(block, axis, distance):
    count = lax.axis_size(axis)
    route = [(i, i + distance) for i in range(count - distance)]
    return lax.ppermute(block, axis, route)


def prepare_kernel(weight_ref, block_ref, out_ref):
    energies, padded, width = out_ref.shape
    share = padded - EXTRA
    weight = jnp.full((EXTRA, width), weight_ref[0], jnp.float32)
    first = weight.astype(jnp.bfloat16).astype(jnp.float32)
    second = (weight - first).astype(jnp.bfloat16).astype(jnp.float32)
    third = weight - first - second
    row = lax.broadcasted_iota(jnp.int32, (EXTRA, width), 0)
    tail = jnp.where(row == 0, first, jnp.where(row == 1, second, third)).astype(jnp.bfloat16)
    for k in range(energies):
        out_ref[k, :share, :] = block_ref[k * share:(k + 1) * share, :]
        out_ref[k, share:, :] = tail


def polar_kernel(offsets_ref, got_ref, bare_ref, out_ref, padded, bare_rows, arrived):
    energies, tall, width = got_ref.shape
    share = tall - EXTRA
    place = lax.axis_index("energy")
    start = pl.multiple_of(place * share, share)
    copy = pltpu.make_async_copy(bare_ref.at[pl.ds(start, share), :], bare_rows, arrived)
    copy.start()
    padded[:SHIFTS] = jnp.zeros((SHIFTS, share, width), jnp.float32)
    for e in range(energies):
        padded[SHIFTS + e] = got_ref[e, :share, :].astype(jnp.float32)
    totals = [jnp.zeros((share, width), jnp.float32) for _ in range(FREQS)]
    for e in range(energies):
        tail = got_ref[e, share:, :].astype(jnp.float32)
        weighted = padded[SHIFTS + e] * (tail[0:1] + tail[1:2] + tail[2:3])
        for f in range(FREQS):
            totals[f] += weighted * padded[SHIFTS + e - offsets_ref[f]]
    copy.wait()
    factor = -(width ** -0.5) * energies ** -0.5
    for f in range(FREQS):
        out_ref[f] = totals[f] * (factor * bare_rows[...])


def polar_share(green, weight, offsets, bare):
    energies = lax.axis_size("energy")
    rows, width = green.shape
    share = rows // energies
    sent = pl.pallas_call(
        prepare_kernel,
        out_shape=jax.ShapeDtypeStruct((energies, share + EXTRA, width), green.dtype),
        in_specs=[in_smem, in_vmem],
        out_specs=in_vmem,
        compiler_params=small,
        name="prepare",
    )(weight, green)
    got = lax.all_to_all(sent, "energy", 0, 0, tiled=True)
    return pl.pallas_call(
        polar_kernel,
        out_shape=jax.ShapeDtypeStruct((FREQS, share, width), jnp.float32),
        in_specs=[in_smem, in_vmem, in_place],
        out_specs=in_vmem,
        scratch_shapes=[
            VMEM((SHIFTS + energies, share, width), jnp.float32),
            VMEM((share, width), jnp.float32),
            pltpu.SemaphoreType.DMA,
        ],
        compiler_params=small,
        name="polar",
    )(offsets, got, bare)


def polar_share_plain(green, weight, offsets, bare):
    energies = lax.axis_size("energy")
    rows, width = green.shape
    share = rows // energies
    weights = lax.all_gather(weight, "energy", axis=0, tiled=True)
    got = lax.all_to_all(green.reshape(energies, share, width), "energy", 0, 0, tiled=True)
    wide = got.astype(jnp.float32)
    weighted = wide * weights[:, None, None]
    padded = jnp.concatenate([jnp.zeros((SHIFTS,) + wide.shape[1:], wide.dtype), wide], axis=0)
    own = lax.dynamic_slice_in_dim(bare, lax.axis_index("energy") * share, share, 0)
    factor = -(width ** -0.5) * energies ** -0.5
    chunks = []
    for f in range(FREQS):
        low = lax.dynamic_slice_in_dim(padded, SHIFTS - offsets[f], energies, 0)
        chunks.append(factor * own * jnp.sum(weighted * low, axis=0))
    return jnp.stack(chunks)


def gather_energy(chunk):
    outer = lax.axis_size("energy") // 2
    here = lax.axis_index("energy") // 2
    whole = jnp.zeros((outer,) + chunk.shape, chunk.dtype)
    whole = lax.dynamic_update_index_in_dim(whole, chunk, here, 0)
    for k in range(1, outer):
        route = [(z * 2 + x, (z + k) % outer * 2 + x) for z in range(outer) for x in range(2)]
        got = lax.ppermute(chunk, "energy", route)
        whole = lax.dynamic_update_index_in_dim(whole, got, (here - k) % outer, 0)
    return whole


def gather_square(part):
    energies = lax.axis_size("energy")
    swap = [(e, e ^ 1) for e in range(energies)]
    turn = [(0, 1), (1, 0)]
    cross = [(e * 2 + r, (e ^ 1) * 2 + 1 - r) for e in range(energies) for r in range(2)]
    return [
        part,
        lax.ppermute(part, "energy", swap),
        lax.ppermute(part, "rep", turn),
        lax.ppermute(part, ("energy", "rep"), cross),
    ]


def gathered(chunk):
    energies = lax.axis_size("energy")
    chunk = chunk.astype(coded)
    if energies % 2 or energies > 16 or lax.axis_size("rep") != 2:
        pieces = [lax.all_gather(chunk, ("rep", "energy"), axis=1, tiled=True)]
    else:
        pieces = gather_square(gather_energy(chunk))
    return [piece.astype(jnp.float32) for piece in pieces]


def parts_of(value):
    size = jnp.abs(value)
    exponent = jnp.where(size > 0.0, jnp.floor(jnp.log2(jnp.where(size > 0.0, size, 1.0))), 0.0)
    exponent = jnp.clip(exponent, -120.0, 120.0)
    mantissa = value * jnp.exp2(-exponent)
    first = mantissa.astype(jnp.bfloat16).astype(jnp.float32)
    second = (mantissa - first).astype(jnp.bfloat16).astype(jnp.float32)
    return exponent, first, second


def whole_of(exponent, first, second):
    return (first + second) * jnp.exp2(exponent)


def dyson_kernel(pieces, offsets_ref, steps_ref, level_ref, bare_ref, hamiltonian_ref, two_ref,
                 four_ref, odd_ref, beside_refs, screened_ref, packed_ref, step_ref, own_ref,
                 high, low):
    rows, width = bare_ref.shape
    entry_scale = width ** -0.5
    energy, rep = lax.axis_index("energy"), lax.axis_index("rep")
    if len(pieces) == 1:
        for f in range(FREQS):
            high[f], low[f] = halves(pieces[0][f])
    else:
        outer, _, share, _ = pieces[0].shape
        x = energy % 2
        corners = [(x, rep), (1 - x, rep), (x, 1 - rep), (1 - x, 1 - rep)]
        for piece, (at_x, at_rep) in zip(pieces, corners):
            for z in range(outer):
                start = pl.multiple_of(at_rep * rows + z * 2 * share + at_x * share, share)
                for f in range(FREQS):
                    upper, lower = halves(piece[z, f])
                    high[f, pl.ds(start, share), :] = upper
                    low[f, pl.ds(start, share), :] = lower
    bare = bare_ref[...]
    once = [bare + product(bare, high[f], low[f]) for f in range(FREQS)]
    at = jnp.where(steps_ref[1] > steps_ref[0], 1, 0)
    last = jnp.where(at == 0, once[0], once[1])
    upper, lower = high[at], low[at]
    twice = last + product(product(last, upper, lower), upper, lower)
    other = jnp.minimum(offsets_ref[0], offsets_ref[1])
    less = jnp.where(other == 2, two_ref[...].astype(jnp.float32), odd_ref[...].astype(jnp.float32))
    four = four_ref[...].astype(jnp.float32)
    energy_terms = jnp.zeros((rows, width), jnp.float32)
    for f in range(FREQS):
        count = steps_ref[f]
        value = jnp.where(count == 0, bare, jnp.where(count == 1, once[f], twice))
        value = value.astype(jnp.bfloat16)
        screened_ref[f] = value
        lowered = jnp.where(offsets_ref[f] == SHIFTS, four, less)
        energy_terms += lowered * value.astype(jnp.float32)
    beside = sum(ref[...].astype(jnp.float32) for ref in beside_refs)
    rest = hamiltonian_ref[...] - entry_scale * energy_terms - (0.5 * entry_scale) * beside
    col = lax.broadcasted_iota(jnp.int32, (rows, width), 1)
    row = lax.broadcasted_iota(jnp.int32, (rows, width), 0) + rep * rows
    on = col == row
    diagonal = level_ref[0] + jnp.sum(jnp.where(on, rest, 0.0), axis=1, keepdims=True)
    off = jnp.where(on, 0.0, rest)
    largest = jnp.max(jnp.abs(off), axis=1, keepdims=True)
    largest = jnp.where(largest > 0.0, largest, 1.0)
    unit = off * (1.0 / largest)
    inverse = 1.0 / diagonal
    factor = -largest * inverse
    step_ref[...] = unit * factor
    factor_row = jnp.sum(jnp.where(on, factor, 0.0), axis=0, keepdims=True)
    inverse_row = jnp.sum(jnp.where(on, inverse, 0.0), axis=0, keepdims=True)
    blank = jnp.zeros((1, width), jnp.float32)
    packed_ref[:rows, :] = unit
    packed_ref[rows:, :] = jnp.concatenate(
        [*parts_of(factor_row), *parts_of(inverse_row), blank, blank], axis=0
    )
    own_ref[...] = jnp.concatenate([factor_row, inverse_row] + [blank] * 6, axis=0)


def dyson_rows(pieces, offsets, steps, level, bare, hamiltonian, two, four, odd, beside):
    rows, width = bare.shape
    count, sides = len(pieces), len(beside)

    def kernel(*refs):
        own, rest = refs[:count], refs[count:]
        named, rest = rest[:8], rest[8:]
        dyson_kernel(own, *named, rest[:sides], *rest[sides:])

    return pl.pallas_call(
        kernel,
        out_shape=(
            jax.ShapeDtypeStruct((FREQS, rows, width), jnp.bfloat16),
            jax.ShapeDtypeStruct((rows + EXTRA, width), jnp.float32),
            jax.ShapeDtypeStruct((rows, width), jnp.float32),
            jax.ShapeDtypeStruct((EXTRA, width), jnp.float32),
        ),
        in_specs=[in_vmem] * count + [in_smem] * 3 + [in_vmem] * (5 + sides),
        out_specs=(in_vmem,) * 4,
        scratch_shapes=[VMEM((FREQS, width, width), jnp.bfloat16)] * 2,
        compiler_params=large,
        name="dyson",
    )(*pieces, offsets, steps, level, bare, hamiltonian, two, four, odd, *beside)


def finish_kernel(steps_ref, step_ref, packed_ref, theirs_ref, own_ref, out_ref):
    rows, width = step_ref.shape
    rep = lax.axis_index("rep")
    first = rep == 0
    tail = theirs_ref[rows:, :]
    factors = own_ref[0:1] + whole_of(tail[0:1], tail[1:2], tail[2:3])
    inverses = own_ref[1:2] + whole_of(tail[3:4], tail[4:5], tail[5:6])
    mine = halves(packed_ref[:rows, :])
    theirs = halves(theirs_ref[:rows, :])

    def times_all(value):
        left, right = value[:, :rows], value[:, rows:]
        return product(jnp.where(first, left, right), *mine) + product(
            jnp.where(first, right, left), *theirs
        )

    step = step_ref[...]
    square = times_all(step * factors)
    cube = times_all(square * factors)
    col = lax.broadcasted_iota(jnp.int32, (rows, width), 1)
    row = lax.broadcasted_iota(jnp.int32, (rows, width), 0) + rep * rows
    total = jnp.where(col == row, 1.0, step)
    total = total + jnp.where(steps_ref[0] >= 2, square + cube, 0.0)
    out_ref[...] = total * inverses


def body(
    green_blocks, occupation, offsets, coulomb, hamiltonian, onsite_level, green_steps, screen_steps
):
    green = green_blocks[0, 0]
    bare = coulomb[0]
    rows, width = green.shape
    share = rows // lax.axis_size("energy")
    make = polar_share if share % 16 == 0 else polar_share_plain
    pieces = gathered(make(green, occupation, offsets, bare))

    two = shifted(green, "energy", 2)
    four = shifted(two, "energy", 2)
    odd = shifted(chosen(offsets, two, green), "energy", 1)

    slabs = lax.axis_size("slab")
    if slabs == 2:
        beside = [lax.ppermute(green, "slab", [(0, 1), (1, 0)])]
    else:
        up = [(i, i + 1) for i in range(slabs - 1)]
        down = [(j, i) for i, j in up]
        beside = [lax.ppermute(green, "slab", up), lax.ppermute(green, "slab", down)]

    screened, packed, step, own = dyson_rows(
        pieces, offsets, screen_steps, onsite_level, bare, hamiltonian[0], two, four, odd, beside
    )
    theirs = lax.ppermute(packed.astype(coded), "rep", [(0, 1), (1, 0)]).astype(jnp.float32)
    green_next = pl.pallas_call(
        finish_kernel,
        out_shape=jax.ShapeDtypeStruct((rows, width), jnp.float32),
        in_specs=[in_smem] + [in_vmem] * 4,
        out_specs=in_vmem,
        compiler_params=large,
        name="finish",
    )(green_steps, step, packed, theirs, own)
    return green_next[None, None], screened[:, None]


def chosen_kernel(offsets_ref, two_ref, green_ref, out_ref):
    three = jnp.minimum(offsets_ref[0], offsets_ref[1]) == 3

    @pl.when(three)
    def _():
        out_ref[...] = two_ref[...]

    @pl.when(jnp.logical_not(three))
    def _():
        out_ref[...] = green_ref[...]


def chosen(offsets, two, green):
    return pl.pallas_call(
        chosen_kernel,
        out_shape=jax.ShapeDtypeStruct(green.shape, green.dtype),
        in_specs=[in_smem, in_vmem, in_vmem],
        out_specs=in_vmem,
        compiler_params=small,
        name="chosen",
    )(offsets, two, green)


def solution(mesh):
    return jax.shard_map(
        body,
        mesh=mesh,
        in_specs=(
            P("energy", "slab", "rep", None),
            P("energy"),
            P(),
            P("slab", "rep", None),
            P("slab", "rep", None),
            P("energy"),
            P("energy"),
            P(),
        ),
        out_specs=(P("energy", "slab", "rep", None), P(None, "slab", "rep", None)),
        check_vma=False,
    )
```

```python
import jax
import jax.numpy as jnp
from jax import lax
from jax.experimental import pallas as pl
from jax.experimental.pallas import tpu as pltpu
from jax.sharding import PartitionSpec as P


SHIFTS = 4
FREQS = 2
EXTRA = 8

coded = jnp.float16
VMEM = pltpu.VMEM
in_vmem = pl.BlockSpec(memory_space=pltpu.VMEM)
in_smem = pl.BlockSpec(memory_space=pltpu.SMEM)
in_place = pl.BlockSpec(memory_space=pl.ANY)
in_hbm = pl.BlockSpec(memory_space=pltpu.HBM)
small = pltpu.CompilerParams(vmem_limit_bytes=6 << 20)
large = pltpu.CompilerParams(vmem_limit_bytes=16 << 20)


def held(value):
    return pltpu.with_memory_space_constraint(value, pltpu.HBM)


def halves(value):
    high = value.astype(jnp.bfloat16)
    return high, (value - high.astype(jnp.float32)).astype(jnp.bfloat16)


def dot(first, second):
    return jnp.dot(first, second, preferred_element_type=jnp.float32)


def product(first, high, low):
    top, rest = halves(first)
    return dot(top, high) + dot(top, low) + dot(rest, high)


def shifted(block, axis, distance):
    count = lax.axis_size(axis)
    route = [(i, i + distance) for i in range(count - distance)]
    return lax.ppermute(block, axis, route)


def prepare_kernel(weight_ref, block_ref, out_ref, tail, block_sem, tail_sem):
    energies, padded, width = out_ref.shape
    share = padded - EXTRA
    copies = [
        pltpu.make_async_copy(
            block_ref.at[pl.ds(k * share, share), :], out_ref.at[k, pl.ds(0, share), :],
            block_sem.at[k],
        )
        for k in range(energies)
    ]
    for copy in copies:
        copy.start()
    weight = jnp.full((EXTRA, width), weight_ref[0], jnp.float32)
    first = weight.astype(jnp.bfloat16).astype(jnp.float32)
    second = (weight - first).astype(jnp.bfloat16).astype(jnp.float32)
    third = weight - first - second
    row = lax.broadcasted_iota(jnp.int32, (EXTRA, width), 0)
    parts = jnp.where(row == 0, first, jnp.where(row == 1, second, third))
    tail[...] = parts.astype(jnp.bfloat16)
    tails = [
        pltpu.make_async_copy(tail, out_ref.at[k, pl.ds(share, EXTRA), :], tail_sem.at[k])
        for k in range(energies)
    ]
    for copy in tails:
        copy.start()
    for copy in copies + tails:
        copy.wait()


def polar_kernel(offsets_ref, got_ref, bare_ref, out_ref, padded, bare_rows, arrived):
    energies, tall, width = got_ref.shape
    share = tall - EXTRA
    place = lax.axis_index("energy")
    start = pl.multiple_of(place * share, share)
    copy = pltpu.make_async_copy(bare_ref.at[pl.ds(start, share), :], bare_rows, arrived)
    copy.start()
    padded[:SHIFTS] = jnp.zeros((SHIFTS, share, width), jnp.float32)
    for e in range(energies):
        padded[SHIFTS + e] = got_ref[e, :share, :].astype(jnp.float32)
    totals = [jnp.zeros((share, width), jnp.float32) for _ in range(FREQS)]
    for e in range(energies):
        tail = got_ref[e, share:, :].astype(jnp.float32)
        weighted = padded[SHIFTS + e] * (tail[0:1] + tail[1:2] + tail[2:3])
        for f in range(FREQS):
            totals[f] += weighted * padded[SHIFTS + e - offsets_ref[f]]
    copy.wait()
    factor = -(width ** -0.5) * energies ** -0.5
    for f in range(FREQS):
        out_ref[f] = totals[f] * (factor * bare_rows[...])


def polar_share(green, weight, offsets, bare):
    energies = lax.axis_size("energy")
    rows, width = green.shape
    share = rows // energies
    sent = pl.pallas_call(
        prepare_kernel,
        out_shape=jax.ShapeDtypeStruct((energies, share + EXTRA, width), green.dtype),
        in_specs=[in_smem, in_hbm],
        out_specs=in_hbm,
        scratch_shapes=[
            VMEM((EXTRA, width), green.dtype),
            pltpu.SemaphoreType.DMA((energies,)),
            pltpu.SemaphoreType.DMA((energies,)),
        ],
        compiler_params=small,
        name="prepare",
    )(weight, held(green))
    got = lax.all_to_all(sent, "energy", 0, 0, tiled=True)
    return pl.pallas_call(
        polar_kernel,
        out_shape=jax.ShapeDtypeStruct((FREQS, share, width), jnp.float32),
        in_specs=[in_smem, in_vmem, in_place],
        out_specs=in_vmem,
        scratch_shapes=[
            VMEM((SHIFTS + energies, share, width), jnp.float32),
            VMEM((share, width), jnp.float32),
            pltpu.SemaphoreType.DMA,
        ],
        compiler_params=small,
        name="polar",
    )(offsets, got, bare)


def polar_share_plain(green, weight, offsets, bare):
    energies = lax.axis_size("energy")
    rows, width = green.shape
    share = rows // energies
    weights = lax.all_gather(weight, "energy", axis=0, tiled=True)
    got = lax.all_to_all(green.reshape(energies, share, width), "energy", 0, 0, tiled=True)
    wide = got.astype(jnp.float32)
    weighted = wide * weights[:, None, None]
    padded = jnp.concatenate([jnp.zeros((SHIFTS,) + wide.shape[1:], wide.dtype), wide], axis=0)
    own = lax.dynamic_slice_in_dim(bare, lax.axis_index("energy") * share, share, 0)
    factor = -(width ** -0.5) * energies ** -0.5
    chunks = []
    for f in range(FREQS):
        low = lax.dynamic_slice_in_dim(padded, SHIFTS - offsets[f], energies, 0)
        chunks.append(factor * own * jnp.sum(weighted * low, axis=0))
    return jnp.stack(chunks)


def gather_energy(chunk):
    outer = lax.axis_size("energy") // 2
    here = lax.axis_index("energy") // 2
    whole = jnp.zeros((outer,) + chunk.shape, chunk.dtype)
    whole = lax.dynamic_update_index_in_dim(whole, chunk, here, 0)
    for k in range(outer - 1, 0, -1):
        route = [(z * 2 + x, (z + k) % outer * 2 + x) for z in range(outer) for x in range(2)]
        got = lax.ppermute(chunk, "energy", route)
        whole = lax.dynamic_update_index_in_dim(whole, got, (here - k) % outer, 0)
    return whole


def gather_square(part):
    energies = lax.axis_size("energy")
    swap = [(e, e ^ 1) for e in range(energies)]
    turn = [(0, 1), (1, 0)]
    cross = [(e * 2 + r, (e ^ 1) * 2 + 1 - r) for e in range(energies) for r in range(2)]
    apart = lax.ppermute(part, ("energy", "rep"), cross)
    beside = lax.ppermute(part, "energy", swap)
    above = lax.ppermute(part, "rep", turn)
    return [part, beside, above, apart]


def gathered(chunk):
    energies = lax.axis_size("energy")
    chunk = chunk.astype(coded)
    if energies % 2 or energies > 16 or lax.axis_size("rep") != 2:
        pieces = [lax.all_gather(chunk, ("rep", "energy"), axis=1, tiled=True)]
    else:
        pieces = gather_square(gather_energy(chunk))
    return [piece.astype(jnp.float32) for piece in pieces]


def parts_of(value):
    size = jnp.abs(value)
    exponent = jnp.where(size > 0.0, jnp.floor(jnp.log2(jnp.where(size > 0.0, size, 1.0))), 0.0)
    exponent = jnp.clip(exponent, -120.0, 120.0)
    mantissa = value * jnp.exp2(-exponent)
    first = mantissa.astype(jnp.bfloat16).astype(jnp.float32)
    second = (mantissa - first).astype(jnp.bfloat16).astype(jnp.float32)
    return exponent, first, second


def whole_of(exponent, first, second):
    return (first + second) * jnp.exp2(exponent)


def dyson_kernel(pieces, offsets_ref, steps_ref, level_ref, bare_ref, hamiltonian_ref, two_ref,
                 four_ref, odd_ref, beside_refs, screened_ref, packed_ref, step_ref, own_ref,
                 high, low):
    rows, width = bare_ref.shape
    entry_scale = width ** -0.5
    energy, rep = lax.axis_index("energy"), lax.axis_index("rep")
    if len(pieces) == 1:
        for f in range(FREQS):
            high[f], low[f] = halves(pieces[0][f])
    else:
        outer, _, share, _ = pieces[0].shape
        x = energy % 2
        corners = [(x, rep), (1 - x, rep), (x, 1 - rep), (1 - x, 1 - rep)]
        for piece, (at_x, at_rep) in zip(pieces, corners):
            for z in range(outer):
                start = pl.multiple_of(at_rep * rows + z * 2 * share + at_x * share, share)
                for f in range(FREQS):
                    upper, lower = halves(piece[z, f])
                    high[f, pl.ds(start, share), :] = upper
                    low[f, pl.ds(start, share), :] = lower
    bare = bare_ref[...]
    once = [bare + product(bare, high[f], low[f]) for f in range(FREQS)]
    at = jnp.where(steps_ref[1] > steps_ref[0], 1, 0)
    last = jnp.where(at == 0, once[0], once[1])
    upper, lower = high[at], low[at]
    twice = last + product(product(last, upper, lower), upper, lower)
    other = jnp.minimum(offsets_ref[0], offsets_ref[1])
    less = jnp.where(other == 2, two_ref[...].astype(jnp.float32), odd_ref[...].astype(jnp.float32))
    four = four_ref[...].astype(jnp.float32)
    energy_terms = jnp.zeros((rows, width), jnp.float32)
    for f in range(FREQS):
        count = steps_ref[f]
        value = jnp.where(count == 0, bare, jnp.where(count == 1, once[f], twice))
        value = value.astype(jnp.bfloat16)
        screened_ref[f] = value
        lowered = jnp.where(offsets_ref[f] == SHIFTS, four, less)
        energy_terms += lowered * value.astype(jnp.float32)
    beside = sum(ref[...].astype(jnp.float32) for ref in beside_refs)
    rest = hamiltonian_ref[...] - entry_scale * energy_terms - (0.5 * entry_scale) * beside
    col = lax.broadcasted_iota(jnp.int32, (rows, width), 1)
    row = lax.broadcasted_iota(jnp.int32, (rows, width), 0) + rep * rows
    on = col == row
    diagonal = level_ref[0] + jnp.sum(jnp.where(on, rest, 0.0), axis=1, keepdims=True)
    off = jnp.where(on, 0.0, rest)
    largest = jnp.max(jnp.abs(off), axis=1, keepdims=True)
    largest = jnp.where(largest > 0.0, largest, 1.0)
    unit = off * (1.0 / largest)
    inverse = 1.0 / diagonal
    factor = -largest * inverse
    step_ref[...] = unit * factor
    factor_row = jnp.sum(jnp.where(on, factor, 0.0), axis=0, keepdims=True)
    inverse_row = jnp.sum(jnp.where(on, inverse, 0.0), axis=0, keepdims=True)
    blank = jnp.zeros((1, width), jnp.float32)
    packed_ref[:rows, :] = unit
    packed_ref[rows:, :] = jnp.concatenate(
        [*parts_of(factor_row), *parts_of(inverse_row), blank, blank], axis=0
    )
    own_ref[...] = jnp.concatenate([factor_row, inverse_row] + [blank] * 6, axis=0)


def dyson_rows(pieces, offsets, steps, level, bare, hamiltonian, two, four, odd, beside):
    rows, width = bare.shape
    count, sides = len(pieces), len(beside)

    def kernel(*refs):
        own, rest = refs[:count], refs[count:]
        named, rest = rest[:8], rest[8:]
        dyson_kernel(own, *named, rest[:sides], *rest[sides:])

    return pl.pallas_call(
        kernel,
        out_shape=(
            jax.ShapeDtypeStruct((FREQS, rows, width), jnp.bfloat16),
            jax.ShapeDtypeStruct((rows + EXTRA, width), jnp.float32),
            jax.ShapeDtypeStruct((rows, width), jnp.float32),
            jax.ShapeDtypeStruct((EXTRA, width), jnp.float32),
        ),
        in_specs=[in_vmem] * count + [in_smem] * 3 + [in_vmem] * (5 + sides),
        out_specs=(in_vmem,) * 4,
        scratch_shapes=[VMEM((FREQS, width, width), jnp.bfloat16)] * 2,
        compiler_params=large,
        name="dyson",
    )(*pieces, offsets, steps, level, bare, hamiltonian, two, four, odd, *beside)


def finish_kernel(steps_ref, step_ref, packed_ref, theirs_ref, own_ref, out_ref):
    rows, width = step_ref.shape
    rep = lax.axis_index("rep")
    first = rep == 0
    tail = theirs_ref[rows:, :]
    factors = own_ref[0:1] + whole_of(tail[0:1], tail[1:2], tail[2:3])
    inverses = own_ref[1:2] + whole_of(tail[3:4], tail[4:5], tail[5:6])
    mine = halves(packed_ref[:rows, :])
    theirs = halves(theirs_ref[:rows, :])

    def times_all(value):
        left, right = value[:, :rows], value[:, rows:]
        return product(jnp.where(first, left, right), *mine) + product(
            jnp.where(first, right, left), *theirs
        )

    step = step_ref[...]
    square = times_all(step * factors)
    cube = times_all(square * factors)
    col = lax.broadcasted_iota(jnp.int32, (rows, width), 1)
    row = lax.broadcasted_iota(jnp.int32, (rows, width), 0) + rep * rows
    total = jnp.where(col == row, 1.0, step)
    total = total + jnp.where(steps_ref[0] >= 2, square + cube, 0.0)
    out_ref[...] = total * inverses


def body(
    green_blocks, occupation, offsets, coulomb, hamiltonian, onsite_level, green_steps, screen_steps
):
    green = green_blocks[0, 0]
    bare = coulomb[0]
    rows, width = green.shape
    share = rows // lax.axis_size("energy")
    make = polar_share if share % 16 == 0 else polar_share_plain
    pieces = gathered(make(green, occupation, offsets, bare))

    two = shifted(green, "energy", 2)
    four = shifted(two, "energy", 2)
    odd = shifted(chosen(offsets, (screen_steps, green_steps, onsite_level), two, green), "energy", 1)

    slabs = lax.axis_size("slab")
    if slabs == 2:
        beside = [lax.ppermute(green, "slab", [(0, 1), (1, 0)])]
    else:
        up = [(i, i + 1) for i in range(slabs - 1)]
        down = [(j, i) for i, j in up]
        beside = [lax.ppermute(green, "slab", up), lax.ppermute(green, "slab", down)]

    screened, packed, step, own = dyson_rows(
        pieces, offsets, screen_steps, onsite_level, bare, hamiltonian[0], two, four, odd, beside
    )
    theirs = lax.ppermute(packed.astype(coded), "rep", [(0, 1), (1, 0)]).astype(jnp.float32)
    green_next = pl.pallas_call(
        finish_kernel,
        out_shape=jax.ShapeDtypeStruct((rows, width), jnp.float32),
        in_specs=[in_smem] + [in_vmem] * 4,
        out_specs=in_vmem,
        compiler_params=large,
        name="finish",
    )(green_steps, step, packed, theirs, own)
    return green_next[None, None], screened[:, None]


def chosen_kernel(offsets_ref, screen_ref, green_steps_ref, level_ref, two_ref, green_ref, out_ref):
    three = jnp.minimum(offsets_ref[0], offsets_ref[1]) == 3

    @pl.when(three)
    def _():
        out_ref[...] = two_ref[...]

    @pl.when(jnp.logical_not(three))
    def _():
        out_ref[...] = green_ref[...]


def chosen(offsets, scalars, two, green):
    return pl.pallas_call(
        chosen_kernel,
        out_shape=jax.ShapeDtypeStruct(green.shape, green.dtype),
        in_specs=[in_smem] * 4 + [in_vmem] * 2,
        out_specs=in_vmem,
        compiler_params=small,
        name="chosen",
    )(offsets, *scalars, two, green)


def solution(mesh):
    return jax.shard_map(
        body,
        mesh=mesh,
        in_specs=(
            P("energy", "slab", "rep", None),
            P("energy"),
            P(),
            P("slab", "rep", None),
            P("slab", "rep", None),
            P("energy"),
            P("energy"),
            P(),
        ),
        out_specs=(P("energy", "slab", "rep", None), P(None, "slab", "rep", None)),
        check_vma=False,
    )
```

```python
import jax
import jax.numpy as jnp
from jax import lax
from jax.experimental import pallas as pl
from jax.experimental.pallas import tpu as pltpu
from jax.sharding import PartitionSpec as P


SHIFTS = 4
FREQS = 2
EXTRA = 8

coded = jnp.float16
VMEM = pltpu.VMEM
in_vmem = pl.BlockSpec(memory_space=pltpu.VMEM)
in_smem = pl.BlockSpec(memory_space=pltpu.SMEM)
in_place = pl.BlockSpec(memory_space=pl.ANY)
small = pltpu.CompilerParams(vmem_limit_bytes=6 << 20)
large = pltpu.CompilerParams(vmem_limit_bytes=16 << 20)


def halves(value):
    high = value.astype(jnp.bfloat16)
    return high, (value - high.astype(jnp.float32)).astype(jnp.bfloat16)


def dot(first, second):
    return jnp.dot(first, second, preferred_element_type=jnp.float32)


def product(first, high, low):
    top, rest = halves(first)
    return dot(top, high) + dot(top, low) + dot(rest, high)


def shifted(block, axis, distance):
    count = lax.axis_size(axis)
    route = [(i, i + distance) for i in range(count - distance)]
    return lax.ppermute(block, axis, route)


def prepare_kernel(weight_ref, block_ref, out_ref):
    energies, padded, width = out_ref.shape
    share = padded - EXTRA
    weight = jnp.full((EXTRA, width), weight_ref[0], jnp.float32)
    first = weight.astype(jnp.bfloat16).astype(jnp.float32)
    second = (weight - first).astype(jnp.bfloat16).astype(jnp.float32)
    third = weight - first - second
    row = lax.broadcasted_iota(jnp.int32, (EXTRA, width), 0)
    tail = jnp.where(row == 0, first, jnp.where(row == 1, second, third)).astype(jnp.bfloat16)
    for k in range(energies):
        out_ref[k, :share, :] = block_ref[k * share:(k + 1) * share, :]
        out_ref[k, share:, :] = tail


def polar_kernel(offsets_ref, got_ref, bare_ref, out_ref, padded, bare_rows, arrived):
    energies, tall, width = got_ref.shape
    share = tall - EXTRA
    place = lax.axis_index("energy")
    start = pl.multiple_of(place * share, share)
    copy = pltpu.make_async_copy(bare_ref.at[pl.ds(start, share), :], bare_rows, arrived)
    copy.start()
    padded[:SHIFTS] = jnp.zeros((SHIFTS, share, width), jnp.float32)
    for e in range(energies):
        padded[SHIFTS + e] = got_ref[e, :share, :].astype(jnp.float32)
    totals = [jnp.zeros((share, width), jnp.float32) for _ in range(FREQS)]
    for e in range(energies):
        tail = got_ref[e, share:, :].astype(jnp.float32)
        weighted = padded[SHIFTS + e] * (tail[0:1] + tail[1:2] + tail[2:3])
        for f in range(FREQS):
            totals[f] += weighted * padded[SHIFTS + e - offsets_ref[f]]
    copy.wait()
    factor = -(width ** -0.5) * energies ** -0.5
    for f in range(FREQS):
        out_ref[f] = totals[f] * (factor * bare_rows[...])


def polar_share(green, weight, offsets, bare):
    energies = lax.axis_size("energy")
    rows, width = green.shape
    share = rows // energies
    sent = pl.pallas_call(
        prepare_kernel,
        out_shape=jax.ShapeDtypeStruct((energies, share + EXTRA, width), green.dtype),
        in_specs=[in_smem, in_vmem],
        out_specs=in_vmem,
        compiler_params=small,
        name="prepare",
    )(weight, green)
    got = lax.all_to_all(sent, "energy", 0, 0, tiled=True)
    return pl.pallas_call(
        polar_kernel,
        out_shape=jax.ShapeDtypeStruct((FREQS, share, width), jnp.float32),
        in_specs=[in_smem, in_vmem, in_place],
        out_specs=in_vmem,
        scratch_shapes=[
            VMEM((SHIFTS + energies, share, width), jnp.float32),
            VMEM((share, width), jnp.float32),
            pltpu.SemaphoreType.DMA,
        ],
        compiler_params=small,
        name="polar",
    )(offsets, got, bare)


def polar_share_plain(green, weight, offsets, bare):
    energies = lax.axis_size("energy")
    rows, width = green.shape
    share = rows // energies
    weights = lax.all_gather(weight, "energy", axis=0, tiled=True)
    got = lax.all_to_all(green.reshape(energies, share, width), "energy", 0, 0, tiled=True)
    wide = got.astype(jnp.float32)
    weighted = wide * weights[:, None, None]
    padded = jnp.concatenate([jnp.zeros((SHIFTS,) + wide.shape[1:], wide.dtype), wide], axis=0)
    own = lax.dynamic_slice_in_dim(bare, lax.axis_index("energy") * share, share, 0)
    factor = -(width ** -0.5) * energies ** -0.5
    chunks = []
    for f in range(FREQS):
        low = lax.dynamic_slice_in_dim(padded, SHIFTS - offsets[f], energies, 0)
        chunks.append(factor * own * jnp.sum(weighted * low, axis=0))
    return jnp.stack(chunks)


def gather_energy(chunk):
    outer = lax.axis_size("energy") // 2
    here = lax.axis_index("energy") // 2
    whole = jnp.zeros((outer,) + chunk.shape, chunk.dtype)
    whole = lax.dynamic_update_index_in_dim(whole, chunk, here, 0)
    for k in range(outer - 1, 0, -1):
        route = [(z * 2 + x, (z + k) % outer * 2 + x) for z in range(outer) for x in range(2)]
        got = lax.ppermute(chunk, "energy", route)
        whole = lax.dynamic_update_index_in_dim(whole, got, (here - k) % outer, 0)
    return whole


def gather_square(part):
    energies = lax.axis_size("energy")
    swap = [(e, e ^ 1) for e in range(energies)]
    turn = [(0, 1), (1, 0)]
    cross = [(e * 2 + r, (e ^ 1) * 2 + 1 - r) for e in range(energies) for r in range(2)]
    apart = lax.ppermute(part, ("energy", "rep"), cross)
    beside = lax.ppermute(part, "energy", swap)
    above = lax.ppermute(part, "rep", turn)
    return [part, beside, above, apart]


def gathered(chunk):
    energies = lax.axis_size("energy")
    chunk = chunk.astype(coded)
    if energies % 2 or energies > 16 or lax.axis_size("rep") != 2:
        pieces = [lax.all_gather(chunk, ("rep", "energy"), axis=1, tiled=True)]
    else:
        pieces = gather_square(gather_energy(chunk))
    return [piece.astype(jnp.float32) for piece in pieces]


def parts_of(value):
    size = jnp.abs(value)
    exponent = jnp.where(size > 0.0, jnp.floor(jnp.log2(jnp.where(size > 0.0, size, 1.0))), 0.0)
    exponent = jnp.clip(exponent, -120.0, 120.0)
    mantissa = value * jnp.exp2(-exponent)
    first = mantissa.astype(jnp.bfloat16).astype(jnp.float32)
    second = (mantissa - first).astype(jnp.bfloat16).astype(jnp.float32)
    return exponent, first, second


def whole_of(exponent, first, second):
    return (first + second) * jnp.exp2(exponent)


def dyson_kernel(pieces, offsets_ref, steps_ref, level_ref, bare_ref, hamiltonian_ref, two_ref,
                 four_ref, odd_ref, beside_refs, screened_ref, packed_ref, step_ref, own_ref,
                 high, low):
    rows, width = bare_ref.shape
    entry_scale = width ** -0.5
    energy, rep = lax.axis_index("energy"), lax.axis_index("rep")
    if len(pieces) == 1:
        for f in range(FREQS):
            high[f], low[f] = halves(pieces[0][f])
    else:
        outer, _, share, _ = pieces[0].shape
        x = energy % 2
        corners = [(x, rep), (1 - x, rep), (x, 1 - rep), (1 - x, 1 - rep)]
        for piece, (at_x, at_rep) in zip(pieces, corners):
            for z in range(outer):
                start = pl.multiple_of(at_rep * rows + z * 2 * share + at_x * share, share)
                for f in range(FREQS):
                    upper, lower = halves(piece[z, f])
                    high[f, pl.ds(start, share), :] = upper
                    low[f, pl.ds(start, share), :] = lower
    bare = bare_ref[...]
    once = [bare + product(bare, high[f], low[f]) for f in range(FREQS)]
    at = jnp.where(steps_ref[1] > steps_ref[0], 1, 0)
    last = jnp.where(at == 0, once[0], once[1])
    upper, lower = high[at], low[at]
    twice = last + product(product(last, upper, lower), upper, lower)
    other = jnp.minimum(offsets_ref[0], offsets_ref[1])
    less = jnp.where(other == 2, two_ref[...].astype(jnp.float32), odd_ref[...].astype(jnp.float32))
    four = four_ref[...].astype(jnp.float32)
    energy_terms = jnp.zeros((rows, width), jnp.float32)
    for f in range(FREQS):
        count = steps_ref[f]
        value = jnp.where(count == 0, bare, jnp.where(count == 1, once[f], twice))
        value = value.astype(jnp.bfloat16)
        screened_ref[f] = value
        lowered = jnp.where(offsets_ref[f] == SHIFTS, four, less)
        energy_terms += lowered * value.astype(jnp.float32)
    beside = sum(ref[...].astype(jnp.float32) for ref in beside_refs)
    rest = hamiltonian_ref[...] - entry_scale * energy_terms - (0.5 * entry_scale) * beside
    col = lax.broadcasted_iota(jnp.int32, (rows, width), 1)
    row = lax.broadcasted_iota(jnp.int32, (rows, width), 0) + rep * rows
    on = col == row
    diagonal = level_ref[0] + jnp.sum(jnp.where(on, rest, 0.0), axis=1, keepdims=True)
    off = jnp.where(on, 0.0, rest)
    largest = jnp.max(jnp.abs(off), axis=1, keepdims=True)
    largest = jnp.where(largest > 0.0, largest, 1.0)
    unit = off * (1.0 / largest)
    inverse = 1.0 / diagonal
    factor = -largest * inverse
    step_ref[...] = unit * factor
    factor_row = jnp.sum(jnp.where(on, factor, 0.0), axis=0, keepdims=True)
    inverse_row = jnp.sum(jnp.where(on, inverse, 0.0), axis=0, keepdims=True)
    blank = jnp.zeros((1, width), jnp.float32)
    packed_ref[:rows, :] = unit
    packed_ref[rows:, :] = jnp.concatenate(
        [*parts_of(factor_row), *parts_of(inverse_row), blank, blank], axis=0
    )
    own_ref[...] = jnp.concatenate([factor_row, inverse_row] + [blank] * 6, axis=0)


def dyson_rows(pieces, offsets, steps, level, bare, hamiltonian, two, four, odd, beside):
    rows, width = bare.shape
    count, sides = len(pieces), len(beside)

    def kernel(*refs):
        own, rest = refs[:count], refs[count:]
        named, rest = rest[:8], rest[8:]
        dyson_kernel(own, *named, rest[:sides], *rest[sides:])

    return pl.pallas_call(
        kernel,
        out_shape=(
            jax.ShapeDtypeStruct((FREQS, rows, width), jnp.bfloat16),
            jax.ShapeDtypeStruct((rows + EXTRA, width), jnp.float32),
            jax.ShapeDtypeStruct((rows, width), jnp.float32),
            jax.ShapeDtypeStruct((EXTRA, width), jnp.float32),
        ),
        in_specs=[in_vmem] * count + [in_smem] * 3 + [in_vmem] * (5 + sides),
        out_specs=(in_vmem,) * 4,
        scratch_shapes=[VMEM((FREQS, width, width), jnp.bfloat16)] * 2,
        compiler_params=large,
        name="dyson",
    )(*pieces, offsets, steps, level, bare, hamiltonian, two, four, odd, *beside)


def finish_kernel(steps_ref, step_ref, packed_ref, theirs_ref, own_ref, out_ref):
    rows, width = step_ref.shape
    rep = lax.axis_index("rep")
    first = rep == 0
    tail = theirs_ref[rows:, :]
    factors = own_ref[0:1] + whole_of(tail[0:1], tail[1:2], tail[2:3])
    inverses = own_ref[1:2] + whole_of(tail[3:4], tail[4:5], tail[5:6])
    mine = halves(packed_ref[:rows, :])
    theirs = halves(theirs_ref[:rows, :])

    def times_all(value):
        left, right = value[:, :rows], value[:, rows:]
        return product(jnp.where(first, left, right), *mine) + product(
            jnp.where(first, right, left), *theirs
        )

    step = step_ref[...]
    square = times_all(step * factors)
    cube = times_all(square * factors)
    col = lax.broadcasted_iota(jnp.int32, (rows, width), 1)
    row = lax.broadcasted_iota(jnp.int32, (rows, width), 0) + rep * rows
    total = jnp.where(col == row, 1.0, step)
    total = total + jnp.where(steps_ref[0] >= 2, square + cube, 0.0)
    out_ref[...] = total * inverses


def body(
    green_blocks, occupation, offsets, coulomb, hamiltonian, onsite_level, green_steps, screen_steps
):
    green = green_blocks[0, 0]
    bare = coulomb[0]
    rows, width = green.shape
    share = rows // lax.axis_size("energy")
    make = polar_share if share % 16 == 0 else polar_share_plain
    pieces = gathered(make(green, occupation, offsets, bare))

    two = shifted(green, "energy", 2)
    four = shifted(two, "energy", 2)
    odd = shifted(chosen(offsets, (screen_steps, green_steps, onsite_level), two, green), "energy", 1)

    slabs = lax.axis_size("slab")
    if slabs == 2:
        beside = [lax.ppermute(green, "slab", [(0, 1), (1, 0)])]
    else:
        up = [(i, i + 1) for i in range(slabs - 1)]
        down = [(j, i) for i, j in up]
        beside = [lax.ppermute(green, "slab", up), lax.ppermute(green, "slab", down)]

    screened, packed, step, own = dyson_rows(
        pieces, offsets, screen_steps, onsite_level, bare, hamiltonian[0], two, four, odd, beside
    )
    theirs = lax.ppermute(packed.astype(coded), "rep", [(0, 1), (1, 0)]).astype(jnp.float32)
    green_next = pl.pallas_call(
        finish_kernel,
        out_shape=jax.ShapeDtypeStruct((rows, width), jnp.float32),
        in_specs=[in_smem] + [in_vmem] * 4,
        out_specs=in_vmem,
        compiler_params=large,
        name="finish",
    )(green_steps, step, packed, theirs, own)
    return green_next[None, None], screened[:, None]


def chosen_kernel(offsets_ref, screen_ref, green_steps_ref, level_ref, two_ref, green_ref, out_ref):
    three = jnp.minimum(offsets_ref[0], offsets_ref[1]) == 3

    @pl.when(three)
    def _():
        out_ref[...] = two_ref[...]

    @pl.when(jnp.logical_not(three))
    def _():
        out_ref[...] = green_ref[...]


def chosen(offsets, scalars, two, green):
    return pl.pallas_call(
        chosen_kernel,
        out_shape=jax.ShapeDtypeStruct(green.shape, green.dtype),
        in_specs=[in_smem] * 4 + [in_vmem] * 2,
        out_specs=in_vmem,
        compiler_params=small,
        name="chosen",
    )(offsets, *scalars, two, green)


def solution(mesh):
    return jax.shard_map(
        body,
        mesh=mesh,
        in_specs=(
            P("energy", "slab", "rep", None),
            P("energy"),
            P(),
            P("slab", "rep", None),
            P("slab", "rep", None),
            P("energy"),
            P("energy"),
            P(),
        ),
        out_specs=(P("energy", "slab", "rep", None), P(None, "slab", "rep", None)),
        check_vma=False,
    )
```

```python
import jax
import jax.numpy as jnp
from jax import lax
from jax.experimental import pallas as pl
from jax.experimental.pallas import tpu as pltpu
from jax.sharding import PartitionSpec as P


SHIFTS = 4
FREQS = 2
EXTRA = 8

coded = jnp.float16
VMEM = pltpu.VMEM
in_vmem = pl.BlockSpec(memory_space=pltpu.VMEM)
in_smem = pl.BlockSpec(memory_space=pltpu.SMEM)
in_place = pl.BlockSpec(memory_space=pl.ANY)
in_hbm = pl.BlockSpec(memory_space=pltpu.HBM)
small = pltpu.CompilerParams(vmem_limit_bytes=6 << 20)
large = pltpu.CompilerParams(vmem_limit_bytes=16 << 20)


def held(value):
    return pltpu.with_memory_space_constraint(value, pltpu.HBM)


def halves(value):
    high = value.astype(jnp.bfloat16)
    return high, (value - high.astype(jnp.float32)).astype(jnp.bfloat16)


def dot(first, second):
    return jnp.dot(first, second, preferred_element_type=jnp.float32)


def product(first, high, low):
    top, rest = halves(first)
    return dot(top, high) + dot(top, low) + dot(rest, high)


def shifted(block, axis, distance):
    count = lax.axis_size(axis)
    route = [(i, i + distance) for i in range(count - distance)]
    return lax.ppermute(block, axis, route)


def in_squares():
    energies = lax.axis_size("energy")
    return energies % 2 == 0 and energies <= 16 and lax.axis_size("rep") == 2


def share_of(place):
    outer = lax.axis_size("energy") // 2
    return place % 2 * outer + place // 2 if in_squares() else place


def prepare_kernel(weight_ref, block_ref, out_ref, held_rows, read_sems, write_sems):
    energies, padded, width = out_ref.shape
    share = padded - EXTRA
    reads = [
        pltpu.make_async_copy(
            block_ref.at[pl.ds(share_of(k) * share, share), :],
            held_rows.at[k, pl.ds(0, share), :], read_sems.at[k],
        )
        for k in range(energies)
    ]
    for copy in reads:
        copy.start()
    weight = jnp.full((EXTRA, width), weight_ref[0], jnp.float32)
    first = weight.astype(jnp.bfloat16).astype(jnp.float32)
    second = (weight - first).astype(jnp.bfloat16).astype(jnp.float32)
    third = weight - first - second
    row = lax.broadcasted_iota(jnp.int32, (EXTRA, width), 0)
    tail = jnp.where(row == 0, first, jnp.where(row == 1, second, third)).astype(jnp.bfloat16)
    writes = [
        pltpu.make_async_copy(held_rows.at[k], out_ref.at[k], write_sems.at[k])
        for k in range(energies)
    ]
    for k in range(energies):
        held_rows[k, share:, :] = tail
    for k in range(energies):
        reads[k].wait()
        writes[k].start()
    for copy in writes:
        copy.wait()


def polar_kernel(offsets_ref, screen_ref, green_steps_ref, level_ref, got_ref, bare_ref, out_ref, padded, bare_rows, arrived):
    energies, tall, width = got_ref.shape
    share = tall - EXTRA
    start = pl.multiple_of(share_of(lax.axis_index("energy")) * share, share)
    copy = pltpu.make_async_copy(bare_ref.at[pl.ds(start, share), :], bare_rows, arrived)
    copy.start()
    padded[:SHIFTS] = jnp.zeros((SHIFTS, share, width), jnp.float32)
    for e in range(energies):
        padded[SHIFTS + e] = got_ref[e, :share, :].astype(jnp.float32)
    totals = [jnp.zeros((share, width), jnp.float32) for _ in range(FREQS)]
    for e in range(energies):
        tail = got_ref[e, share:, :].astype(jnp.float32)
        weighted = padded[SHIFTS + e] * (tail[0:1] + tail[1:2] + tail[2:3])
        for f in range(FREQS):
            totals[f] += weighted * padded[SHIFTS + e - offsets_ref[f]]
    copy.wait()
    factor = -(width ** -0.5) * energies ** -0.5
    for f in range(FREQS):
        out_ref[f] = totals[f] * (factor * bare_rows[...])


def polar_share(green, weight, offsets, bare, scalars):
    energies = lax.axis_size("energy")
    rows, width = green.shape
    share = rows // energies
    sent = pl.pallas_call(
        prepare_kernel,
        out_shape=jax.ShapeDtypeStruct((energies, share + EXTRA, width), green.dtype),
        in_specs=[in_smem, in_hbm],
        out_specs=in_hbm,
        scratch_shapes=[
            VMEM((energies, share + EXTRA, width), green.dtype),
            pltpu.SemaphoreType.DMA((energies,)),
            pltpu.SemaphoreType.DMA((energies,)),
        ],
        compiler_params=small,
        name="prepare",
    )(weight, held(green))
    got = lax.all_to_all(sent, "energy", 0, 0, tiled=True)
    return pl.pallas_call(
        polar_kernel,
        out_shape=jax.ShapeDtypeStruct((FREQS, share, width), jnp.float32),
        in_specs=[in_smem] * 4 + [in_vmem, in_place],
        out_specs=in_vmem,
        scratch_shapes=[
            VMEM((SHIFTS + energies, share, width), jnp.float32),
            VMEM((share, width), jnp.float32),
            pltpu.SemaphoreType.DMA,
        ],
        compiler_params=small,
        name="polar",
    )(offsets, *scalars, got, bare)


def polar_share_plain(green, weight, offsets, bare, scalars):
    energies = lax.axis_size("energy")
    rows, width = green.shape
    share = rows // energies
    weights = lax.all_gather(weight, "energy", axis=0, tiled=True)
    parts = green.reshape(energies, share, width)
    parts = jnp.stack([parts[share_of(k)] for k in range(energies)]) if in_squares() else parts
    got = lax.all_to_all(parts, "energy", 0, 0, tiled=True)
    wide = got.astype(jnp.float32)
    weighted = wide * weights[:, None, None]
    padded = jnp.concatenate([jnp.zeros((SHIFTS,) + wide.shape[1:], wide.dtype), wide], axis=0)
    own = lax.dynamic_slice_in_dim(bare, share_of(lax.axis_index("energy")) * share, share, 0)
    factor = -(width ** -0.5) * energies ** -0.5
    chunks = []
    for f in range(FREQS):
        low = lax.dynamic_slice_in_dim(padded, SHIFTS - offsets[f], energies, 0)
        chunks.append(factor * own * jnp.sum(weighted * low, axis=0))
    return jnp.stack(chunks)


def gather_energy(chunk):
    outer = lax.axis_size("energy") // 2
    here = lax.axis_index("energy") // 2
    whole = jnp.zeros((outer,) + chunk.shape, chunk.dtype)
    whole = lax.dynamic_update_index_in_dim(whole, chunk, here, 0)
    for k in range(outer - 1, 0, -1):
        route = [(z * 2 + x, (z + k) % outer * 2 + x) for z in range(outer) for x in range(2)]
        got = lax.ppermute(chunk, "energy", route)
        whole = lax.dynamic_update_index_in_dim(whole, got, (here - k) % outer, 0)
    return whole


def gather_square(part):
    energies = lax.axis_size("energy")
    swap = [(e, e ^ 1) for e in range(energies)]
    turn = [(0, 1), (1, 0)]
    cross = [(e * 2 + r, (e ^ 1) * 2 + 1 - r) for e in range(energies) for r in range(2)]
    apart = lax.ppermute(part, ("energy", "rep"), cross)
    beside = lax.ppermute(part, "energy", swap)
    above = lax.ppermute(part, "rep", turn)
    return [part, beside, above, apart]


def gathered(chunk):
    chunk = chunk.astype(coded)
    if in_squares():
        pieces = gather_square(gather_energy(chunk))
    else:
        pieces = [lax.all_gather(chunk, ("rep", "energy"), axis=1, tiled=True)]
    return [piece.astype(jnp.float32) for piece in pieces]


def parts_of(value):
    size = jnp.abs(value)
    exponent = jnp.where(size > 0.0, jnp.floor(jnp.log2(jnp.where(size > 0.0, size, 1.0))), 0.0)
    exponent = jnp.clip(exponent, -120.0, 120.0)
    mantissa = value * jnp.exp2(-exponent)
    first = mantissa.astype(jnp.bfloat16).astype(jnp.float32)
    second = (mantissa - first).astype(jnp.bfloat16).astype(jnp.float32)
    return exponent, first, second


def whole_of(exponent, first, second):
    return (first + second) * jnp.exp2(exponent)


def dyson_kernel(pieces, offsets_ref, steps_ref, level_ref, bare_ref, hamiltonian_ref, two_ref,
                 four_ref, odd_ref, beside_refs, screened_ref, packed_ref, step_ref, own_ref,
                 high, low, made, hamiltonian_rows, made_sem, hamiltonian_sem):
    rows, width = bare_ref.shape
    entry_scale = width ** -0.5
    read = pltpu.make_async_copy(hamiltonian_ref, hamiltonian_rows, hamiltonian_sem)
    read.start()
    energy, rep = lax.axis_index("energy"), lax.axis_index("rep")
    if len(pieces) == 1:
        for f in range(FREQS):
            high[f], low[f] = halves(pieces[0][f])
    else:
        outer, _, share, _ = pieces[0].shape
        x = energy % 2
        corners = [(x, rep), (1 - x, rep), (x, 1 - rep), (1 - x, 1 - rep)]
        for piece, (at_x, at_rep) in zip(pieces, corners):
            for z in range(outer):
                start = pl.multiple_of(at_rep * rows + (at_x * outer + z) * share, share)
                for f in range(FREQS):
                    upper, lower = halves(piece[z, f])
                    high[f, pl.ds(start, share), :] = upper
                    low[f, pl.ds(start, share), :] = lower
    bare = bare_ref[...]
    once = [bare + product(bare, high[f], low[f]) for f in range(FREQS)]
    at = jnp.where(steps_ref[1] > steps_ref[0], 1, 0)
    last = jnp.where(at == 0, once[0], once[1])
    upper, lower = high[at], low[at]
    twice = last + product(product(last, upper, lower), upper, lower)
    other = jnp.minimum(offsets_ref[0], offsets_ref[1])
    less = jnp.where(other == 2, two_ref[...].astype(jnp.float32), odd_ref[...].astype(jnp.float32))
    four = four_ref[...].astype(jnp.float32)
    energy_terms = jnp.zeros((rows, width), jnp.float32)
    for f in range(FREQS):
        count = steps_ref[f]
        value = jnp.where(count == 0, bare, jnp.where(count == 1, once[f], twice))
        value = value.astype(jnp.bfloat16)
        made[f] = value
        lowered = jnp.where(offsets_ref[f] == SHIFTS, four, less)
        energy_terms += lowered * value.astype(jnp.float32)
    beside = sum(ref[...].astype(jnp.float32) for ref in beside_refs)
    write = pltpu.make_async_copy(made, screened_ref, made_sem)
    write.start()
    read.wait()
    rest = hamiltonian_rows[...] - entry_scale * energy_terms - (0.5 * entry_scale) * beside
    col = lax.broadcasted_iota(jnp.int32, (rows, width), 1)
    row = lax.broadcasted_iota(jnp.int32, (rows, width), 0) + rep * rows
    on = col == row
    diagonal = level_ref[0] + jnp.sum(jnp.where(on, rest, 0.0), axis=1, keepdims=True)
    off = jnp.where(on, 0.0, rest)
    largest = jnp.max(jnp.abs(off), axis=1, keepdims=True)
    largest = jnp.where(largest > 0.0, largest, 1.0)
    unit = off * (1.0 / largest)
    inverse = 1.0 / diagonal
    factor = -largest * inverse
    step_ref[...] = unit * factor
    factor_row = jnp.sum(jnp.where(on, factor, 0.0), axis=0, keepdims=True)
    inverse_row = jnp.sum(jnp.where(on, inverse, 0.0), axis=0, keepdims=True)
    blank = jnp.zeros((1, width), jnp.float32)
    packed_ref[:rows, :] = unit
    packed_ref[rows:, :] = jnp.concatenate(
        [*parts_of(factor_row), *parts_of(inverse_row), blank, blank], axis=0
    )
    own_ref[...] = jnp.concatenate([factor_row, inverse_row] + [blank] * 6, axis=0)
    write.wait()


def dyson_rows(pieces, offsets, steps, level, bare, hamiltonian, two, four, odd, beside):
    rows, width = bare.shape
    count, sides = len(pieces), len(beside)

    def kernel(*refs):
        own, rest = refs[:count], refs[count:]
        named, rest = rest[:8], rest[8:]
        dyson_kernel(own, *named, rest[:sides], *rest[sides:])

    return pl.pallas_call(
        kernel,
        out_shape=(
            jax.ShapeDtypeStruct((FREQS, rows, width), jnp.bfloat16),
            jax.ShapeDtypeStruct((rows + EXTRA, width), jnp.float32),
            jax.ShapeDtypeStruct((rows, width), jnp.float32),
            jax.ShapeDtypeStruct((EXTRA, width), jnp.float32),
        ),
        in_specs=[in_vmem] * count + [in_smem] * 3 + [in_vmem, in_hbm] + [in_vmem] * (3 + sides),
        out_specs=(in_hbm,) + (in_vmem,) * 3,
        scratch_shapes=[VMEM((FREQS, width, width), jnp.bfloat16)] * 2
        + [VMEM((FREQS, rows, width), jnp.bfloat16), VMEM((rows, width), jnp.float32)]
        + [pltpu.SemaphoreType.DMA] * 2,
        compiler_params=large,
        name="dyson",
    )(*pieces, offsets, steps, level, bare, held(hamiltonian), two, four, odd, *beside)


def columns(value, first):
    rows = value.shape[0]
    left, right = value[:, :rows], value[:, rows:]
    return jnp.where(first, left, right), jnp.where(first, right, left)


def begin_kernel(step_ref, packed_ref, own_ref, square_ref, high_ref, low_ref):
    rows, _ = step_ref.shape
    high, low = halves(packed_ref[:rows, :])
    high_ref[...], low_ref[...] = high, low
    near, _ = columns(step_ref[...] * own_ref[0:1], lax.axis_index("rep") == 0)
    square_ref[...] = product(near, high, low)


def finish_kernel(steps_ref, step_ref, square_ref, high_ref, low_ref, theirs_ref, own_ref, out_ref,
                  made, sems):
    rows, _ = step_ref.shape
    rep = lax.axis_index("rep")
    first = rep == 0
    tail = theirs_ref[rows:, :]
    factors = own_ref[0:1] + whole_of(tail[0:1], tail[1:2], tail[2:3])
    inverses = own_ref[1:2] + whole_of(tail[3:4], tail[4:5], tail[5:6])
    theirs = halves(theirs_ref[:rows, :])
    step = step_ref[...]
    _, far = columns(step * factors, first)
    square = square_ref[...] + product(far, *theirs)
    near, far = columns(square * factors, first)
    writes = []
    for half in range(2):
        at = slice(half * rows, (half + 1) * rows)
        cube = product(near, high_ref[:, at], low_ref[:, at]) + product(
            far, theirs[0][:, at], theirs[1][:, at]
        )
        col = lax.broadcasted_iota(jnp.int32, (rows, rows), 1) + half * rows
        row = lax.broadcasted_iota(jnp.int32, (rows, rows), 0) + rep * rows
        total = jnp.where(col == row, 1.0, step[:, at])
        total = total + jnp.where(steps_ref[0] >= 2, square[:, at] + cube, 0.0)
        made[:, at] = total * inverses[:, at]
        writes.append(pltpu.make_async_copy(made.at[:, at], out_ref.at[:, at], sems.at[half]))
        writes[-1].start()
    for write in writes:
        write.wait()


def body(
    green_blocks, occupation, offsets, coulomb, hamiltonian, onsite_level, green_steps, screen_steps
):
    green = green_blocks[0, 0]
    bare = coulomb[0]
    rows, width = green.shape
    share = rows // lax.axis_size("energy")
    make = polar_share if share % 16 == 0 else polar_share_plain
    scalars = (screen_steps, green_steps, onsite_level)
    pieces = gathered(make(green, occupation, offsets, bare, scalars))

    two = shifted(green, "energy", 2)
    four = shifted(two, "energy", 2)
    odd = shifted(chosen(offsets, two, green), "energy", 1)

    slabs = lax.axis_size("slab")
    if slabs == 2:
        beside = [lax.ppermute(green, "slab", [(0, 1), (1, 0)])]
    else:
        up = [(i, i + 1) for i in range(slabs - 1)]
        down = [(j, i) for i, j in up]
        beside = [lax.ppermute(green, "slab", up), lax.ppermute(green, "slab", down)]

    screened, packed, step, own = dyson_rows(
        pieces, offsets, screen_steps, onsite_level, bare, hamiltonian[0], two, four, odd, beside
    )
    theirs = lax.ppermute(packed.astype(coded), "rep", [(0, 1), (1, 0)]).astype(jnp.float32)
    wide = jax.ShapeDtypeStruct((rows, width), jnp.float32)
    thin = jax.ShapeDtypeStruct((rows, width), jnp.bfloat16)
    square, high, low = pl.pallas_call(
        begin_kernel,
        out_shape=(wide, thin, thin),
        in_specs=[in_vmem] * 3,
        out_specs=(in_vmem,) * 3,
        compiler_params=small,
        name="begin",
    )(step, packed, own)
    green_next = pl.pallas_call(
        finish_kernel,
        out_shape=wide,
        in_specs=[in_smem] + [in_vmem] * 6,
        out_specs=in_hbm,
        scratch_shapes=[VMEM((rows, width), jnp.float32), pltpu.SemaphoreType.DMA((2,))],
        compiler_params=large,
        name="finish",
    )(green_steps, step, square, high, low, theirs, own)
    return green_next[None, None], screened[:, None]


def chosen_kernel(offsets_ref, two_ref, green_ref, out_ref):
    three = jnp.minimum(offsets_ref[0], offsets_ref[1]) == 3

    @pl.when(three)
    def _():
        out_ref[...] = two_ref[...]

    @pl.when(jnp.logical_not(three))
    def _():
        out_ref[...] = green_ref[...]


def chosen(offsets, two, green):
    return pl.pallas_call(
        chosen_kernel,
        out_shape=jax.ShapeDtypeStruct(green.shape, green.dtype),
        in_specs=[in_smem, in_vmem, in_vmem],
        out_specs=in_vmem,
        compiler_params=small,
        name="chosen",
    )(offsets, two, green)


def solution(mesh):
    return jax.shard_map(
        body,
        mesh=mesh,
        in_specs=(
            P("energy", "slab", "rep", None),
            P("energy"),
            P(),
            P("slab", "rep", None),
            P("slab", "rep", None),
            P("energy"),
            P("energy"),
            P(),
        ),
        out_specs=(P("energy", "slab", "rep", None), P(None, "slab", "rep", None)),
        check_vma=False,
    )
```

```python
import jax
import jax.numpy as jnp
from jax import lax
from jax.experimental import pallas as pl
from jax.experimental.pallas import tpu as pltpu
from jax.sharding import PartitionSpec as P


SHIFTS = 4
FREQS = 2
EXTRA = 8

coded = jnp.float16
VMEM = pltpu.VMEM
in_vmem = pl.BlockSpec(memory_space=pltpu.VMEM)
in_smem = pl.BlockSpec(memory_space=pltpu.SMEM)
in_place = pl.BlockSpec(memory_space=pl.ANY)
in_hbm = pl.BlockSpec(memory_space=pltpu.HBM)
small = pltpu.CompilerParams(vmem_limit_bytes=6 << 20)
large = pltpu.CompilerParams(vmem_limit_bytes=16 << 20)


def held(value):
    return pltpu.with_memory_space_constraint(value, pltpu.HBM)


def halves(value):
    high = value.astype(jnp.bfloat16)
    return high, (value - high.astype(jnp.float32)).astype(jnp.bfloat16)


def dot(first, second):
    return jnp.dot(first, second, preferred_element_type=jnp.float32)


def product(first, high, low):
    top, rest = halves(first)
    return dot(top, high) + dot(top, low) + dot(rest, high)


def shifted(block, axis, distance):
    count = lax.axis_size(axis)
    route = [(i, i + distance) for i in range(count - distance)]
    return lax.ppermute(block, axis, route)


def in_squares():
    energies = lax.axis_size("energy")
    return energies % 2 == 0 and energies <= 16 and lax.axis_size("rep") == 2


def share_of(place):
    outer = lax.axis_size("energy") // 2
    return place % 2 * outer + place // 2 if in_squares() else place


def prepare_kernel(weight_ref, block_ref, out_ref, held_rows, read_sems, write_sems):
    energies, padded, width = out_ref.shape
    share = padded - EXTRA
    reads = [
        pltpu.make_async_copy(
            block_ref.at[pl.ds(share_of(k) * share, share), :],
            held_rows.at[k, pl.ds(0, share), :], read_sems.at[k],
        )
        for k in range(energies)
    ]
    for copy in reads:
        copy.start()
    weight = jnp.full((EXTRA, width), weight_ref[0], jnp.float32)
    first = weight.astype(jnp.bfloat16).astype(jnp.float32)
    second = (weight - first).astype(jnp.bfloat16).astype(jnp.float32)
    third = weight - first - second
    row = lax.broadcasted_iota(jnp.int32, (EXTRA, width), 0)
    tail = jnp.where(row == 0, first, jnp.where(row == 1, second, third)).astype(jnp.bfloat16)
    writes = [
        pltpu.make_async_copy(held_rows.at[k], out_ref.at[k], write_sems.at[k])
        for k in range(energies)
    ]
    for k in range(energies):
        held_rows[k, share:, :] = tail
    for k in range(energies):
        reads[k].wait()
        writes[k].start()
    for copy in writes:
        copy.wait()


def polar_kernel(offsets_ref, screen_ref, green_steps_ref, level_ref, got_ref, bare_ref, out_ref, padded, bare_rows, arrived):
    energies, tall, width = got_ref.shape
    share = tall - EXTRA
    start = pl.multiple_of(share_of(lax.axis_index("energy")) * share, share)
    copy = pltpu.make_async_copy(bare_ref.at[pl.ds(start, share), :], bare_rows, arrived)
    copy.start()
    padded[:SHIFTS] = jnp.zeros((SHIFTS, share, width), jnp.float32)
    for e in range(energies):
        padded[SHIFTS + e] = got_ref[e, :share, :].astype(jnp.float32)
    totals = [jnp.zeros((share, width), jnp.float32) for _ in range(FREQS)]
    for e in range(energies):
        tail = got_ref[e, share:, :].astype(jnp.float32)
        weighted = padded[SHIFTS + e] * (tail[0:1] + tail[1:2] + tail[2:3])
        for f in range(FREQS):
            totals[f] += weighted * padded[SHIFTS + e - offsets_ref[f]]
    copy.wait()
    factor = -(width ** -0.5) * energies ** -0.5
    for f in range(FREQS):
        out_ref[f] = totals[f] * (factor * bare_rows[...])


def polar_share(green, weight, offsets, bare, scalars):
    energies = lax.axis_size("energy")
    rows, width = green.shape
    share = rows // energies
    sent = pl.pallas_call(
        prepare_kernel,
        out_shape=jax.ShapeDtypeStruct((energies, share + EXTRA, width), green.dtype),
        in_specs=[in_smem, in_hbm],
        out_specs=in_hbm,
        scratch_shapes=[
            VMEM((energies, share + EXTRA, width), green.dtype),
            pltpu.SemaphoreType.DMA((energies,)),
            pltpu.SemaphoreType.DMA((energies,)),
        ],
        compiler_params=small,
        name="prepare",
    )(weight, held(green))
    got = lax.all_to_all(sent, "energy", 0, 0, tiled=True)
    return pl.pallas_call(
        polar_kernel,
        out_shape=jax.ShapeDtypeStruct((FREQS, share, width), jnp.float32),
        in_specs=[in_smem] * 4 + [in_vmem, in_place],
        out_specs=in_vmem,
        scratch_shapes=[
            VMEM((SHIFTS + energies, share, width), jnp.float32),
            VMEM((share, width), jnp.float32),
            pltpu.SemaphoreType.DMA,
        ],
        compiler_params=small,
        name="polar",
    )(offsets, *scalars, got, bare)


def polar_share_plain(green, weight, offsets, bare, scalars):
    energies = lax.axis_size("energy")
    rows, width = green.shape
    share = rows // energies
    weights = lax.all_gather(weight, "energy", axis=0, tiled=True)
    parts = green.reshape(energies, share, width)
    parts = jnp.stack([parts[share_of(k)] for k in range(energies)]) if in_squares() else parts
    got = lax.all_to_all(parts, "energy", 0, 0, tiled=True)
    wide = got.astype(jnp.float32)
    weighted = wide * weights[:, None, None]
    padded = jnp.concatenate([jnp.zeros((SHIFTS,) + wide.shape[1:], wide.dtype), wide], axis=0)
    own = lax.dynamic_slice_in_dim(bare, share_of(lax.axis_index("energy")) * share, share, 0)
    factor = -(width ** -0.5) * energies ** -0.5
    chunks = []
    for f in range(FREQS):
        low = lax.dynamic_slice_in_dim(padded, SHIFTS - offsets[f], energies, 0)
        chunks.append(factor * own * jnp.sum(weighted * low, axis=0))
    return jnp.stack(chunks)


def gather_energy(chunk):
    outer = lax.axis_size("energy") // 2
    here = lax.axis_index("energy") // 2
    wholes = [
        lax.dynamic_update_index_in_dim(jnp.zeros((outer,) + part.shape, part.dtype), part, here, 0)
        for part in chunk
    ]
    for k in range(outer - 1, 0, -1):
        route = [(z * 2 + x, (z + k) % outer * 2 + x) for z in range(outer) for x in range(2)]
        got = lax.ppermute(chunk, "energy", route)
        wholes = [
            lax.dynamic_update_index_in_dim(whole, part, (here - k) % outer, 0)
            for whole, part in zip(wholes, got)
        ]
    return wholes


def gather_square(parts):
    energies = lax.axis_size("energy")

    def along_x(part):
        return lax.ppermute(part, "energy", [(e, e ^ 1) for e in range(energies)])

    def along_rep(part):
        return lax.ppermute(part, "rep", [(0, 1), (1, 0)])

    beside = [along_x(part) for part in parts]
    above = [along_rep(part) for part in parts]
    apart = [along_rep(beside[0]), along_x(above[1])]
    return [*parts, *beside, *above, *apart]


def gathered(chunk):
    chunk = chunk.astype(coded)
    if in_squares():
        pieces = gather_square(gather_energy(chunk))
    else:
        pieces = [lax.all_gather(chunk, ("rep", "energy"), axis=1, tiled=True)]
    return [piece.astype(jnp.float32) for piece in pieces]


def parts_of(value):
    size = jnp.abs(value)
    exponent = jnp.where(size > 0.0, jnp.floor(jnp.log2(jnp.where(size > 0.0, size, 1.0))), 0.0)
    exponent = jnp.clip(exponent, -120.0, 120.0)
    mantissa = value * jnp.exp2(-exponent)
    first = mantissa.astype(jnp.bfloat16).astype(jnp.float32)
    second = (mantissa - first).astype(jnp.bfloat16).astype(jnp.float32)
    return exponent, first, second


def whole_of(exponent, first, second):
    return (first + second) * jnp.exp2(exponent)


def dyson_kernel(pieces, offsets_ref, steps_ref, level_ref, bare_ref, hamiltonian_ref, two_ref,
                 four_ref, odd_ref, beside_refs, screened_ref, packed_ref, step_ref, own_ref,
                 high, low, made, hamiltonian_rows, made_sem, hamiltonian_sem):
    rows, width = bare_ref.shape
    entry_scale = width ** -0.5
    read = pltpu.make_async_copy(hamiltonian_ref, hamiltonian_rows, hamiltonian_sem)
    read.start()
    energy, rep = lax.axis_index("energy"), lax.axis_index("rep")
    if len(pieces) == 1:
        for f in range(FREQS):
            high[f], low[f] = halves(pieces[0][f])
    else:
        outer, share, _ = pieces[0].shape
        x = energy % 2
        corners = [(x, rep), (1 - x, rep), (x, 1 - rep), (1 - x, 1 - rep)]
        for place, (at_x, at_rep) in enumerate(corners):
            start = pl.multiple_of(at_rep * rows + at_x * outer * share, outer * share)
            for f in range(FREQS):
                piece = pieces[place * FREQS + f][...].reshape(outer * share, width)
                upper, lower = halves(piece)
                high[f, pl.ds(start, outer * share), :] = upper
                low[f, pl.ds(start, outer * share), :] = lower
    bare = bare_ref[...]
    once = [bare + product(bare, high[f], low[f]) for f in range(FREQS)]
    at = jnp.where(steps_ref[1] > steps_ref[0], 1, 0)
    last = jnp.where(at == 0, once[0], once[1])
    upper, lower = high[at], low[at]
    twice = last + product(product(last, upper, lower), upper, lower)
    other = jnp.minimum(offsets_ref[0], offsets_ref[1])
    less = jnp.where(other == 2, two_ref[...].astype(jnp.float32), odd_ref[...].astype(jnp.float32))
    four = four_ref[...].astype(jnp.float32)
    energy_terms = jnp.zeros((rows, width), jnp.float32)
    for f in range(FREQS):
        count = steps_ref[f]
        value = jnp.where(count == 0, bare, jnp.where(count == 1, once[f], twice))
        value = value.astype(jnp.bfloat16)
        made[f] = value
        lowered = jnp.where(offsets_ref[f] == SHIFTS, four, less)
        energy_terms += lowered * value.astype(jnp.float32)
    beside = sum(ref[...].astype(jnp.float32) for ref in beside_refs)
    write = pltpu.make_async_copy(made, screened_ref, made_sem)
    write.start()
    read.wait()
    rest = hamiltonian_rows[...] - entry_scale * energy_terms - (0.5 * entry_scale) * beside
    col = lax.broadcasted_iota(jnp.int32, (rows, width), 1)
    row = lax.broadcasted_iota(jnp.int32, (rows, width), 0) + rep * rows
    on = col == row
    diagonal = level_ref[0] + jnp.sum(jnp.where(on, rest, 0.0), axis=1, keepdims=True)
    off = jnp.where(on, 0.0, rest)
    largest = jnp.max(jnp.abs(off), axis=1, keepdims=True)
    largest = jnp.where(largest > 0.0, largest, 1.0)
    unit = off * (1.0 / largest)
    inverse = 1.0 / diagonal
    factor = -largest * inverse
    step_ref[...] = unit * factor
    factor_row = jnp.sum(jnp.where(on, factor, 0.0), axis=0, keepdims=True)
    inverse_row = jnp.sum(jnp.where(on, inverse, 0.0), axis=0, keepdims=True)
    blank = jnp.zeros((1, width), jnp.float32)
    packed_ref[:rows, :] = unit
    packed_ref[rows:, :] = jnp.concatenate(
        [*parts_of(factor_row), *parts_of(inverse_row), blank, blank], axis=0
    )
    own_ref[...] = jnp.concatenate([factor_row, inverse_row] + [blank] * 6, axis=0)
    write.wait()


def dyson_rows(pieces, offsets, steps, level, bare, hamiltonian, two, four, odd, beside):
    rows, width = bare.shape
    count, sides = len(pieces), len(beside)

    def kernel(*refs):
        own, rest = refs[:count], refs[count:]
        named, rest = rest[:8], rest[8:]
        dyson_kernel(own, *named, rest[:sides], *rest[sides:])

    return pl.pallas_call(
        kernel,
        out_shape=(
            jax.ShapeDtypeStruct((FREQS, rows, width), jnp.bfloat16),
            jax.ShapeDtypeStruct((rows + EXTRA, width), jnp.float32),
            jax.ShapeDtypeStruct((rows, width), jnp.float32),
            jax.ShapeDtypeStruct((EXTRA, width), jnp.float32),
        ),
        in_specs=[in_vmem] * count + [in_smem] * 3 + [in_vmem, in_hbm] + [in_vmem] * (3 + sides),
        out_specs=(in_hbm,) + (in_vmem,) * 3,
        scratch_shapes=[VMEM((FREQS, width, width), jnp.bfloat16)] * 2
        + [VMEM((FREQS, rows, width), jnp.bfloat16), VMEM((rows, width), jnp.float32)]
        + [pltpu.SemaphoreType.DMA] * 2,
        compiler_params=large,
        name="dyson",
    )(*pieces, offsets, steps, level, bare, held(hamiltonian), two, four, odd, *beside)


def columns(value, first):
    rows = value.shape[0]
    left, right = value[:, :rows], value[:, rows:]
    return jnp.where(first, left, right), jnp.where(first, right, left)


def begin_kernel(step_ref, packed_ref, own_ref, square_ref, high_ref, low_ref):
    rows, _ = step_ref.shape
    high, low = halves(packed_ref[:rows, :])
    high_ref[...], low_ref[...] = high, low
    near, _ = columns(step_ref[...] * own_ref[0:1], lax.axis_index("rep") == 0)
    square_ref[...] = product(near, high, low)


def finish_kernel(steps_ref, step_ref, square_ref, high_ref, low_ref, theirs_ref, own_ref, out_ref,
                  made, sems):
    rows, _ = step_ref.shape
    rep = lax.axis_index("rep")
    first = rep == 0
    tail = theirs_ref[rows:, :]
    factors = own_ref[0:1] + whole_of(tail[0:1], tail[1:2], tail[2:3])
    inverses = own_ref[1:2] + whole_of(tail[3:4], tail[4:5], tail[5:6])
    theirs = halves(theirs_ref[:rows, :])
    step = step_ref[...]
    _, far = columns(step * factors, first)
    square = square_ref[...] + product(far, *theirs)
    near, far = columns(square * factors, first)
    writes = []
    for half in range(2):
        at = slice(half * rows, (half + 1) * rows)
        cube = product(near, high_ref[:, at], low_ref[:, at]) + product(
            far, theirs[0][:, at], theirs[1][:, at]
        )
        col = lax.broadcasted_iota(jnp.int32, (rows, rows), 1) + half * rows
        row = lax.broadcasted_iota(jnp.int32, (rows, rows), 0) + rep * rows
        total = jnp.where(col == row, 1.0, step[:, at])
        total = total + jnp.where(steps_ref[0] >= 2, square[:, at] + cube, 0.0)
        made[:, at] = total * inverses[:, at]
        writes.append(pltpu.make_async_copy(made.at[:, at], out_ref.at[:, at], sems.at[half]))
        writes[-1].start()
    for write in writes:
        write.wait()


def body(
    green_blocks, occupation, offsets, coulomb, hamiltonian, onsite_level, green_steps, screen_steps
):
    green = green_blocks[0, 0]
    bare = coulomb[0]
    rows, width = green.shape
    share = rows // lax.axis_size("energy")
    make = polar_share if share % 16 == 0 else polar_share_plain
    scalars = (screen_steps, green_steps, onsite_level)
    pieces = gathered(make(green, occupation, offsets, bare, scalars))

    two = shifted(green, "energy", 2)
    four = shifted(two, "energy", 2)
    odd = shifted(chosen(offsets, two, green), "energy", 1)

    slabs = lax.axis_size("slab")
    if slabs == 2:
        beside = [lax.ppermute(green, "slab", [(0, 1), (1, 0)])]
    else:
        up = [(i, i + 1) for i in range(slabs - 1)]
        down = [(j, i) for i, j in up]
        beside = [lax.ppermute(green, "slab", up), lax.ppermute(green, "slab", down)]

    screened, packed, step, own = dyson_rows(
        pieces, offsets, screen_steps, onsite_level, bare, hamiltonian[0], two, four, odd, beside
    )
    theirs = lax.ppermute(packed.astype(coded), "rep", [(0, 1), (1, 0)]).astype(jnp.float32)
    wide = jax.ShapeDtypeStruct((rows, width), jnp.float32)
    thin = jax.ShapeDtypeStruct((rows, width), jnp.bfloat16)
    square, high, low = pl.pallas_call(
        begin_kernel,
        out_shape=(wide, thin, thin),
        in_specs=[in_vmem] * 3,
        out_specs=(in_vmem,) * 3,
        compiler_params=small,
        name="begin",
    )(step, packed, own)
    green_next = pl.pallas_call(
        finish_kernel,
        out_shape=wide,
        in_specs=[in_smem] + [in_vmem] * 6,
        out_specs=in_hbm,
        scratch_shapes=[VMEM((rows, width), jnp.float32), pltpu.SemaphoreType.DMA((2,))],
        compiler_params=large,
        name="finish",
    )(green_steps, step, square, high, low, theirs, own)
    return green_next[None, None], screened[:, None]


def chosen_kernel(offsets_ref, two_ref, green_ref, out_ref):
    three = jnp.minimum(offsets_ref[0], offsets_ref[1]) == 3

    @pl.when(three)
    def _():
        out_ref[...] = two_ref[...]

    @pl.when(jnp.logical_not(three))
    def _():
        out_ref[...] = green_ref[...]


def chosen(offsets, two, green):
    return pl.pallas_call(
        chosen_kernel,
        out_shape=jax.ShapeDtypeStruct(green.shape, green.dtype),
        in_specs=[in_smem, in_vmem, in_vmem],
        out_specs=in_vmem,
        compiler_params=small,
        name="chosen",
    )(offsets, two, green)


def solution(mesh):
    return jax.shard_map(
        body,
        mesh=mesh,
        in_specs=(
            P("energy", "slab", "rep", None),
            P("energy"),
            P(),
            P("slab", "rep", None),
            P("slab", "rep", None),
            P("energy"),
            P("energy"),
            P(),
        ),
        out_specs=(P("energy", "slab", "rep", None), P(None, "slab", "rep", None)),
        check_vma=False,
    )
```

```python
import jax
import jax.numpy as jnp
from jax import lax
from jax.experimental import pallas as pl
from jax.experimental.pallas import tpu as pltpu
from jax.sharding import PartitionSpec as P


SHIFTS = 4
FREQS = 2
EXTRA = 8

coded = jnp.float16
VMEM = pltpu.VMEM
in_vmem = pl.BlockSpec(memory_space=pltpu.VMEM)
in_smem = pl.BlockSpec(memory_space=pltpu.SMEM)
in_place = pl.BlockSpec(memory_space=pl.ANY)
in_hbm = pl.BlockSpec(memory_space=pltpu.HBM)
small = pltpu.CompilerParams(vmem_limit_bytes=6 << 20)
large = pltpu.CompilerParams(vmem_limit_bytes=16 << 20)


def held(value):
    return pltpu.with_memory_space_constraint(value, pltpu.HBM)


def halves(value):
    high = value.astype(jnp.bfloat16)
    return high, (value - high.astype(jnp.float32)).astype(jnp.bfloat16)


def dot(first, second):
    return jnp.dot(first, second, preferred_element_type=jnp.float32)


def product(first, high, low):
    top, rest = halves(first)
    return dot(top, high) + dot(top, low) + dot(rest, high)


def shifted(block, axis, distance):
    count = lax.axis_size(axis)
    return lax.ppermute(block, axis, [(i, (i + distance) % count) for i in range(count)])


def in_squares():
    energies = lax.axis_size("energy")
    return energies % 2 == 0 and energies <= 16 and lax.axis_size("rep") == 2


def share_of(place):
    outer = lax.axis_size("energy") // 2
    return place % 2 * outer + place // 2 if in_squares() else place


def prepare_kernel(weight_ref, block_ref, out_ref, held_rows, read_sems, write_sems):
    energies, padded, width = out_ref.shape
    share = padded - EXTRA
    reads = [
        pltpu.make_async_copy(
            block_ref.at[pl.ds(share_of(k) * share, share), :],
            held_rows.at[k, pl.ds(0, share), :], read_sems.at[k],
        )
        for k in range(energies)
    ]
    for copy in reads:
        copy.start()
    weight = jnp.full((EXTRA, width), weight_ref[0], jnp.float32)
    first = weight.astype(jnp.bfloat16).astype(jnp.float32)
    second = (weight - first).astype(jnp.bfloat16).astype(jnp.float32)
    third = weight - first - second
    row = lax.broadcasted_iota(jnp.int32, (EXTRA, width), 0)
    tail = jnp.where(row == 0, first, jnp.where(row == 1, second, third)).astype(jnp.bfloat16)
    writes = [
        pltpu.make_async_copy(held_rows.at[k], out_ref.at[k], write_sems.at[k])
        for k in range(energies)
    ]
    for k in range(energies):
        held_rows[k, share:, :] = tail
    for k in range(energies):
        reads[k].wait()
        writes[k].start()
    for copy in writes:
        copy.wait()


def polar_kernel(offsets_ref, screen_ref, green_steps_ref, level_ref, got_ref, bare_ref, out_ref, padded, bare_rows, arrived):
    energies, tall, width = got_ref.shape
    share = tall - EXTRA
    start = pl.multiple_of(share_of(lax.axis_index("energy")) * share, share)
    copy = pltpu.make_async_copy(bare_ref.at[pl.ds(start, share), :], bare_rows, arrived)
    copy.start()
    padded[:SHIFTS] = jnp.zeros((SHIFTS, share, width), jnp.float32)
    for e in range(energies):
        padded[SHIFTS + e] = got_ref[e, :share, :].astype(jnp.float32)
    totals = [jnp.zeros((share, width), jnp.float32) for _ in range(FREQS)]
    for e in range(energies):
        tail = got_ref[e, share:, :].astype(jnp.float32)
        weighted = padded[SHIFTS + e] * (tail[0:1] + tail[1:2] + tail[2:3])
        for f in range(FREQS):
            totals[f] += weighted * padded[SHIFTS + e - offsets_ref[f]]
    copy.wait()
    factor = -(width ** -0.5) * energies ** -0.5
    for f in range(FREQS):
        out_ref[f] = totals[f] * (factor * bare_rows[...])


def polar_share(green, weight, offsets, bare, scalars):
    energies = lax.axis_size("energy")
    rows, width = green.shape
    share = rows // energies
    sent = pl.pallas_call(
        prepare_kernel,
        out_shape=jax.ShapeDtypeStruct((energies, share + EXTRA, width), green.dtype),
        in_specs=[in_smem, in_hbm],
        out_specs=in_hbm,
        scratch_shapes=[
            VMEM((energies, share + EXTRA, width), green.dtype),
            pltpu.SemaphoreType.DMA((energies,)),
            pltpu.SemaphoreType.DMA((energies,)),
        ],
        compiler_params=small,
        name="prepare",
    )(weight, held(green))
    got = lax.all_to_all(sent, "energy", 0, 0, tiled=True)
    return pl.pallas_call(
        polar_kernel,
        out_shape=jax.ShapeDtypeStruct((FREQS, share, width), jnp.float32),
        in_specs=[in_smem] * 4 + [in_vmem, in_place],
        out_specs=in_vmem,
        scratch_shapes=[
            VMEM((SHIFTS + energies, share, width), jnp.float32),
            VMEM((share, width), jnp.float32),
            pltpu.SemaphoreType.DMA,
        ],
        compiler_params=small,
        name="polar",
    )(offsets, *scalars, got, bare)


def polar_share_plain(green, weight, offsets, bare, scalars):
    energies = lax.axis_size("energy")
    rows, width = green.shape
    share = rows // energies
    weights = lax.all_gather(weight, "energy", axis=0, tiled=True)
    parts = green.reshape(energies, share, width)
    parts = jnp.stack([parts[share_of(k)] for k in range(energies)]) if in_squares() else parts
    got = lax.all_to_all(parts, "energy", 0, 0, tiled=True)
    wide = got.astype(jnp.float32)
    weighted = wide * weights[:, None, None]
    padded = jnp.concatenate([jnp.zeros((SHIFTS,) + wide.shape[1:], wide.dtype), wide], axis=0)
    own = lax.dynamic_slice_in_dim(bare, share_of(lax.axis_index("energy")) * share, share, 0)
    factor = -(width ** -0.5) * energies ** -0.5
    chunks = []
    for f in range(FREQS):
        low = lax.dynamic_slice_in_dim(padded, SHIFTS - offsets[f], energies, 0)
        chunks.append(factor * own * jnp.sum(weighted * low, axis=0))
    return jnp.stack(chunks)


def gather_energy(chunk):
    outer = lax.axis_size("energy") // 2
    here = lax.axis_index("energy") // 2
    wholes = [
        lax.dynamic_update_index_in_dim(jnp.zeros((outer,) + part.shape, part.dtype), part, here, 0)
        for part in chunk
    ]
    for k in range(outer - 1, 0, -1):
        route = [(z * 2 + x, (z + k) % outer * 2 + x) for z in range(outer) for x in range(2)]
        got = lax.ppermute(chunk, "energy", route)
        wholes = [
            lax.dynamic_update_index_in_dim(whole, part, (here - k) % outer, 0)
            for whole, part in zip(wholes, got)
        ]
    return wholes


def gather_square(parts):
    energies = lax.axis_size("energy")

    def along_x(part):
        return lax.ppermute(part, "energy", [(e, e ^ 1) for e in range(energies)])

    def along_rep(part):
        return lax.ppermute(part, "rep", [(0, 1), (1, 0)])

    beside = [along_x(part) for part in parts]
    above = [along_rep(part) for part in parts]
    apart = [along_rep(beside[0]), along_x(above[1])]
    return [*parts, *beside, *above, *apart]


def gathered(chunk):
    chunk = chunk.astype(coded)
    if in_squares():
        pieces = gather_square(gather_energy(chunk))
    else:
        pieces = [lax.all_gather(chunk, ("rep", "energy"), axis=1, tiled=True)]
    return [piece.astype(jnp.float32) for piece in pieces]


def parts_of(value):
    size = jnp.abs(value)
    exponent = jnp.where(size > 0.0, jnp.floor(jnp.log2(jnp.where(size > 0.0, size, 1.0))), 0.0)
    exponent = jnp.clip(exponent, -120.0, 120.0)
    mantissa = value * jnp.exp2(-exponent)
    first = mantissa.astype(jnp.bfloat16).astype(jnp.float32)
    second = (mantissa - first).astype(jnp.bfloat16).astype(jnp.float32)
    return exponent, first, second


def whole_of(exponent, first, second):
    return (first + second) * jnp.exp2(exponent)


def corner_start(place, block, rows):
    x, rep = lax.axis_index("energy") % 2, lax.axis_index("rep")
    at_x = 1 - x if place % 2 else x
    at_rep = 1 - rep if place >= 2 else rep
    return pl.multiple_of(at_rep * rows + at_x * block, block)


def early_kernel(pieces, bare_ref, once_ref, high, low):
    rows, width = bare_ref.shape
    if len(pieces) == 1:
        for f in range(FREQS):
            high[f], low[f] = halves(pieces[0][f])
    else:
        outer, share, _ = pieces[0].shape
        block = outer * share
        empty = jnp.zeros((block, width), jnp.bfloat16)
        for f in range(FREQS):
            for place in range(4):
                at = pl.ds(corner_start(place, block, rows), block)
                if place == 3:
                    high[f, at, :], low[f, at, :] = empty, empty
                else:
                    upper, lower = halves(pieces[place * FREQS + f][...].reshape(block, width))
                    high[f, at, :], low[f, at, :] = upper, lower
    bare = bare_ref[...]
    for f in range(FREQS):
        once_ref[f] = bare + product(bare, high[f], low[f])


def dyson_kernel(apart, early, offsets_ref, steps_ref, level_ref, bare_ref, hamiltonian_ref, two_ref,
                 four_ref, odd_ref, beside_refs, screened_ref, packed_ref, step_ref, own_ref,
                 high, low, made, hamiltonian_rows, made_sem, hamiltonian_sem):
    once_ref, high_ref, low_ref = early
    rows, width = bare_ref.shape
    entry_scale = width ** -0.5
    read = pltpu.make_async_copy(hamiltonian_ref, hamiltonian_rows, hamiltonian_sem)
    read.start()
    energy, rep = lax.axis_index("energy"), lax.axis_index("rep")
    bare = bare_ref[...]
    once = [once_ref[f] for f in range(FREQS)]
    at = jnp.where(steps_ref[1] > steps_ref[0], 1, 0)
    high[...], low[...] = high_ref[at], low_ref[at]
    if apart:
        outer, share, _ = apart[0].shape
        block = outer * share
        start = corner_start(3, block, rows)
        beyond = bare_ref[:, pl.ds(start, block)]
        parts = [halves(ref[...].reshape(block, width)) for ref in apart]
        once = [once[f] + product(beyond, *parts[f]) for f in range(FREQS)]
        high[pl.ds(start, block), :] = jnp.where(at == 0, parts[0][0], parts[1][0])
        low[pl.ds(start, block), :] = jnp.where(at == 0, parts[0][1], parts[1][1])
    last = jnp.where(at == 0, once[0], once[1])
    upper, lower = high[...], low[...]
    twice = last + product(product(last, upper, lower), upper, lower)
    other = jnp.minimum(offsets_ref[0], offsets_ref[1])
    less = jnp.where(other == 2, two_ref[...], odd_ref[...])
    four = four_ref[...]
    energy_terms = jnp.zeros((rows, width), jnp.float32)
    for f in range(FREQS):
        count = steps_ref[f]
        value = jnp.where(count == 0, bare, jnp.where(count == 1, once[f], twice))
        value = value.astype(jnp.bfloat16)
        made[f] = value
        lowered = jnp.where(offsets_ref[f] == SHIFTS, four, less).astype(jnp.float32)
        lowered = jnp.where(energy >= offsets_ref[f], lowered, 0.0)
        energy_terms += lowered * value.astype(jnp.float32)
    write = pltpu.make_async_copy(made, screened_ref, made_sem)
    write.start()
    read.wait()
    beside = sum(ref[...].astype(jnp.float32) for ref in beside_refs)
    rest = hamiltonian_rows[...] - entry_scale * energy_terms - (0.5 * entry_scale) * beside
    col = lax.broadcasted_iota(jnp.int32, (rows, width), 1)
    row = lax.broadcasted_iota(jnp.int32, (rows, width), 0) + rep * rows
    on = col == row
    diagonal = level_ref[0] + jnp.sum(jnp.where(on, rest, 0.0), axis=1, keepdims=True)
    off = jnp.where(on, 0.0, rest)
    largest = jnp.max(jnp.abs(off), axis=1, keepdims=True)
    largest = jnp.where(largest > 0.0, largest, 1.0)
    unit = off * (1.0 / largest)
    inverse = 1.0 / diagonal
    factor = -largest * inverse
    step_ref[...] = unit * factor
    factor_row = jnp.sum(jnp.where(on, factor, 0.0), axis=0, keepdims=True)
    inverse_row = jnp.sum(jnp.where(on, inverse, 0.0), axis=0, keepdims=True)
    blank = jnp.zeros((1, width), jnp.float32)
    packed_ref[:rows, :] = unit
    packed_ref[rows:, :] = jnp.concatenate(
        [*parts_of(factor_row), *parts_of(inverse_row), blank, blank], axis=0
    )
    own_ref[...] = jnp.concatenate([factor_row, inverse_row] + [blank] * 6, axis=0)
    write.wait()


def dyson_rows(pieces, offsets, steps, level, bare, hamiltonian, two, four, odd, beside):
    rows, width = bare.shape
    sides = len(beside)
    known, apart = (pieces, []) if len(pieces) == 1 else (pieces[:-FREQS], pieces[-FREQS:])
    count = len(known)

    def first_kernel(*refs):
        early_kernel(refs[:count], *refs[count:])

    early = pl.pallas_call(
        first_kernel,
        out_shape=(jax.ShapeDtypeStruct((FREQS, rows, width), jnp.float32),)
        + (jax.ShapeDtypeStruct((FREQS, width, width), jnp.bfloat16),) * 2,
        in_specs=[in_vmem] * (count + 1),
        out_specs=(in_vmem,) * 3,
        compiler_params=large,
        name="early",
    )(*known, bare)

    def kernel(*refs):
        far, rest = refs[:len(apart)], refs[len(apart):]
        done, rest = rest[:3], rest[3:]
        named, rest = rest[:8], rest[8:]
        dyson_kernel(far, done, *named, rest[:sides], *rest[sides:])

    return pl.pallas_call(
        kernel,
        out_shape=(
            jax.ShapeDtypeStruct((FREQS, rows, width), jnp.bfloat16),
            jax.ShapeDtypeStruct((rows + EXTRA, width), jnp.float32),
            jax.ShapeDtypeStruct((rows, width), jnp.float32),
            jax.ShapeDtypeStruct((EXTRA, width), jnp.float32),
        ),
        in_specs=[in_vmem] * (len(apart) + 3) + [in_smem] * 3 + [in_vmem, in_hbm]
        + [in_vmem] * (3 + sides),
        out_specs=(in_hbm,) + (in_vmem,) * 3,
        scratch_shapes=[VMEM((width, width), jnp.bfloat16)] * 2
        + [VMEM((FREQS, rows, width), jnp.bfloat16), VMEM((rows, width), jnp.float32)]
        + [pltpu.SemaphoreType.DMA] * 2,
        compiler_params=large,
        name="dyson",
    )(*apart, *early, offsets, steps, level, bare, held(hamiltonian), two, four, odd, *beside)


def columns(value, first):
    rows = value.shape[0]
    left, right = value[:, :rows], value[:, rows:]
    return jnp.where(first, left, right), jnp.where(first, right, left)


def begin_kernel(step_ref, packed_ref, own_ref, square_ref, high_ref, low_ref):
    rows, _ = step_ref.shape
    high, low = halves(packed_ref[:rows, :])
    high_ref[...], low_ref[...] = high, low
    near, _ = columns(step_ref[...] * own_ref[0:1], lax.axis_index("rep") == 0)
    square_ref[...] = product(near, high, low)


def finish_kernel(steps_ref, step_ref, square_ref, high_ref, low_ref, theirs_ref, own_ref, out_ref,
                  made, sems):
    rows, _ = step_ref.shape
    rep = lax.axis_index("rep")
    first = rep == 0
    tail = theirs_ref[rows:, :]
    factors = own_ref[0:1] + whole_of(tail[0:1], tail[1:2], tail[2:3])
    inverses = own_ref[1:2] + whole_of(tail[3:4], tail[4:5], tail[5:6])
    theirs = halves(theirs_ref[:rows, :])
    step = step_ref[...]
    _, far = columns(step * factors, first)
    square = square_ref[...] + product(far, *theirs)
    near, far = columns(square * factors, first)
    writes = []
    for half in range(2):
        at = slice(half * rows, (half + 1) * rows)
        cube = product(near, high_ref[:, at], low_ref[:, at]) + product(
            far, theirs[0][:, at], theirs[1][:, at]
        )
        col = lax.broadcasted_iota(jnp.int32, (rows, rows), 1) + half * rows
        row = lax.broadcasted_iota(jnp.int32, (rows, rows), 0) + rep * rows
        total = jnp.where(col == row, 1.0, step[:, at])
        total = total + jnp.where(steps_ref[0] >= 2, square[:, at] + cube, 0.0)
        made[:, at] = total * inverses[:, at]
        writes.append(pltpu.make_async_copy(made.at[:, at], out_ref.at[:, at], sems.at[half]))
        writes[-1].start()
    for write in writes:
        write.wait()


def body(
    green_blocks, occupation, offsets, coulomb, hamiltonian, onsite_level, green_steps, screen_steps
):
    green = green_blocks[0, 0]
    bare = coulomb[0]
    rows, width = green.shape
    share = rows // lax.axis_size("energy")
    make = polar_share if share % 16 == 0 else polar_share_plain
    scalars = (screen_steps, green_steps, onsite_level)
    pieces = gathered(make(green, occupation, offsets, bare, scalars))

    two = shifted(green, "energy", 2)
    four = shifted(two, "energy", 2)
    odd = shifted(chosen(offsets, two, green), "energy", 1)

    slabs = lax.axis_size("slab")
    if slabs == 2:
        beside = [lax.ppermute(green, "slab", [(0, 1), (1, 0)])]
    else:
        up = [(i, i + 1) for i in range(slabs - 1)]
        down = [(j, i) for i, j in up]
        beside = [lax.ppermute(green, "slab", up), lax.ppermute(green, "slab", down)]

    screened, packed, step, own = dyson_rows(
        pieces, offsets, screen_steps, onsite_level, bare, hamiltonian[0], two, four, odd, beside
    )
    theirs = lax.ppermute(packed.astype(coded), "rep", [(0, 1), (1, 0)]).astype(jnp.float32)
    wide = jax.ShapeDtypeStruct((rows, width), jnp.float32)
    thin = jax.ShapeDtypeStruct((rows, width), jnp.bfloat16)
    square, high, low = pl.pallas_call(
        begin_kernel,
        out_shape=(wide, thin, thin),
        in_specs=[in_vmem] * 3,
        out_specs=(in_vmem,) * 3,
        compiler_params=small,
        name="begin",
    )(step, packed, own)
    green_next = pl.pallas_call(
        finish_kernel,
        out_shape=wide,
        in_specs=[in_smem] + [in_vmem] * 6,
        out_specs=in_hbm,
        scratch_shapes=[VMEM((rows, width), jnp.float32), pltpu.SemaphoreType.DMA((2,))],
        compiler_params=large,
        name="finish",
    )(green_steps, step, square, high, low, theirs, own)
    return green_next[None, None], screened[:, None]


def chosen_kernel(offsets_ref, two_ref, green_ref, out_ref):
    three = jnp.minimum(offsets_ref[0], offsets_ref[1]) == 3

    @pl.when(three)
    def _():
        out_ref[...] = two_ref[...]

    @pl.when(jnp.logical_not(three))
    def _():
        out_ref[...] = green_ref[...]


def chosen(offsets, two, green):
    return pl.pallas_call(
        chosen_kernel,
        out_shape=jax.ShapeDtypeStruct(green.shape, green.dtype),
        in_specs=[in_smem, in_vmem, in_vmem],
        out_specs=in_vmem,
        compiler_params=small,
        name="chosen",
    )(offsets, two, green)


def solution(mesh):
    return jax.shard_map(
        body,
        mesh=mesh,
        in_specs=(
            P("energy", "slab", "rep", None),
            P("energy"),
            P(),
            P("slab", "rep", None),
            P("slab", "rep", None),
            P("energy"),
            P("energy"),
            P(),
        ),
        out_specs=(P("energy", "slab", "rep", None), P(None, "slab", "rep", None)),
        check_vma=False,
    )
```

```python
import jax
import jax.numpy as jnp
from jax import lax
from jax.experimental import pallas as pl
from jax.experimental.pallas import tpu as pltpu
from jax.sharding import PartitionSpec as P


SHIFTS = 4
FREQS = 2
EXTRA = 8

coded = jnp.float16
VMEM = pltpu.VMEM
in_vmem = pl.BlockSpec(memory_space=pltpu.VMEM)
in_smem = pl.BlockSpec(memory_space=pltpu.SMEM)
in_place = pl.BlockSpec(memory_space=pl.ANY)
in_hbm = pl.BlockSpec(memory_space=pltpu.HBM)
small = pltpu.CompilerParams(vmem_limit_bytes=6 << 20)
large = pltpu.CompilerParams(vmem_limit_bytes=16 << 20)


def held(value):
    return pltpu.with_memory_space_constraint(value, pltpu.HBM)


def halves(value):
    high = value.astype(jnp.bfloat16)
    return high, (value - high.astype(jnp.float32)).astype(jnp.bfloat16)


def dot(first, second):
    return jnp.dot(first, second, preferred_element_type=jnp.float32)


def product(first, high, low):
    top, rest = halves(first)
    return dot(top, high) + dot(top, low) + dot(rest, high)


def shifted(block, axis, distance, around=True):
    count = lax.axis_size(axis)
    route = [(i, (i + distance) % count) for i in range(count if around else count - distance)]
    return lax.ppermute(block, axis, route)


def in_squares():
    energies = lax.axis_size("energy")
    return energies % 2 == 0 and energies <= 16 and lax.axis_size("rep") == 2


def share_of(place):
    outer = lax.axis_size("energy") // 2
    return place % 2 * outer + place // 2 if in_squares() else place


def prepare_kernel(weight_ref, block_ref, out_ref, held_rows, read_sems, write_sems):
    energies, padded, width = out_ref.shape
    share = padded - EXTRA
    reads = [
        pltpu.make_async_copy(
            block_ref.at[pl.ds(share_of(k) * share, share), :],
            held_rows.at[k, pl.ds(0, share), :], read_sems.at[k],
        )
        for k in range(energies)
    ]
    for copy in reads:
        copy.start()
    weight = jnp.full((EXTRA, width), weight_ref[0], jnp.float32)
    first = weight.astype(jnp.bfloat16).astype(jnp.float32)
    second = (weight - first).astype(jnp.bfloat16).astype(jnp.float32)
    third = weight - first - second
    row = lax.broadcasted_iota(jnp.int32, (EXTRA, width), 0)
    tail = jnp.where(row == 0, first, jnp.where(row == 1, second, third)).astype(jnp.bfloat16)
    writes = [
        pltpu.make_async_copy(held_rows.at[k], out_ref.at[k], write_sems.at[k])
        for k in range(energies)
    ]
    for k in range(energies):
        held_rows[k, share:, :] = tail
    for k in range(energies):
        reads[k].wait()
        writes[k].start()
    for copy in writes:
        copy.wait()


def polar_kernel(offsets_ref, screen_ref, green_steps_ref, level_ref, got_ref, bare_ref, out_ref, padded, bare_rows, arrived):
    energies, tall, width = got_ref.shape
    share = tall - EXTRA
    start = pl.multiple_of(share_of(lax.axis_index("energy")) * share, share)
    copy = pltpu.make_async_copy(bare_ref.at[pl.ds(start, share), :], bare_rows, arrived)
    copy.start()
    padded[:SHIFTS] = jnp.zeros((SHIFTS, share, width), jnp.float32)
    for e in range(energies):
        padded[SHIFTS + e] = got_ref[e, :share, :].astype(jnp.float32)
    totals = [jnp.zeros((share, width), jnp.float32) for _ in range(FREQS)]
    for e in range(energies):
        tail = got_ref[e, share:, :].astype(jnp.float32)
        weighted = padded[SHIFTS + e] * (tail[0:1] + tail[1:2] + tail[2:3])
        for f in range(FREQS):
            totals[f] += weighted * padded[SHIFTS + e - offsets_ref[f]]
    copy.wait()
    factor = -(width ** -0.5) * energies ** -0.5
    for f in range(FREQS):
        out_ref[f] = totals[f] * (factor * bare_rows[...])


def polar_share(green, weight, offsets, bare, scalars):
    energies = lax.axis_size("energy")
    rows, width = green.shape
    share = rows // energies
    sent = pl.pallas_call(
        prepare_kernel,
        out_shape=jax.ShapeDtypeStruct((energies, share + EXTRA, width), green.dtype),
        in_specs=[in_smem, in_hbm],
        out_specs=in_hbm,
        scratch_shapes=[
            VMEM((energies, share + EXTRA, width), green.dtype),
            pltpu.SemaphoreType.DMA((energies,)),
            pltpu.SemaphoreType.DMA((energies,)),
        ],
        compiler_params=small,
        name="prepare",
    )(weight, held(green))
    got = lax.all_to_all(sent, "energy", 0, 0, tiled=True)
    return pl.pallas_call(
        polar_kernel,
        out_shape=jax.ShapeDtypeStruct((FREQS, share, width), jnp.float32),
        in_specs=[in_smem] * 4 + [in_vmem, in_place],
        out_specs=in_vmem,
        scratch_shapes=[
            VMEM((SHIFTS + energies, share, width), jnp.float32),
            VMEM((share, width), jnp.float32),
            pltpu.SemaphoreType.DMA,
        ],
        compiler_params=small,
        name="polar",
    )(offsets, *scalars, got, bare)


def polar_share_plain(green, weight, offsets, bare, scalars):
    energies = lax.axis_size("energy")
    rows, width = green.shape
    share = rows // energies
    weights = lax.all_gather(weight, "energy", axis=0, tiled=True)
    parts = green.reshape(energies, share, width)
    parts = jnp.stack([parts[share_of(k)] for k in range(energies)]) if in_squares() else parts
    got = lax.all_to_all(parts, "energy", 0, 0, tiled=True)
    wide = got.astype(jnp.float32)
    weighted = wide * weights[:, None, None]
    padded = jnp.concatenate([jnp.zeros((SHIFTS,) + wide.shape[1:], wide.dtype), wide], axis=0)
    own = lax.dynamic_slice_in_dim(bare, share_of(lax.axis_index("energy")) * share, share, 0)
    factor = -(width ** -0.5) * energies ** -0.5
    chunks = []
    for f in range(FREQS):
        low = lax.dynamic_slice_in_dim(padded, SHIFTS - offsets[f], energies, 0)
        chunks.append(factor * own * jnp.sum(weighted * low, axis=0))
    return jnp.stack(chunks)


def gather_energy(chunk):
    outer = lax.axis_size("energy") // 2
    here = lax.axis_index("energy") // 2
    wholes = [
        lax.dynamic_update_index_in_dim(jnp.zeros((outer,) + part.shape, part.dtype), part, here, 0)
        for part in chunk
    ]
    for k in range(outer - 1, 0, -1):
        route = [(z * 2 + x, (z + k) % outer * 2 + x) for z in range(outer) for x in range(2)]
        got = lax.ppermute(chunk, "energy", route)
        wholes = [
            lax.dynamic_update_index_in_dim(whole, part, (here - k) % outer, 0)
            for whole, part in zip(wholes, got)
        ]
    return wholes


def gather_square(parts):
    energies = lax.axis_size("energy")

    def along_x(part):
        return lax.ppermute(part, "energy", [(e, e ^ 1) for e in range(energies)])

    def along_rep(part):
        return lax.ppermute(part, "rep", [(0, 1), (1, 0)])

    beside = [along_x(part) for part in parts]
    above = [along_rep(part) for part in parts]
    apart = [along_rep(beside[0]), along_x(above[1])]
    return [*parts, *beside, *above, *apart]


def gathered(chunk):
    chunk = chunk.astype(coded)
    if in_squares():
        pieces = gather_square(gather_energy(chunk))
    else:
        pieces = [lax.all_gather(chunk, ("rep", "energy"), axis=1, tiled=True)]
    return [piece.astype(jnp.float32) for piece in pieces]


def parts_of(value):
    size = jnp.abs(value)
    exponent = jnp.where(size > 0.0, jnp.floor(jnp.log2(jnp.where(size > 0.0, size, 1.0))), 0.0)
    exponent = jnp.clip(exponent, -120.0, 120.0)
    mantissa = value * jnp.exp2(-exponent)
    first = mantissa.astype(jnp.bfloat16).astype(jnp.float32)
    second = (mantissa - first).astype(jnp.bfloat16).astype(jnp.float32)
    return exponent, first, second


def whole_of(exponent, first, second):
    return (first + second) * jnp.exp2(exponent)


def corner_start(place, block, rows):
    x, rep = lax.axis_index("energy") % 2, lax.axis_index("rep")
    at_x = 1 - x if place % 2 else x
    at_rep = 1 - rep if place >= 2 else rep
    return pl.multiple_of(at_rep * rows + at_x * block, block)


def early_kernel(pieces, bare_ref, once_ref, high, low):
    rows, width = bare_ref.shape
    if len(pieces) == 1:
        for f in range(FREQS):
            high[f], low[f] = halves(pieces[0][f])
    else:
        outer, share, _ = pieces[0].shape
        block = outer * share
        empty = jnp.zeros((block, width), jnp.bfloat16)
        for f in range(FREQS):
            for place in range(4):
                at = pl.ds(corner_start(place, block, rows), block)
                if place == 3:
                    high[f, at, :], low[f, at, :] = empty, empty
                else:
                    upper, lower = halves(pieces[place * FREQS + f][...].reshape(block, width))
                    high[f, at, :], low[f, at, :] = upper, lower
    bare = bare_ref[...]
    for f in range(FREQS):
        once_ref[f] = bare + product(bare, high[f], low[f])


def dyson_kernel(apart, early, offsets_ref, steps_ref, level_ref, bare_ref, hamiltonian_ref, two_ref,
                 four_ref, odd_ref, beside_refs, screened_ref, packed_ref, step_ref, own_ref,
                 high, low, made, hamiltonian_rows, made_sem, hamiltonian_sem):
    once_ref, high_ref, low_ref = early
    rows, width = bare_ref.shape
    entry_scale = width ** -0.5
    read = pltpu.make_async_copy(hamiltonian_ref, hamiltonian_rows, hamiltonian_sem)
    read.start()
    energy, rep = lax.axis_index("energy"), lax.axis_index("rep")
    bare = bare_ref[...]
    once = [once_ref[f] for f in range(FREQS)]
    at = jnp.where(steps_ref[1] > steps_ref[0], 1, 0)
    high[...], low[...] = high_ref[at], low_ref[at]
    if apart:
        outer, share, _ = apart[0].shape
        block = outer * share
        start = corner_start(3, block, rows)
        beyond = bare_ref[:, pl.ds(start, block)]
        parts = [halves(ref[...].reshape(block, width)) for ref in apart]
        once = [once[f] + product(beyond, *parts[f]) for f in range(FREQS)]
        high[pl.ds(start, block), :] = jnp.where(at == 0, parts[0][0], parts[1][0])
        low[pl.ds(start, block), :] = jnp.where(at == 0, parts[0][1], parts[1][1])
    last = jnp.where(at == 0, once[0], once[1])
    upper, lower = high[...], low[...]
    twice = last + product(product(last, upper, lower), upper, lower)
    other = jnp.minimum(offsets_ref[0], offsets_ref[1])
    less = jnp.where(other == 2, two_ref[...], odd_ref[...])
    four = four_ref[...]
    energy_terms = jnp.zeros((rows, width), jnp.float32)
    for f in range(FREQS):
        count = steps_ref[f]
        value = jnp.where(count == 0, bare, jnp.where(count == 1, once[f], twice))
        value = value.astype(jnp.bfloat16)
        made[f] = value
        lowered = jnp.where(offsets_ref[f] == SHIFTS, four, less).astype(jnp.float32)
        lowered = jnp.where(energy >= offsets_ref[f], lowered, 0.0)
        energy_terms += lowered * value.astype(jnp.float32)
    write = pltpu.make_async_copy(made, screened_ref, made_sem)
    write.start()
    read.wait()
    beside = sum(ref[...].astype(jnp.float32) for ref in beside_refs)
    rest = hamiltonian_rows[...] - entry_scale * energy_terms - (0.5 * entry_scale) * beside
    col = lax.broadcasted_iota(jnp.int32, (rows, width), 1)
    row = lax.broadcasted_iota(jnp.int32, (rows, width), 0) + rep * rows
    on = col == row
    diagonal = level_ref[0] + jnp.sum(jnp.where(on, rest, 0.0), axis=1, keepdims=True)
    off = jnp.where(on, 0.0, rest)
    largest = jnp.max(jnp.abs(off), axis=1, keepdims=True)
    largest = jnp.where(largest > 0.0, largest, 1.0)
    unit = off * (1.0 / largest)
    inverse = 1.0 / diagonal
    factor = -largest * inverse
    step_ref[...] = unit * factor
    factor_row = jnp.sum(jnp.where(on, factor, 0.0), axis=0, keepdims=True)
    inverse_row = jnp.sum(jnp.where(on, inverse, 0.0), axis=0, keepdims=True)
    blank = jnp.zeros((1, width), jnp.float32)
    packed_ref[:rows, :] = unit
    packed_ref[rows:, :] = jnp.concatenate(
        [*parts_of(factor_row), *parts_of(inverse_row), blank, blank], axis=0
    )
    own_ref[...] = jnp.concatenate([factor_row, inverse_row] + [blank] * 6, axis=0)
    write.wait()


def dyson_rows(pieces, offsets, steps, level, bare, hamiltonian, two, four, odd, beside):
    rows, width = bare.shape
    sides = len(beside)
    known, apart = (pieces, []) if len(pieces) == 1 else (pieces[:-FREQS], pieces[-FREQS:])
    count = len(known)

    def first_kernel(*refs):
        early_kernel(refs[:count], *refs[count:])

    early = pl.pallas_call(
        first_kernel,
        out_shape=(jax.ShapeDtypeStruct((FREQS, rows, width), jnp.float32),)
        + (jax.ShapeDtypeStruct((FREQS, width, width), jnp.bfloat16),) * 2,
        in_specs=[in_vmem] * (count + 1),
        out_specs=(in_vmem,) * 3,
        compiler_params=large,
        name="early",
    )(*known, bare)

    def kernel(*refs):
        far, rest = refs[:len(apart)], refs[len(apart):]
        done, rest = rest[:3], rest[3:]
        named, rest = rest[:8], rest[8:]
        dyson_kernel(far, done, *named, rest[:sides], *rest[sides:])

    return pl.pallas_call(
        kernel,
        out_shape=(
            jax.ShapeDtypeStruct((FREQS, rows, width), jnp.bfloat16),
            jax.ShapeDtypeStruct((rows + EXTRA, width), jnp.float32),
            jax.ShapeDtypeStruct((rows, width), jnp.float32),
            jax.ShapeDtypeStruct((EXTRA, width), jnp.float32),
        ),
        in_specs=[in_vmem] * (len(apart) + 3) + [in_smem] * 3 + [in_vmem, in_hbm]
        + [in_vmem] * (3 + sides),
        out_specs=(in_hbm,) + (in_vmem,) * 3,
        scratch_shapes=[VMEM((width, width), jnp.bfloat16)] * 2
        + [VMEM((FREQS, rows, width), jnp.bfloat16), VMEM((rows, width), jnp.float32)]
        + [pltpu.SemaphoreType.DMA] * 2,
        compiler_params=large,
        name="dyson",
    )(*apart, *early, offsets, steps, level, bare, held(hamiltonian), two, four, odd, *beside)


def columns(value, first):
    rows = value.shape[0]
    left, right = value[:, :rows], value[:, rows:]
    return jnp.where(first, left, right), jnp.where(first, right, left)


def begin_kernel(step_ref, packed_ref, own_ref, square_ref, high_ref, low_ref):
    rows, _ = step_ref.shape
    high, low = halves(packed_ref[:rows, :])
    high_ref[...], low_ref[...] = high, low
    near, _ = columns(step_ref[...] * own_ref[0:1], lax.axis_index("rep") == 0)
    square_ref[...] = product(near, high, low)


def finish_kernel(steps_ref, step_ref, square_ref, high_ref, low_ref, theirs_ref, own_ref, out_ref,
                  made, sems):
    rows, _ = step_ref.shape
    rep = lax.axis_index("rep")
    first = rep == 0
    tail = theirs_ref[rows:, :]
    factors = own_ref[0:1] + whole_of(tail[0:1], tail[1:2], tail[2:3])
    inverses = own_ref[1:2] + whole_of(tail[3:4], tail[4:5], tail[5:6])
    theirs = halves(theirs_ref[:rows, :])
    step = step_ref[...]
    _, far = columns(step * factors, first)
    square = square_ref[...] + product(far, *theirs)
    near, far = columns(square * factors, first)
    writes = []
    for half in range(2):
        at = slice(half * rows, (half + 1) * rows)
        cube = product(near, high_ref[:, at], low_ref[:, at]) + product(
            far, theirs[0][:, at], theirs[1][:, at]
        )
        col = lax.broadcasted_iota(jnp.int32, (rows, rows), 1) + half * rows
        row = lax.broadcasted_iota(jnp.int32, (rows, rows), 0) + rep * rows
        total = jnp.where(col == row, 1.0, step[:, at])
        total = total + jnp.where(steps_ref[0] >= 2, square[:, at] + cube, 0.0)
        made[:, at] = total * inverses[:, at]
        writes.append(pltpu.make_async_copy(made.at[:, at], out_ref.at[:, at], sems.at[half]))
        writes[-1].start()
    for write in writes:
        write.wait()


def body(
    green_blocks, occupation, offsets, coulomb, hamiltonian, onsite_level, green_steps, screen_steps
):
    green = green_blocks[0, 0]
    bare = coulomb[0]
    rows, width = green.shape
    share = rows // lax.axis_size("energy")
    make = polar_share if share % 16 == 0 else polar_share_plain
    scalars = (screen_steps, green_steps, onsite_level)
    pieces = gathered(make(green, occupation, offsets, bare, scalars))

    two = shifted(green, "energy", 2, around=False)
    four = shifted(two, "energy", 2)
    odd = shifted(chosen(offsets, two, green), "energy", 1)

    slabs = lax.axis_size("slab")
    if slabs == 2:
        beside = [lax.ppermute(green, "slab", [(0, 1), (1, 0)])]
    else:
        up = [(i, i + 1) for i in range(slabs - 1)]
        down = [(j, i) for i, j in up]
        beside = [lax.ppermute(green, "slab", up), lax.ppermute(green, "slab", down)]

    screened, packed, step, own = dyson_rows(
        pieces, offsets, screen_steps, onsite_level, bare, hamiltonian[0], two, four, odd, beside
    )
    theirs = lax.ppermute(packed.astype(coded), "rep", [(0, 1), (1, 0)]).astype(jnp.float32)
    wide = jax.ShapeDtypeStruct((rows, width), jnp.float32)
    thin = jax.ShapeDtypeStruct((rows, width), jnp.bfloat16)
    square, high, low = pl.pallas_call(
        begin_kernel,
        out_shape=(wide, thin, thin),
        in_specs=[in_vmem] * 3,
        out_specs=(in_vmem,) * 3,
        compiler_params=small,
        name="begin",
    )(step, packed, own)
    green_next = pl.pallas_call(
        finish_kernel,
        out_shape=wide,
        in_specs=[in_smem] + [in_vmem] * 6,
        out_specs=in_hbm,
        scratch_shapes=[VMEM((rows, width), jnp.float32), pltpu.SemaphoreType.DMA((2,))],
        compiler_params=large,
        name="finish",
    )(green_steps, step, square, high, low, theirs, own)
    return green_next[None, None], screened[:, None]


def chosen_kernel(offsets_ref, two_ref, green_ref, out_ref):
    three = jnp.minimum(offsets_ref[0], offsets_ref[1]) == 3

    @pl.when(three)
    def _():
        out_ref[...] = two_ref[...]

    @pl.when(jnp.logical_not(three))
    def _():
        out_ref[...] = green_ref[...]


def chosen(offsets, two, green):
    return pl.pallas_call(
        chosen_kernel,
        out_shape=jax.ShapeDtypeStruct(green.shape, green.dtype),
        in_specs=[in_smem, in_vmem, in_vmem],
        out_specs=in_vmem,
        compiler_params=small,
        name="chosen",
    )(offsets, two, green)


def solution(mesh):
    return jax.shard_map(
        body,
        mesh=mesh,
        in_specs=(
            P("energy", "slab", "rep", None),
            P("energy"),
            P(),
            P("slab", "rep", None),
            P("slab", "rep", None),
            P("energy"),
            P("energy"),
            P(),
        ),
        out_specs=(P("energy", "slab", "rep", None), P(None, "slab", "rep", None)),
        check_vma=False,
    )
```

```python
import jax
import jax.numpy as jnp
from jax import lax
from jax.experimental import pallas as pl
from jax.experimental.pallas import tpu as pltpu
from jax.sharding import PartitionSpec as P


SHIFTS = 4
FREQS = 2
EXTRA = 8

coded = jnp.float16
VMEM = pltpu.VMEM
in_vmem = pl.BlockSpec(memory_space=pltpu.VMEM)
in_smem = pl.BlockSpec(memory_space=pltpu.SMEM)
in_place = pl.BlockSpec(memory_space=pl.ANY)
in_hbm = pl.BlockSpec(memory_space=pltpu.HBM)
small = pltpu.CompilerParams(vmem_limit_bytes=6 << 20)
large = pltpu.CompilerParams(vmem_limit_bytes=16 << 20)


def held(value):
    return pltpu.with_memory_space_constraint(value, pltpu.HBM)


def halves(value):
    high = value.astype(jnp.bfloat16)
    return high, (value - high.astype(jnp.float32)).astype(jnp.bfloat16)


def dot(first, second):
    return jnp.dot(first, second, preferred_element_type=jnp.float32)


def product(first, high, low):
    top, rest = halves(first)
    return dot(top, high) + dot(top, low) + dot(rest, high)


def shifted(block, axis, distance):
    count = lax.axis_size(axis)
    route = [(i, i + distance) for i in range(count - distance)]
    return lax.ppermute(block, axis, route)


def in_squares():
    energies = lax.axis_size("energy")
    return energies % 2 == 0 and energies <= 16 and lax.axis_size("rep") == 2


def share_of(place):
    outer = lax.axis_size("energy") // 2
    return place % 2 * outer + place // 2 if in_squares() else place


def prepare_kernel(weight_ref, block_ref, out_ref, held_rows, read_sems, write_sems):
    energies, padded, width = out_ref.shape
    share = padded - EXTRA
    reads = [
        pltpu.make_async_copy(
            block_ref.at[pl.ds(share_of(k) * share, share), :],
            held_rows.at[k, pl.ds(0, share), :], read_sems.at[k],
        )
        for k in range(energies)
    ]
    for copy in reads:
        copy.start()
    weight = jnp.full((EXTRA, width), weight_ref[0], jnp.float32)
    first = weight.astype(jnp.bfloat16).astype(jnp.float32)
    second = (weight - first).astype(jnp.bfloat16).astype(jnp.float32)
    third = weight - first - second
    row = lax.broadcasted_iota(jnp.int32, (EXTRA, width), 0)
    tail = jnp.where(row == 0, first, jnp.where(row == 1, second, third)).astype(jnp.bfloat16)
    writes = [
        pltpu.make_async_copy(held_rows.at[k], out_ref.at[k], write_sems.at[k])
        for k in range(energies)
    ]
    for k in range(energies):
        held_rows[k, share:, :] = tail
    for k in range(energies):
        reads[k].wait()
        writes[k].start()
    for copy in writes:
        copy.wait()


def polar_kernel(offsets_ref, screen_ref, green_steps_ref, level_ref, got_ref, bare_ref, out_ref, padded, bare_rows, arrived):
    energies, tall, width = got_ref.shape
    share = tall - EXTRA
    start = pl.multiple_of(share_of(lax.axis_index("energy")) * share, share)
    copy = pltpu.make_async_copy(bare_ref.at[pl.ds(start, share), :], bare_rows, arrived)
    copy.start()
    padded[:SHIFTS] = jnp.zeros((SHIFTS, share, width), jnp.float32)
    for e in range(energies):
        padded[SHIFTS + e] = got_ref[e, :share, :].astype(jnp.float32)
    totals = [jnp.zeros((share, width), jnp.float32) for _ in range(FREQS)]
    for e in range(energies):
        tail = got_ref[e, share:, :].astype(jnp.float32)
        weighted = padded[SHIFTS + e] * (tail[0:1] + tail[1:2] + tail[2:3])
        for f in range(FREQS):
            totals[f] += weighted * padded[SHIFTS + e - offsets_ref[f]]
    copy.wait()
    factor = -(width ** -0.5) * energies ** -0.5
    for f in range(FREQS):
        out_ref[f] = totals[f] * (factor * bare_rows[...])


def polar_share(green, weight, offsets, bare, scalars):
    energies = lax.axis_size("energy")
    rows, width = green.shape
    share = rows // energies
    sent = pl.pallas_call(
        prepare_kernel,
        out_shape=jax.ShapeDtypeStruct((energies, share + EXTRA, width), green.dtype),
        in_specs=[in_smem, in_hbm],
        out_specs=in_hbm,
        scratch_shapes=[
            VMEM((energies, share + EXTRA, width), green.dtype),
            pltpu.SemaphoreType.DMA((energies,)),
            pltpu.SemaphoreType.DMA((energies,)),
        ],
        compiler_params=small,
        name="prepare",
    )(weight, held(green))
    got = lax.all_to_all(sent, "energy", 0, 0, tiled=True)
    return pl.pallas_call(
        polar_kernel,
        out_shape=jax.ShapeDtypeStruct((FREQS, share, width), jnp.float32),
        in_specs=[in_smem] * 4 + [in_vmem, in_place],
        out_specs=in_vmem,
        scratch_shapes=[
            VMEM((SHIFTS + energies, share, width), jnp.float32),
            VMEM((share, width), jnp.float32),
            pltpu.SemaphoreType.DMA,
        ],
        compiler_params=small,
        name="polar",
    )(offsets, *scalars, got, bare)


def polar_share_plain(green, weight, offsets, bare, scalars):
    energies = lax.axis_size("energy")
    rows, width = green.shape
    share = rows // energies
    weights = lax.all_gather(weight, "energy", axis=0, tiled=True)
    parts = green.reshape(energies, share, width)
    parts = jnp.stack([parts[share_of(k)] for k in range(energies)]) if in_squares() else parts
    got = lax.all_to_all(parts, "energy", 0, 0, tiled=True)
    wide = got.astype(jnp.float32)
    weighted = wide * weights[:, None, None]
    padded = jnp.concatenate([jnp.zeros((SHIFTS,) + wide.shape[1:], wide.dtype), wide], axis=0)
    own = lax.dynamic_slice_in_dim(bare, share_of(lax.axis_index("energy")) * share, share, 0)
    factor = -(width ** -0.5) * energies ** -0.5
    chunks = []
    for f in range(FREQS):
        low = lax.dynamic_slice_in_dim(padded, SHIFTS - offsets[f], energies, 0)
        chunks.append(factor * own * jnp.sum(weighted * low, axis=0))
    return jnp.stack(chunks)


def gather_energy(chunk):
    outer = lax.axis_size("energy") // 2
    here = lax.axis_index("energy") // 2
    wholes = [
        lax.dynamic_update_index_in_dim(jnp.zeros((outer,) + part.shape, part.dtype), part, here, 0)
        for part in chunk
    ]
    for k in range(outer - 1, 0, -1):
        route = [(z * 2 + x, (z + k) % outer * 2 + x) for z in range(outer) for x in range(2)]
        got = lax.ppermute(chunk, "energy", route)
        wholes = [
            lax.dynamic_update_index_in_dim(whole, part, (here - k) % outer, 0)
            for whole, part in zip(wholes, got)
        ]
    return wholes


def gather_square(parts):
    energies = lax.axis_size("energy")

    def along_x(part):
        return lax.ppermute(part, "energy", [(e, e ^ 1) for e in range(energies)])

    def along_rep(part):
        return lax.ppermute(part, "rep", [(0, 1), (1, 0)])

    beside = [along_x(part) for part in parts]
    above = [along_rep(part) for part in parts]
    apart = [along_rep(beside[0]), along_x(above[1])]
    return [*parts, *beside, *above, *apart]


def gathered(chunk):
    chunk = chunk.astype(coded)
    if in_squares():
        pieces = gather_square(gather_energy(chunk))
    else:
        pieces = [lax.all_gather(chunk, ("rep", "energy"), axis=1, tiled=True)]
    return [piece.astype(jnp.float32) for piece in pieces]


def parts_of(value):
    size = jnp.abs(value)
    exponent = jnp.where(size > 0.0, jnp.floor(jnp.log2(jnp.where(size > 0.0, size, 1.0))), 0.0)
    exponent = jnp.clip(exponent, -120.0, 120.0)
    mantissa = value * jnp.exp2(-exponent)
    first = mantissa.astype(jnp.bfloat16).astype(jnp.float32)
    second = (mantissa - first).astype(jnp.bfloat16).astype(jnp.float32)
    return exponent, first, second


def whole_of(exponent, first, second):
    return (first + second) * jnp.exp2(exponent)


def corner_start(place, block, rows):
    x, rep = lax.axis_index("energy") % 2, lax.axis_index("rep")
    at_x = 1 - x if place % 2 else x
    at_rep = 1 - rep if place >= 2 else rep
    return pl.multiple_of(at_rep * rows + at_x * block, block)


def early_kernel(pieces, bare_ref, once_ref, high, low):
    rows, width = bare_ref.shape
    if len(pieces) == 1:
        for f in range(FREQS):
            high[f], low[f] = halves(pieces[0][f])
    else:
        outer, share, _ = pieces[0].shape
        block = outer * share
        empty = jnp.zeros((block, width), jnp.bfloat16)
        for f in range(FREQS):
            for place in range(4):
                at = pl.ds(corner_start(place, block, rows), block)
                if place == 3:
                    high[f, at, :], low[f, at, :] = empty, empty
                else:
                    upper, lower = halves(pieces[place * FREQS + f][...].reshape(block, width))
                    high[f, at, :], low[f, at, :] = upper, lower
    bare = bare_ref[...]
    for f in range(FREQS):
        once_ref[f] = bare + product(bare, high[f], low[f])


def dyson_kernel(apart, early, offsets_ref, steps_ref, level_ref, bare_ref, hamiltonian_ref, two_ref,
                 four_ref, odd_ref, beside_refs, screened_ref, packed_ref, step_ref, own_ref,
                 high, low, made, hamiltonian_rows, made_sem, hamiltonian_sem):
    once_ref, high_ref, low_ref = early
    rows, width = bare_ref.shape
    entry_scale = width ** -0.5
    read = pltpu.make_async_copy(hamiltonian_ref, hamiltonian_rows, hamiltonian_sem)
    read.start()
    rep = lax.axis_index("rep")
    bare = bare_ref[...]
    once = [once_ref[f] for f in range(FREQS)]
    at = jnp.where(steps_ref[1] > steps_ref[0], 1, 0)
    high[...], low[...] = high_ref[at], low_ref[at]
    if apart:
        outer, share, _ = apart[0].shape
        block = outer * share
        start = corner_start(3, block, rows)
        beyond = bare_ref[:, pl.ds(start, block)]
        parts = [halves(ref[...].reshape(block, width)) for ref in apart]
        once = [once[f] + product(beyond, *parts[f]) for f in range(FREQS)]
        high[pl.ds(start, block), :] = jnp.where(at == 0, parts[0][0], parts[1][0])
        low[pl.ds(start, block), :] = jnp.where(at == 0, parts[0][1], parts[1][1])
    last = jnp.where(at == 0, once[0], once[1])
    upper, lower = high[...], low[...]
    twice = last + product(product(last, upper, lower), upper, lower)
    other = jnp.minimum(offsets_ref[0], offsets_ref[1])
    less = jnp.where(other == 2, two_ref[...], odd_ref[...])
    four = four_ref[...]
    energy_terms = jnp.zeros((rows, width), jnp.float32)
    for f in range(FREQS):
        count = steps_ref[f]
        value = jnp.where(count == 0, bare, jnp.where(count == 1, once[f], twice))
        value = value.astype(jnp.bfloat16)
        made[f] = value
        lowered = jnp.where(offsets_ref[f] == SHIFTS, four, less).astype(jnp.float32)
        energy_terms += lowered * value.astype(jnp.float32)
    write = pltpu.make_async_copy(made, screened_ref, made_sem)
    write.start()
    read.wait()
    beside = sum(ref[...].astype(jnp.float32) for ref in beside_refs)
    rest = hamiltonian_rows[...] - entry_scale * energy_terms - (0.5 * entry_scale) * beside
    col = lax.broadcasted_iota(jnp.int32, (rows, width), 1)
    row = lax.broadcasted_iota(jnp.int32, (rows, width), 0) + rep * rows
    on = col == row
    diagonal = level_ref[0] + jnp.sum(jnp.where(on, rest, 0.0), axis=1, keepdims=True)
    off = jnp.where(on, 0.0, rest)
    largest = jnp.max(jnp.abs(off), axis=1, keepdims=True)
    largest = jnp.where(largest > 0.0, largest, 1.0)
    unit = off * (1.0 / largest)
    inverse = 1.0 / diagonal
    factor = -largest * inverse
    step_ref[...] = unit * factor
    factor_row = jnp.sum(jnp.where(on, factor, 0.0), axis=0, keepdims=True)
    inverse_row = jnp.sum(jnp.where(on, inverse, 0.0), axis=0, keepdims=True)
    blank = jnp.zeros((1, width), jnp.float32)
    packed_ref[:rows, :] = unit
    packed_ref[rows:, :] = jnp.concatenate(
        [*parts_of(factor_row), *parts_of(inverse_row), blank, blank], axis=0
    )
    own_ref[...] = jnp.concatenate([factor_row, inverse_row] + [blank] * 6, axis=0)
    write.wait()


def dyson_rows(pieces, offsets, steps, level, bare, hamiltonian, two, four, odd, beside):
    rows, width = bare.shape
    sides = len(beside)
    known, apart = (pieces, []) if len(pieces) == 1 else (pieces[:-FREQS], pieces[-FREQS:])
    count = len(known)

    def first_kernel(*refs):
        early_kernel(refs[:count], *refs[count:])

    early = pl.pallas_call(
        first_kernel,
        out_shape=(jax.ShapeDtypeStruct((FREQS, rows, width), jnp.float32),)
        + (jax.ShapeDtypeStruct((FREQS, width, width), jnp.bfloat16),) * 2,
        in_specs=[in_vmem] * (count + 1),
        out_specs=(in_vmem,) * 3,
        compiler_params=large,
        name="early",
    )(*known, bare)

    def kernel(*refs):
        far, rest = refs[:len(apart)], refs[len(apart):]
        done, rest = rest[:3], rest[3:]
        named, rest = rest[:8], rest[8:]
        dyson_kernel(far, done, *named, rest[:sides], *rest[sides:])

    return pl.pallas_call(
        kernel,
        out_shape=(
            jax.ShapeDtypeStruct((FREQS, rows, width), jnp.bfloat16),
            jax.ShapeDtypeStruct((rows + EXTRA, width), jnp.float32),
            jax.ShapeDtypeStruct((rows, width), jnp.float32),
            jax.ShapeDtypeStruct((EXTRA, width), jnp.float32),
        ),
        in_specs=[in_vmem] * (len(apart) + 3) + [in_smem] * 3 + [in_vmem, in_hbm]
        + [in_vmem] * (3 + sides),
        out_specs=(in_hbm,) + (in_vmem,) * 3,
        scratch_shapes=[VMEM((width, width), jnp.bfloat16)] * 2
        + [VMEM((FREQS, rows, width), jnp.bfloat16), VMEM((rows, width), jnp.float32)]
        + [pltpu.SemaphoreType.DMA] * 2,
        compiler_params=large,
        name="dyson",
    )(*apart, *early, offsets, steps, level, bare, held(hamiltonian), two, four, odd, *beside)


def columns(value, first):
    rows = value.shape[0]
    left, right = value[:, :rows], value[:, rows:]
    return jnp.where(first, left, right), jnp.where(first, right, left)


def begin_kernel(step_ref, packed_ref, own_ref, square_ref, high_ref, low_ref):
    rows, _ = step_ref.shape
    high, low = halves(packed_ref[:rows, :])
    high_ref[...], low_ref[...] = high, low
    near, _ = columns(step_ref[...] * own_ref[0:1], lax.axis_index("rep") == 0)
    square_ref[...] = product(near, high, low)


def finish_kernel(steps_ref, step_ref, square_ref, high_ref, low_ref, theirs_ref, own_ref, out_ref,
                  made, sems):
    rows, _ = step_ref.shape
    rep = lax.axis_index("rep")
    first = rep == 0
    tail = theirs_ref[rows:, :]
    factors = own_ref[0:1] + whole_of(tail[0:1], tail[1:2], tail[2:3])
    inverses = own_ref[1:2] + whole_of(tail[3:4], tail[4:5], tail[5:6])
    theirs = halves(theirs_ref[:rows, :])
    step = step_ref[...]
    _, far = columns(step * factors, first)
    square = square_ref[...] + product(far, *theirs)
    near, far = columns(square * factors, first)
    writes = []
    for half in range(2):
        at = slice(half * rows, (half + 1) * rows)
        cube = product(near, high_ref[:, at], low_ref[:, at]) + product(
            far, theirs[0][:, at], theirs[1][:, at]
        )
        col = lax.broadcasted_iota(jnp.int32, (rows, rows), 1) + half * rows
        row = lax.broadcasted_iota(jnp.int32, (rows, rows), 0) + rep * rows
        total = jnp.where(col == row, 1.0, step[:, at])
        total = total + jnp.where(steps_ref[0] >= 2, square[:, at] + cube, 0.0)
        made[:, at] = total * inverses[:, at]
        writes.append(pltpu.make_async_copy(made.at[:, at], out_ref.at[:, at], sems.at[half]))
        writes[-1].start()
    for write in writes:
        write.wait()


def body(
    green_blocks, occupation, offsets, coulomb, hamiltonian, onsite_level, green_steps, screen_steps
):
    green = green_blocks[0, 0]
    bare = coulomb[0]
    rows, width = green.shape
    share = rows // lax.axis_size("energy")
    make = polar_share if share % 16 == 0 else polar_share_plain
    scalars = (screen_steps, green_steps, onsite_level)
    pieces = gathered(make(green, occupation, offsets, bare, scalars))

    two = shifted(green, "energy", 2)
    four = shifted(two, "energy", 2)
    odd = shifted(chosen(offsets, two, green), "energy", 1)

    slabs = lax.axis_size("slab")
    if slabs == 2:
        beside = [lax.ppermute(green, "slab", [(0, 1), (1, 0)])]
    else:
        up = [(i, i + 1) for i in range(slabs - 1)]
        down = [(j, i) for i, j in up]
        beside = [lax.ppermute(green, "slab", up), lax.ppermute(green, "slab", down)]

    screened, packed, step, own = dyson_rows(
        pieces, offsets, screen_steps, onsite_level, bare, hamiltonian[0], two, four, odd, beside
    )
    theirs = lax.ppermute(packed.astype(coded), "rep", [(0, 1), (1, 0)]).astype(jnp.float32)
    wide = jax.ShapeDtypeStruct((rows, width), jnp.float32)
    thin = jax.ShapeDtypeStruct((rows, width), jnp.bfloat16)
    square, high, low = pl.pallas_call(
        begin_kernel,
        out_shape=(wide, thin, thin),
        in_specs=[in_vmem] * 3,
        out_specs=(in_vmem,) * 3,
        compiler_params=small,
        name="begin",
    )(step, packed, own)
    green_next = pl.pallas_call(
        finish_kernel,
        out_shape=wide,
        in_specs=[in_smem] + [in_vmem] * 6,
        out_specs=in_hbm,
        scratch_shapes=[VMEM((rows, width), jnp.float32), pltpu.SemaphoreType.DMA((2,))],
        compiler_params=large,
        name="finish",
    )(green_steps, step, square, high, low, theirs, own)
    return green_next[None, None], screened[:, None]


def chosen_kernel(offsets_ref, two_ref, green_ref, out_ref):
    three = jnp.minimum(offsets_ref[0], offsets_ref[1]) == 3

    @pl.when(three)
    def _():
        out_ref[...] = two_ref[...]

    @pl.when(jnp.logical_not(three))
    def _():
        out_ref[...] = green_ref[...]


def chosen(offsets, two, green):
    return pl.pallas_call(
        chosen_kernel,
        out_shape=jax.ShapeDtypeStruct(green.shape, green.dtype),
        in_specs=[in_smem, in_vmem, in_vmem],
        out_specs=in_vmem,
        compiler_params=small,
        name="chosen",
    )(offsets, two, green)


def solution(mesh):
    return jax.shard_map(
        body,
        mesh=mesh,
        in_specs=(
            P("energy", "slab", "rep", None),
            P("energy"),
            P(),
            P("slab", "rep", None),
            P("slab", "rep", None),
            P("energy"),
            P("energy"),
            P(),
        ),
        out_specs=(P("energy", "slab", "rep", None), P(None, "slab", "rep", None)),
        check_vma=False,
    )
```

```python
import jax
import jax.numpy as jnp
from jax import lax
from jax.experimental import pallas as pl
from jax.experimental.pallas import tpu as pltpu
from jax.sharding import PartitionSpec as P


SHIFTS = 4
FREQS = 2
EXTRA = 8

coded = jnp.float16
VMEM = pltpu.VMEM
in_vmem = pl.BlockSpec(memory_space=pltpu.VMEM)
in_smem = pl.BlockSpec(memory_space=pltpu.SMEM)
in_place = pl.BlockSpec(memory_space=pl.ANY)
in_hbm = pl.BlockSpec(memory_space=pltpu.HBM)
small = pltpu.CompilerParams(vmem_limit_bytes=6 << 20)
large = pltpu.CompilerParams(vmem_limit_bytes=16 << 20)


def held(value):
    return pltpu.with_memory_space_constraint(value, pltpu.HBM)


def halves(value):
    high = value.astype(jnp.bfloat16)
    return high, (value - high.astype(jnp.float32)).astype(jnp.bfloat16)


def dot(first, second):
    return jnp.dot(first, second, preferred_element_type=jnp.float32)


def product(first, high, low):
    top, rest = halves(first)
    return dot(top, high) + dot(top, low) + dot(rest, high)


def shifted(block, axis, distance):
    count = lax.axis_size(axis)
    route = [(i, i + distance) for i in range(count - distance)]
    return lax.ppermute(block, axis, route)


def in_squares():
    energies = lax.axis_size("energy")
    return energies % 2 == 0 and energies <= 16 and lax.axis_size("rep") == 2


def share_of(place):
    outer = lax.axis_size("energy") // 2
    return place % 2 * outer + place // 2 if in_squares() else place


def weight_rows(weight, first_row, width):
    weight = jnp.full((EXTRA, width), weight, jnp.float32)
    first = weight.astype(jnp.bfloat16).astype(jnp.float32)
    second = (weight - first).astype(jnp.bfloat16).astype(jnp.float32)
    third = weight - first - second
    row = lax.broadcasted_iota(jnp.int32, (EXTRA, width), 0) - first_row
    later = jnp.where(row == 1, second, jnp.where(row == 2, third, 0.0))
    return jnp.where(row == 0, first, later)


def prepare_kernel(weight_ref, block_ref, out_ref, arrived):
    half, width = out_ref.shape[0] - EXTRA, out_ref.shape[1]
    x = lax.axis_index("energy") % 2
    start = pl.multiple_of((1 - x) * half, half)
    copy = pltpu.make_async_copy(
        block_ref.at[pl.ds(start, half), :], out_ref.at[pl.ds(0, half), :], arrived
    )
    copy.start()
    out_ref[half:, :] = weight_rows(weight_ref[0], 3, width).astype(out_ref.dtype)
    copy.wait()


def arrange_kernel(weight_ref, block_ref, got_ref, *out_refs):
    outer = len(out_refs) + 1
    half, width = got_ref.shape[0] - EXTRA, got_ref.shape[1]
    share = half // outer
    x, z = lax.axis_index("energy") % 2, lax.axis_index("energy") // 2
    tail = weight_rows(weight_ref[0], 0, width) + got_ref[half:, :].astype(jnp.float32)
    tail = tail.astype(got_ref.dtype)
    for k, out_ref in enumerate(out_refs, 1):
        at = (z + k) % outer * share
        mine = pl.ds(pl.multiple_of(x * half + at, share), share)
        out_ref[:share, :] = block_ref[mine, :]
        out_ref[share:2 * share, :] = got_ref[pl.ds(pl.multiple_of(at, share), share), :]
        out_ref[2 * share:, :] = tail


def polar_kernel(received, weight_ref, offsets_ref, block_ref, got_ref, bare_ref, out_ref,
                 padded, weighted, bare_rows, arrived):
    _, share, width = out_ref.shape
    energies = weighted.shape[0]
    outer = energies // 2
    half = outer * share
    energy = lax.axis_index("energy")
    x, z = energy % 2, energy // 2
    start = pl.multiple_of(x * half + z * share, share)
    copy = pltpu.make_async_copy(bare_ref.at[pl.ds(start, share), :], bare_rows, arrived)
    copy.start()
    padded[:SHIFTS] = jnp.zeros((SHIFTS, share, width), jnp.float32)

    def place(at, rows, weight):
        rows = rows.astype(jnp.float32)
        padded[SHIFTS + at] = rows
        weighted[at] = rows * weight

    def total(tail, row):
        return tail[row:row + 1] + tail[row + 1:row + 2] + tail[row + 2:row + 3]

    place(energy, block_ref[pl.ds(start, share), :], weight_ref[0])
    place(
        z * 2 + 1 - x,
        got_ref[pl.ds(pl.multiple_of(z * share, share), share), :],
        total(got_ref[half:, :].astype(jnp.float32), 3),
    )
    for k, ref in enumerate(received, 1):
        behind = (z + outer - k) % outer * 2
        tail = ref[2 * share:, :].astype(jnp.float32)
        place(behind + x, ref[:share, :], total(tail, 0))
        place(behind + 1 - x, ref[share:2 * share, :], total(tail, 3))
    totals = [jnp.zeros((share, width), jnp.float32) for _ in range(FREQS)]
    for e in range(energies):
        own = weighted[e]
        for f in range(FREQS):
            totals[f] += own * padded[SHIFTS + e - offsets_ref[f]]
    copy.wait()
    factor = -(width ** -0.5) * energies ** -0.5
    for f in range(FREQS):
        out_ref[f] = totals[f] * (factor * bare_rows[...])


def polar_share(green, weight, offsets, bare, scalars):
    energies = lax.axis_size("energy")
    rows, width = green.shape
    outer = energies // 2
    share = rows // energies
    half = rows // 2
    sent = pl.pallas_call(
        prepare_kernel,
        out_shape=jax.ShapeDtypeStruct((half + EXTRA, width), green.dtype),
        in_specs=[in_smem, in_hbm],
        out_specs=in_vmem,
        scratch_shapes=[pltpu.SemaphoreType.DMA],
        compiler_params=small,
        name="prepare",
    )(weight, held(green))
    got = lax.ppermute(sent, "energy", [(e, e ^ 1) for e in range(energies)])
    shares = pl.pallas_call(
        arrange_kernel,
        out_shape=(jax.ShapeDtypeStruct((2 * share + EXTRA, width), green.dtype),) * (outer - 1),
        in_specs=[in_smem, in_vmem, in_vmem],
        out_specs=(in_vmem,) * (outer - 1),
        compiler_params=small,
        name="arrange",
    )(weight, green, got)
    received = [None] * (outer - 1)
    for k in range(outer - 1, 0, -1):
        route = [(z * 2 + x, (z + k) % outer * 2 + x) for z in range(outer) for x in range(2)]
        received[k - 1] = lax.ppermute(shares[k - 1], "energy", route)

    def kernel(*refs):
        count = outer - 1
        polar_kernel(refs[:count], *refs[count:count + 2], *refs[count + 5:])

    return pl.pallas_call(
        kernel,
        out_shape=jax.ShapeDtypeStruct((FREQS, share, width), jnp.float32),
        in_specs=[in_vmem] * (outer - 1) + [in_smem] * 5 + [in_vmem, in_vmem, in_place],
        out_specs=in_vmem,
        scratch_shapes=[
            VMEM((SHIFTS + energies, share, width), jnp.float32),
            VMEM((energies, share, width), jnp.float32),
            VMEM((share, width), jnp.float32),
            pltpu.SemaphoreType.DMA,
        ],
        compiler_params=small,
        name="polar",
    )(*received, weight, offsets, *scalars, green, got, bare)


def polar_share_plain(green, weight, offsets, bare, scalars):
    energies = lax.axis_size("energy")
    rows, width = green.shape
    share = rows // energies
    weights = lax.all_gather(weight, "energy", axis=0, tiled=True)
    parts = green.reshape(energies, share, width)
    parts = jnp.stack([parts[share_of(k)] for k in range(energies)]) if in_squares() else parts
    got = lax.all_to_all(parts, "energy", 0, 0, tiled=True)
    wide = got.astype(jnp.float32)
    weighted = wide * weights[:, None, None]
    padded = jnp.concatenate([jnp.zeros((SHIFTS,) + wide.shape[1:], wide.dtype), wide], axis=0)
    own = lax.dynamic_slice_in_dim(bare, share_of(lax.axis_index("energy")) * share, share, 0)
    factor = -(width ** -0.5) * energies ** -0.5
    chunks = []
    for f in range(FREQS):
        low = lax.dynamic_slice_in_dim(padded, SHIFTS - offsets[f], energies, 0)
        chunks.append(factor * own * jnp.sum(weighted * low, axis=0))
    return jnp.stack(chunks)


def gather_energy(chunk):
    outer = lax.axis_size("energy") // 2
    here = lax.axis_index("energy") // 2
    wholes = [
        lax.dynamic_update_index_in_dim(jnp.zeros((outer,) + part.shape, part.dtype), part, here, 0)
        for part in chunk
    ]
    for k in range(outer - 1, 0, -1):
        route = [(z * 2 + x, (z + k) % outer * 2 + x) for z in range(outer) for x in range(2)]
        got = lax.ppermute(chunk, "energy", route)
        wholes = [
            lax.dynamic_update_index_in_dim(whole, part, (here - k) % outer, 0)
            for whole, part in zip(wholes, got)
        ]
    return wholes


def gather_square(parts):
    energies = lax.axis_size("energy")

    def along_x(part):
        return lax.ppermute(part, "energy", [(e, e ^ 1) for e in range(energies)])

    def along_rep(part):
        return lax.ppermute(part, "rep", [(0, 1), (1, 0)])

    beside = [along_x(part) for part in parts]
    above = [along_rep(part) for part in parts]
    apart = [along_rep(beside[0]), along_x(above[1])]
    return [*parts, *beside, *above, *apart]


def gathered(chunk):
    chunk = chunk.astype(coded)
    if in_squares():
        pieces = gather_square(gather_energy(chunk))
    else:
        pieces = [lax.all_gather(chunk, ("rep", "energy"), axis=1, tiled=True)]
    return [piece.astype(jnp.float32) for piece in pieces]


def parts_of(value):
    size = jnp.abs(value)
    exponent = jnp.where(size > 0.0, jnp.floor(jnp.log2(jnp.where(size > 0.0, size, 1.0))), 0.0)
    exponent = jnp.clip(exponent, -120.0, 120.0)
    mantissa = value * jnp.exp2(-exponent)
    first = mantissa.astype(jnp.bfloat16).astype(jnp.float32)
    second = (mantissa - first).astype(jnp.bfloat16).astype(jnp.float32)
    return exponent, first, second


def whole_of(exponent, first, second):
    return (first + second) * jnp.exp2(exponent)


def corner_start(place, block, rows):
    x, rep = lax.axis_index("energy") % 2, lax.axis_index("rep")
    at_x = 1 - x if place % 2 else x
    at_rep = 1 - rep if place >= 2 else rep
    return pl.multiple_of(at_rep * rows + at_x * block, block)


def early_kernel(pieces, bare_ref, once_ref, high, low):
    rows, width = bare_ref.shape
    if len(pieces) == 1:
        for f in range(FREQS):
            high[f], low[f] = halves(pieces[0][f])
    else:
        outer, share, _ = pieces[0].shape
        block = outer * share
        empty = jnp.zeros((block, width), jnp.bfloat16)
        for f in range(FREQS):
            for place in range(4):
                at = pl.ds(corner_start(place, block, rows), block)
                if place == 3:
                    high[f, at, :], low[f, at, :] = empty, empty
                else:
                    upper, lower = halves(pieces[place * FREQS + f][...].reshape(block, width))
                    high[f, at, :], low[f, at, :] = upper, lower
    bare = bare_ref[...]
    for f in range(FREQS):
        once_ref[f] = bare + product(bare, high[f], low[f])


def dyson_kernel(apart, early, offsets_ref, steps_ref, level_ref, bare_ref, hamiltonian_ref, two_ref,
                 four_ref, odd_ref, beside_refs, screened_ref, packed_ref, step_ref, own_ref,
                 high, low, made, hamiltonian_rows, made_sem, hamiltonian_sem):
    once_ref, high_ref, low_ref = early
    rows, width = bare_ref.shape
    entry_scale = width ** -0.5
    read = pltpu.make_async_copy(hamiltonian_ref, hamiltonian_rows, hamiltonian_sem)
    read.start()
    rep = lax.axis_index("rep")
    bare = bare_ref[...]
    once = [once_ref[f] for f in range(FREQS)]
    at = jnp.where(steps_ref[1] > steps_ref[0], 1, 0)
    high[...], low[...] = high_ref[at], low_ref[at]
    if apart:
        outer, share, _ = apart[0].shape
        block = outer * share
        start = corner_start(3, block, rows)
        beyond = bare_ref[:, pl.ds(start, block)]
        parts = [halves(ref[...].reshape(block, width)) for ref in apart]
        once = [once[f] + product(beyond, *parts[f]) for f in range(FREQS)]
        high[pl.ds(start, block), :] = jnp.where(at == 0, parts[0][0], parts[1][0])
        low[pl.ds(start, block), :] = jnp.where(at == 0, parts[0][1], parts[1][1])
    last = jnp.where(at == 0, once[0], once[1])
    upper, lower = high[...], low[...]
    twice = last + product(product(last, upper, lower), upper, lower)
    other = jnp.minimum(offsets_ref[0], offsets_ref[1])
    less = jnp.where(other == 2, two_ref[...], odd_ref[...])
    four = four_ref[...]
    energy_terms = jnp.zeros((rows, width), jnp.float32)
    for f in range(FREQS):
        count = steps_ref[f]
        value = jnp.where(count == 0, bare, jnp.where(count == 1, once[f], twice))
        value = value.astype(jnp.bfloat16)
        made[f] = value
        lowered = jnp.where(offsets_ref[f] == SHIFTS, four, less).astype(jnp.float32)
        energy_terms += lowered * value.astype(jnp.float32)
    write = pltpu.make_async_copy(made, screened_ref, made_sem)
    write.start()
    read.wait()
    beside = sum(ref[...].astype(jnp.float32) for ref in beside_refs)
    rest = hamiltonian_rows[...] - entry_scale * energy_terms - (0.5 * entry_scale) * beside
    col = lax.broadcasted_iota(jnp.int32, (rows, width), 1)
    row = lax.broadcasted_iota(jnp.int32, (rows, width), 0) + rep * rows
    on = col == row
    diagonal = level_ref[0] + jnp.sum(jnp.where(on, rest, 0.0), axis=1, keepdims=True)
    off = jnp.where(on, 0.0, rest)
    largest = jnp.max(jnp.abs(off), axis=1, keepdims=True)
    largest = jnp.where(largest > 0.0, largest, 1.0)
    unit = off * (1.0 / largest)
    inverse = 1.0 / diagonal
    factor = -largest * inverse
    step_ref[...] = unit * factor
    factor_row = jnp.sum(jnp.where(on, factor, 0.0), axis=0, keepdims=True)
    inverse_row = jnp.sum(jnp.where(on, inverse, 0.0), axis=0, keepdims=True)
    blank = jnp.zeros((1, width), jnp.float32)
    packed_ref[:rows, :] = unit
    packed_ref[rows:, :] = jnp.concatenate(
        [*parts_of(factor_row), *parts_of(inverse_row), blank, blank], axis=0
    )
    own_ref[...] = jnp.concatenate([factor_row, inverse_row] + [blank] * 6, axis=0)
    write.wait()


def dyson_rows(pieces, offsets, steps, level, bare, hamiltonian, two, four, odd, beside):
    rows, width = bare.shape
    sides = len(beside)
    known, apart = (pieces, []) if len(pieces) == 1 else (pieces[:-FREQS], pieces[-FREQS:])
    count = len(known)

    def first_kernel(*refs):
        early_kernel(refs[:count], *refs[count:])

    early = pl.pallas_call(
        first_kernel,
        out_shape=(jax.ShapeDtypeStruct((FREQS, rows, width), jnp.float32),)
        + (jax.ShapeDtypeStruct((FREQS, width, width), jnp.bfloat16),) * 2,
        in_specs=[in_vmem] * (count + 1),
        out_specs=(in_vmem,) * 3,
        compiler_params=large,
        name="early",
    )(*known, bare)

    def kernel(*refs):
        far, rest = refs[:len(apart)], refs[len(apart):]
        done, rest = rest[:3], rest[3:]
        named, rest = rest[:8], rest[8:]
        dyson_kernel(far, done, *named, rest[:sides], *rest[sides:])

    return pl.pallas_call(
        kernel,
        out_shape=(
            jax.ShapeDtypeStruct((FREQS, rows, width), jnp.bfloat16),
            jax.ShapeDtypeStruct((rows + EXTRA, width), jnp.float32),
            jax.ShapeDtypeStruct((rows, width), jnp.float32),
            jax.ShapeDtypeStruct((EXTRA, width), jnp.float32),
        ),
        in_specs=[in_vmem] * (len(apart) + 3) + [in_smem] * 3 + [in_vmem, in_hbm]
        + [in_vmem] * (3 + sides),
        out_specs=(in_hbm,) + (in_vmem,) * 3,
        scratch_shapes=[VMEM((width, width), jnp.bfloat16)] * 2
        + [VMEM((FREQS, rows, width), jnp.bfloat16), VMEM((rows, width), jnp.float32)]
        + [pltpu.SemaphoreType.DMA] * 2,
        compiler_params=large,
        name="dyson",
    )(*apart, *early, offsets, steps, level, bare, held(hamiltonian), two, four, odd, *beside)


def columns(value, first):
    rows = value.shape[0]
    left, right = value[:, :rows], value[:, rows:]
    return jnp.where(first, left, right), jnp.where(first, right, left)


def begin_kernel(step_ref, packed_ref, own_ref, square_ref, high_ref, low_ref):
    rows, _ = step_ref.shape
    high, low = halves(packed_ref[:rows, :])
    high_ref[...], low_ref[...] = high, low
    near, _ = columns(step_ref[...] * own_ref[0:1], lax.axis_index("rep") == 0)
    square_ref[...] = product(near, high, low)


def finish_kernel(steps_ref, step_ref, square_ref, high_ref, low_ref, theirs_ref, own_ref, out_ref,
                  made, sems):
    rows, _ = step_ref.shape
    rep = lax.axis_index("rep")
    first = rep == 0
    tail = theirs_ref[rows:, :]
    factors = own_ref[0:1] + whole_of(tail[0:1], tail[1:2], tail[2:3])
    inverses = own_ref[1:2] + whole_of(tail[3:4], tail[4:5], tail[5:6])
    theirs = halves(theirs_ref[:rows, :])
    step = step_ref[...]
    _, far = columns(step * factors, first)
    square = square_ref[...] + product(far, *theirs)
    near, far = columns(square * factors, first)
    writes = []
    for half in range(2):
        at = slice(half * rows, (half + 1) * rows)
        cube = product(near, high_ref[:, at], low_ref[:, at]) + product(
            far, theirs[0][:, at], theirs[1][:, at]
        )
        col = lax.broadcasted_iota(jnp.int32, (rows, rows), 1) + half * rows
        row = lax.broadcasted_iota(jnp.int32, (rows, rows), 0) + rep * rows
        total = jnp.where(col == row, 1.0, step[:, at])
        total = total + jnp.where(steps_ref[0] >= 2, square[:, at] + cube, 0.0)
        made[:, at] = total * inverses[:, at]
        writes.append(pltpu.make_async_copy(made.at[:, at], out_ref.at[:, at], sems.at[half]))
        writes[-1].start()
    for write in writes:
        write.wait()


def body(
    green_blocks, occupation, offsets, coulomb, hamiltonian, onsite_level, green_steps, screen_steps
):
    green = green_blocks[0, 0]
    bare = coulomb[0]
    rows, width = green.shape
    share = rows // lax.axis_size("energy")
    make = polar_share if in_squares() and share % 16 == 0 else polar_share_plain
    scalars = (screen_steps, green_steps, onsite_level)
    pieces = gathered(make(green, occupation, offsets, bare, scalars))

    two = shifted(green, "energy", 2)
    four = shifted(two, "energy", 2)
    odd = shifted(chosen(offsets, two, green), "energy", 1)

    slabs = lax.axis_size("slab")
    if slabs == 2:
        beside = [lax.ppermute(green, "slab", [(0, 1), (1, 0)])]
    else:
        up = [(i, i + 1) for i in range(slabs - 1)]
        down = [(j, i) for i, j in up]
        beside = [lax.ppermute(green, "slab", up), lax.ppermute(green, "slab", down)]

    screened, packed, step, own = dyson_rows(
        pieces, offsets, screen_steps, onsite_level, bare, hamiltonian[0], two, four, odd, beside
    )
    theirs = lax.ppermute(packed.astype(coded), "rep", [(0, 1), (1, 0)]).astype(jnp.float32)
    wide = jax.ShapeDtypeStruct((rows, width), jnp.float32)
    thin = jax.ShapeDtypeStruct((rows, width), jnp.bfloat16)
    square, high, low = pl.pallas_call(
        begin_kernel,
        out_shape=(wide, thin, thin),
        in_specs=[in_vmem] * 3,
        out_specs=(in_vmem,) * 3,
        compiler_params=small,
        name="begin",
    )(step, packed, own)
    green_next = pl.pallas_call(
        finish_kernel,
        out_shape=wide,
        in_specs=[in_smem] + [in_vmem] * 6,
        out_specs=in_hbm,
        scratch_shapes=[VMEM((rows, width), jnp.float32), pltpu.SemaphoreType.DMA((2,))],
        compiler_params=large,
        name="finish",
    )(green_steps, step, square, high, low, theirs, own)
    return green_next[None, None], screened[:, None]


def chosen_kernel(offsets_ref, two_ref, green_ref, out_ref):
    three = jnp.minimum(offsets_ref[0], offsets_ref[1]) == 3

    @pl.when(three)
    def _():
        out_ref[...] = two_ref[...]

    @pl.when(jnp.logical_not(three))
    def _():
        out_ref[...] = green_ref[...]


def chosen(offsets, two, green):
    return pl.pallas_call(
        chosen_kernel,
        out_shape=jax.ShapeDtypeStruct(green.shape, green.dtype),
        in_specs=[in_smem, in_vmem, in_vmem],
        out_specs=in_vmem,
        compiler_params=small,
        name="chosen",
    )(offsets, two, green)


def solution(mesh):
    return jax.shard_map(
        body,
        mesh=mesh,
        in_specs=(
            P("energy", "slab", "rep", None),
            P("energy"),
            P(),
            P("slab", "rep", None),
            P("slab", "rep", None),
            P("energy"),
            P("energy"),
            P(),
        ),
        out_specs=(P("energy", "slab", "rep", None), P(None, "slab", "rep", None)),
        check_vma=False,
    )
```

```python
import jax
import jax.numpy as jnp
from jax import lax
from jax.experimental import pallas as pl
from jax.experimental.pallas import tpu as pltpu
from jax.sharding import PartitionSpec as P


SHIFTS = 4
FREQS = 2
EXTRA = 8

coded = jnp.float16
VMEM = pltpu.VMEM
in_vmem = pl.BlockSpec(memory_space=pltpu.VMEM)
in_smem = pl.BlockSpec(memory_space=pltpu.SMEM)
in_place = pl.BlockSpec(memory_space=pl.ANY)
in_hbm = pl.BlockSpec(memory_space=pltpu.HBM)
small = pltpu.CompilerParams(vmem_limit_bytes=6 << 20)
large = pltpu.CompilerParams(vmem_limit_bytes=16 << 20)


def held(value):
    return pltpu.with_memory_space_constraint(value, pltpu.HBM)


def halves(value):
    high = value.astype(jnp.bfloat16)
    return high, (value - high.astype(jnp.float32)).astype(jnp.bfloat16)


def dot(first, second):
    return jnp.dot(first, second, preferred_element_type=jnp.float32)


def product(first, high, low):
    top, rest = halves(first)
    return dot(top, high) + dot(top, low) + dot(rest, high)


def shifted(block, axis, distance):
    count = lax.axis_size(axis)
    route = [(i, i + distance) for i in range(count - distance)]
    return lax.ppermute(block, axis, route)


def in_squares():
    energies = lax.axis_size("energy")
    return energies % 2 == 0 and energies <= 16 and lax.axis_size("rep") == 2


def share_of(place):
    outer = lax.axis_size("energy") // 2
    return place % 2 * outer + place // 2 if in_squares() else place


def weight_rows(weight, first_row, width):
    weight = jnp.full((EXTRA, width), weight, jnp.float32)
    first = weight.astype(jnp.bfloat16).astype(jnp.float32)
    second = (weight - first).astype(jnp.bfloat16).astype(jnp.float32)
    third = weight - first - second
    row = lax.broadcasted_iota(jnp.int32, (EXTRA, width), 0) - first_row
    later = jnp.where(row == 1, second, jnp.where(row == 2, third, 0.0))
    return jnp.where(row == 0, first, later)


def prepare_kernel(weight_ref, block_ref, out_ref, arrived):
    half, width = out_ref.shape[0] - EXTRA, out_ref.shape[1]
    x = lax.axis_index("energy") % 2
    start = pl.multiple_of((1 - x) * half, half)
    copy = pltpu.make_async_copy(
        block_ref.at[pl.ds(start, half), :], out_ref.at[pl.ds(0, half), :], arrived
    )
    copy.start()
    out_ref[half:, :] = weight_rows(weight_ref[0], 3, width).astype(out_ref.dtype)
    copy.wait()


def arrange_kernel(weight_ref, screen_ref, green_steps_ref, level_ref, block_ref, got_ref, *out_refs):
    outer = len(out_refs) + 1
    half, width = got_ref.shape[0] - EXTRA, got_ref.shape[1]
    share = half // outer
    x, z = lax.axis_index("energy") % 2, lax.axis_index("energy") // 2
    tail = weight_rows(weight_ref[0], 0, width) + got_ref[half:, :].astype(jnp.float32)
    tail = tail.astype(got_ref.dtype)
    for k, out_ref in enumerate(out_refs, 1):
        at = (z + k) % outer * share
        mine = pl.ds(pl.multiple_of(x * half + at, share), share)
        out_ref[:share, :] = block_ref[mine, :]
        out_ref[share:2 * share, :] = got_ref[pl.ds(pl.multiple_of(at, share), share), :]
        out_ref[2 * share:, :] = tail


def polar_kernel(received, weight_ref, offsets_ref, block_ref, got_ref, bare_ref, out_ref,
                 padded, weighted, bare_rows, arrived):
    _, share, width = out_ref.shape
    energies = weighted.shape[0]
    outer = energies // 2
    half = outer * share
    energy = lax.axis_index("energy")
    x, z = energy % 2, energy // 2
    start = pl.multiple_of(x * half + z * share, share)
    copy = pltpu.make_async_copy(bare_ref.at[pl.ds(start, share), :], bare_rows, arrived)
    copy.start()
    padded[:SHIFTS] = jnp.zeros((SHIFTS, share, width), jnp.float32)

    def place(at, rows, weight):
        rows = rows.astype(jnp.float32)
        padded[SHIFTS + at] = rows
        weighted[at] = rows * weight

    def total(tail, row):
        return tail[row:row + 1] + tail[row + 1:row + 2] + tail[row + 2:row + 3]

    place(energy, block_ref[pl.ds(start, share), :], weight_ref[0])
    place(
        z * 2 + 1 - x,
        got_ref[pl.ds(pl.multiple_of(z * share, share), share), :],
        total(got_ref[half:, :].astype(jnp.float32), 3),
    )
    for k, ref in enumerate(received, 1):
        behind = (z + outer - k) % outer * 2
        tail = ref[2 * share:, :].astype(jnp.float32)
        place(behind + x, ref[:share, :], total(tail, 0))
        place(behind + 1 - x, ref[share:2 * share, :], total(tail, 3))
    totals = [jnp.zeros((share, width), jnp.float32) for _ in range(FREQS)]
    for e in range(energies):
        own = weighted[e]
        for f in range(FREQS):
            totals[f] += own * padded[SHIFTS + e - offsets_ref[f]]
    copy.wait()
    factor = -(width ** -0.5) * energies ** -0.5
    for f in range(FREQS):
        out_ref[f] = totals[f] * (factor * bare_rows[...])


def polar_share(green, weight, offsets, bare, scalars):
    energies = lax.axis_size("energy")
    rows, width = green.shape
    outer = energies // 2
    share = rows // energies
    half = rows // 2
    sent = pl.pallas_call(
        prepare_kernel,
        out_shape=jax.ShapeDtypeStruct((half + EXTRA, width), green.dtype),
        in_specs=[in_smem, in_hbm],
        out_specs=in_vmem,
        scratch_shapes=[pltpu.SemaphoreType.DMA],
        compiler_params=small,
        name="prepare",
    )(weight, held(green))
    got = lax.ppermute(sent, "energy", [(e, e ^ 1) for e in range(energies)])
    shares = pl.pallas_call(
        arrange_kernel,
        out_shape=(jax.ShapeDtypeStruct((2 * share + EXTRA, width), green.dtype),) * (outer - 1),
        in_specs=[in_smem] * 4 + [in_vmem] * 2,
        out_specs=(in_vmem,) * (outer - 1),
        compiler_params=small,
        name="arrange",
    )(weight, *scalars, green, got)
    received = [None] * (outer - 1)
    for k in range(outer - 1, 0, -1):
        route = [(z * 2 + x, (z + k) % outer * 2 + x) for z in range(outer) for x in range(2)]
        received[k - 1] = lax.ppermute(shares[k - 1], "energy", route)

    def kernel(*refs):
        count = outer - 1
        polar_kernel(refs[:count], *refs[count:])

    return pl.pallas_call(
        kernel,
        out_shape=jax.ShapeDtypeStruct((FREQS, share, width), jnp.float32),
        in_specs=[in_vmem] * (outer - 1) + [in_smem] * 2 + [in_vmem, in_vmem, in_place],
        out_specs=in_vmem,
        scratch_shapes=[
            VMEM((SHIFTS + energies, share, width), jnp.float32),
            VMEM((energies, share, width), jnp.float32),
            VMEM((share, width), jnp.float32),
            pltpu.SemaphoreType.DMA,
        ],
        compiler_params=small,
        name="polar",
    )(*received, weight, offsets, green, got, bare)


def polar_share_plain(green, weight, offsets, bare, scalars):
    energies = lax.axis_size("energy")
    rows, width = green.shape
    share = rows // energies
    weights = lax.all_gather(weight, "energy", axis=0, tiled=True)
    parts = green.reshape(energies, share, width)
    parts = jnp.stack([parts[share_of(k)] for k in range(energies)]) if in_squares() else parts
    got = lax.all_to_all(parts, "energy", 0, 0, tiled=True)
    wide = got.astype(jnp.float32)
    weighted = wide * weights[:, None, None]
    padded = jnp.concatenate([jnp.zeros((SHIFTS,) + wide.shape[1:], wide.dtype), wide], axis=0)
    own = lax.dynamic_slice_in_dim(bare, share_of(lax.axis_index("energy")) * share, share, 0)
    factor = -(width ** -0.5) * energies ** -0.5
    chunks = []
    for f in range(FREQS):
        low = lax.dynamic_slice_in_dim(padded, SHIFTS - offsets[f], energies, 0)
        chunks.append(factor * own * jnp.sum(weighted * low, axis=0))
    return jnp.stack(chunks)


def gather_energy(chunk):
    outer = lax.axis_size("energy") // 2
    here = lax.axis_index("energy") // 2
    wholes = [
        lax.dynamic_update_index_in_dim(jnp.zeros((outer,) + part.shape, part.dtype), part, here, 0)
        for part in chunk
    ]
    for k in range(outer - 1, 0, -1):
        route = [(z * 2 + x, (z + k) % outer * 2 + x) for z in range(outer) for x in range(2)]
        got = lax.ppermute(chunk, "energy", route)
        wholes = [
            lax.dynamic_update_index_in_dim(whole, part, (here - k) % outer, 0)
            for whole, part in zip(wholes, got)
        ]
    return wholes


def gather_square(parts):
    energies = lax.axis_size("energy")

    def along_x(part):
        return lax.ppermute(part, "energy", [(e, e ^ 1) for e in range(energies)])

    def along_rep(part):
        return lax.ppermute(part, "rep", [(0, 1), (1, 0)])

    beside = [along_x(part) for part in parts]
    above = [along_rep(part) for part in parts]
    apart = [along_rep(beside[0]), along_x(above[1])]
    return [*parts, *beside, *above, *apart]


def gathered(chunk):
    chunk = chunk.astype(coded)
    if in_squares():
        pieces = gather_square(gather_energy(chunk))
    else:
        pieces = [lax.all_gather(chunk, ("rep", "energy"), axis=1, tiled=True)]
    return [piece.astype(jnp.float32) for piece in pieces]


def parts_of(value):
    size = jnp.abs(value)
    exponent = jnp.where(size > 0.0, jnp.floor(jnp.log2(jnp.where(size > 0.0, size, 1.0))), 0.0)
    exponent = jnp.clip(exponent, -120.0, 120.0)
    mantissa = value * jnp.exp2(-exponent)
    first = mantissa.astype(jnp.bfloat16).astype(jnp.float32)
    second = (mantissa - first).astype(jnp.bfloat16).astype(jnp.float32)
    return exponent, first, second


def whole_of(exponent, first, second):
    return (first + second) * jnp.exp2(exponent)


def corner_start(place, block, rows):
    x, rep = lax.axis_index("energy") % 2, lax.axis_index("rep")
    at_x = 1 - x if place % 2 else x
    at_rep = 1 - rep if place >= 2 else rep
    return pl.multiple_of(at_rep * rows + at_x * block, block)


def early_kernel(pieces, bare_ref, once_ref, high, low):
    rows, width = bare_ref.shape
    if len(pieces) == 1:
        for f in range(FREQS):
            high[f], low[f] = halves(pieces[0][f])
    else:
        outer, share, _ = pieces[0].shape
        block = outer * share
        empty = jnp.zeros((block, width), jnp.bfloat16)
        for f in range(FREQS):
            for place in range(4):
                at = pl.ds(corner_start(place, block, rows), block)
                if place == 3:
                    high[f, at, :], low[f, at, :] = empty, empty
                else:
                    upper, lower = halves(pieces[place * FREQS + f][...].reshape(block, width))
                    high[f, at, :], low[f, at, :] = upper, lower
    bare = bare_ref[...]
    for f in range(FREQS):
        once_ref[f] = bare + product(bare, high[f], low[f])


def dyson_kernel(apart, early, offsets_ref, steps_ref, level_ref, bare_ref, hamiltonian_ref, two_ref,
                 four_ref, odd_ref, beside_refs, screened_ref, packed_ref, step_ref, own_ref,
                 high, low, made, hamiltonian_rows, made_sem, hamiltonian_sem):
    once_ref, high_ref, low_ref = early
    rows, width = bare_ref.shape
    entry_scale = width ** -0.5
    read = pltpu.make_async_copy(hamiltonian_ref, hamiltonian_rows, hamiltonian_sem)
    read.start()
    rep = lax.axis_index("rep")
    bare = bare_ref[...]
    once = [once_ref[f] for f in range(FREQS)]
    at = jnp.where(steps_ref[1] > steps_ref[0], 1, 0)
    high[...], low[...] = high_ref[at], low_ref[at]
    if apart:
        outer, share, _ = apart[0].shape
        block = outer * share
        start = corner_start(3, block, rows)
        beyond = bare_ref[:, pl.ds(start, block)]
        parts = [halves(ref[...].reshape(block, width)) for ref in apart]
        once = [once[f] + product(beyond, *parts[f]) for f in range(FREQS)]
        high[pl.ds(start, block), :] = jnp.where(at == 0, parts[0][0], parts[1][0])
        low[pl.ds(start, block), :] = jnp.where(at == 0, parts[0][1], parts[1][1])
    last = jnp.where(at == 0, once[0], once[1])
    upper, lower = high[...], low[...]
    twice = last + product(product(last, upper, lower), upper, lower)
    other = jnp.minimum(offsets_ref[0], offsets_ref[1])
    less = jnp.where(other == 2, two_ref[...], odd_ref[...])
    four = four_ref[...]
    energy_terms = jnp.zeros((rows, width), jnp.float32)
    for f in range(FREQS):
        count = steps_ref[f]
        value = jnp.where(count == 0, bare, jnp.where(count == 1, once[f], twice))
        value = value.astype(jnp.bfloat16)
        made[f] = value
        lowered = jnp.where(offsets_ref[f] == SHIFTS, four, less).astype(jnp.float32)
        energy_terms += lowered * value.astype(jnp.float32)
    write = pltpu.make_async_copy(made, screened_ref, made_sem)
    write.start()
    read.wait()
    beside = sum(ref[...].astype(jnp.float32) for ref in beside_refs)
    rest = hamiltonian_rows[...] - entry_scale * energy_terms - (0.5 * entry_scale) * beside
    col = lax.broadcasted_iota(jnp.int32, (rows, width), 1)
    row = lax.broadcasted_iota(jnp.int32, (rows, width), 0) + rep * rows
    on = col == row
    diagonal = level_ref[0] + jnp.sum(jnp.where(on, rest, 0.0), axis=1, keepdims=True)
    off = jnp.where(on, 0.0, rest)
    largest = jnp.max(jnp.abs(off), axis=1, keepdims=True)
    largest = jnp.where(largest > 0.0, largest, 1.0)
    unit = off * (1.0 / largest)
    inverse = 1.0 / diagonal
    factor = -largest * inverse
    step_ref[...] = unit * factor
    factor_row = jnp.sum(jnp.where(on, factor, 0.0), axis=0, keepdims=True)
    inverse_row = jnp.sum(jnp.where(on, inverse, 0.0), axis=0, keepdims=True)
    blank = jnp.zeros((1, width), jnp.float32)
    packed_ref[:rows, :] = unit
    packed_ref[rows:, :] = jnp.concatenate(
        [*parts_of(factor_row), *parts_of(inverse_row), blank, blank], axis=0
    )
    own_ref[...] = jnp.concatenate([factor_row, inverse_row] + [blank] * 6, axis=0)
    write.wait()


def dyson_rows(pieces, offsets, steps, level, bare, hamiltonian, two, four, odd, beside):
    rows, width = bare.shape
    sides = len(beside)
    known, apart = (pieces, []) if len(pieces) == 1 else (pieces[:-FREQS], pieces[-FREQS:])
    count = len(known)

    def first_kernel(*refs):
        early_kernel(refs[:count], *refs[count:])

    early = pl.pallas_call(
        first_kernel,
        out_shape=(jax.ShapeDtypeStruct((FREQS, rows, width), jnp.float32),)
        + (jax.ShapeDtypeStruct((FREQS, width, width), jnp.bfloat16),) * 2,
        in_specs=[in_vmem] * (count + 1),
        out_specs=(in_vmem,) * 3,
        compiler_params=large,
        name="early",
    )(*known, bare)

    def kernel(*refs):
        far, rest = refs[:len(apart)], refs[len(apart):]
        done, rest = rest[:3], rest[3:]
        named, rest = rest[:8], rest[8:]
        dyson_kernel(far, done, *named, rest[:sides], *rest[sides:])

    return pl.pallas_call(
        kernel,
        out_shape=(
            jax.ShapeDtypeStruct((FREQS, rows, width), jnp.bfloat16),
            jax.ShapeDtypeStruct((rows + EXTRA, width), jnp.float32),
            jax.ShapeDtypeStruct((rows, width), jnp.float32),
            jax.ShapeDtypeStruct((EXTRA, width), jnp.float32),
        ),
        in_specs=[in_vmem] * (len(apart) + 3) + [in_smem] * 3 + [in_vmem, in_hbm]
        + [in_vmem] * (3 + sides),
        out_specs=(in_hbm,) + (in_vmem,) * 3,
        scratch_shapes=[VMEM((width, width), jnp.bfloat16)] * 2
        + [VMEM((FREQS, rows, width), jnp.bfloat16), VMEM((rows, width), jnp.float32)]
        + [pltpu.SemaphoreType.DMA] * 2,
        compiler_params=large,
        name="dyson",
    )(*apart, *early, offsets, steps, level, bare, held(hamiltonian), two, four, odd, *beside)


def columns(value, first):
    rows = value.shape[0]
    left, right = value[:, :rows], value[:, rows:]
    return jnp.where(first, left, right), jnp.where(first, right, left)


def begin_kernel(step_ref, packed_ref, own_ref, square_ref, high_ref, low_ref):
    rows, _ = step_ref.shape
    high, low = halves(packed_ref[:rows, :])
    high_ref[...], low_ref[...] = high, low
    near, _ = columns(step_ref[...] * own_ref[0:1], lax.axis_index("rep") == 0)
    square_ref[...] = product(near, high, low)


def finish_kernel(steps_ref, step_ref, square_ref, high_ref, low_ref, theirs_ref, own_ref, out_ref,
                  made, sems):
    rows, _ = step_ref.shape
    rep = lax.axis_index("rep")
    first = rep == 0
    tail = theirs_ref[rows:, :]
    factors = own_ref[0:1] + whole_of(tail[0:1], tail[1:2], tail[2:3])
    inverses = own_ref[1:2] + whole_of(tail[3:4], tail[4:5], tail[5:6])
    theirs = halves(theirs_ref[:rows, :])
    step = step_ref[...]
    _, far = columns(step * factors, first)
    square = square_ref[...] + product(far, *theirs)
    near, far = columns(square * factors, first)
    writes = []
    for half in range(2):
        at = slice(half * rows, (half + 1) * rows)
        cube = product(near, high_ref[:, at], low_ref[:, at]) + product(
            far, theirs[0][:, at], theirs[1][:, at]
        )
        col = lax.broadcasted_iota(jnp.int32, (rows, rows), 1) + half * rows
        row = lax.broadcasted_iota(jnp.int32, (rows, rows), 0) + rep * rows
        total = jnp.where(col == row, 1.0, step[:, at])
        total = total + jnp.where(steps_ref[0] >= 2, square[:, at] + cube, 0.0)
        made[:, at] = total * inverses[:, at]
        writes.append(pltpu.make_async_copy(made.at[:, at], out_ref.at[:, at], sems.at[half]))
        writes[-1].start()
    for write in writes:
        write.wait()


def body(
    green_blocks, occupation, offsets, coulomb, hamiltonian, onsite_level, green_steps, screen_steps
):
    green = green_blocks[0, 0]
    bare = coulomb[0]
    rows, width = green.shape
    share = rows // lax.axis_size("energy")
    make = polar_share if in_squares() and share % 16 == 0 else polar_share_plain
    scalars = (screen_steps, green_steps, onsite_level)
    pieces = gathered(make(green, occupation, offsets, bare, scalars))

    two = shifted(green, "energy", 2)
    four = shifted(two, "energy", 2)
    odd = shifted(chosen(offsets, two, green), "energy", 1)

    slabs = lax.axis_size("slab")
    if slabs == 2:
        beside = [lax.ppermute(green, "slab", [(0, 1), (1, 0)])]
    else:
        up = [(i, i + 1) for i in range(slabs - 1)]
        down = [(j, i) for i, j in up]
        beside = [lax.ppermute(green, "slab", up), lax.ppermute(green, "slab", down)]

    screened, packed, step, own = dyson_rows(
        pieces, offsets, screen_steps, onsite_level, bare, hamiltonian[0], two, four, odd, beside
    )
    theirs = lax.ppermute(packed.astype(coded), "rep", [(0, 1), (1, 0)]).astype(jnp.float32)
    wide = jax.ShapeDtypeStruct((rows, width), jnp.float32)
    thin = jax.ShapeDtypeStruct((rows, width), jnp.bfloat16)
    square, high, low = pl.pallas_call(
        begin_kernel,
        out_shape=(wide, thin, thin),
        in_specs=[in_vmem] * 3,
        out_specs=(in_vmem,) * 3,
        compiler_params=small,
        name="begin",
    )(step, packed, own)
    green_next = pl.pallas_call(
        finish_kernel,
        out_shape=wide,
        in_specs=[in_smem] + [in_vmem] * 6,
        out_specs=in_hbm,
        scratch_shapes=[VMEM((rows, width), jnp.float32), pltpu.SemaphoreType.DMA((2,))],
        compiler_params=large,
        name="finish",
    )(green_steps, step, square, high, low, theirs, own)
    return green_next[None, None], screened[:, None]


def chosen_kernel(offsets_ref, two_ref, green_ref, out_ref):
    three = jnp.minimum(offsets_ref[0], offsets_ref[1]) == 3

    @pl.when(three)
    def _():
        out_ref[...] = two_ref[...]

    @pl.when(jnp.logical_not(three))
    def _():
        out_ref[...] = green_ref[...]


def chosen(offsets, two, green):
    return pl.pallas_call(
        chosen_kernel,
        out_shape=jax.ShapeDtypeStruct(green.shape, green.dtype),
        in_specs=[in_smem, in_vmem, in_vmem],
        out_specs=in_vmem,
        compiler_params=small,
        name="chosen",
    )(offsets, two, green)


def solution(mesh):
    return jax.shard_map(
        body,
        mesh=mesh,
        in_specs=(
            P("energy", "slab", "rep", None),
            P("energy"),
            P(),
            P("slab", "rep", None),
            P("slab", "rep", None),
            P("energy"),
            P("energy"),
            P(),
        ),
        out_specs=(P("energy", "slab", "rep", None), P(None, "slab", "rep", None)),
        check_vma=False,
    )
```

```python
import jax
import jax.numpy as jnp
from jax import lax
from jax.experimental import pallas as pl
from jax.experimental.pallas import tpu as pltpu
from jax.sharding import PartitionSpec as P


SHIFTS = 4
FREQS = 2
EXTRA = 8

coded = jnp.float16
VMEM = pltpu.VMEM
in_vmem = pl.BlockSpec(memory_space=pltpu.VMEM)
in_smem = pl.BlockSpec(memory_space=pltpu.SMEM)
in_place = pl.BlockSpec(memory_space=pl.ANY)
in_hbm = pl.BlockSpec(memory_space=pltpu.HBM)
small = pltpu.CompilerParams(vmem_limit_bytes=6 << 20)
large = pltpu.CompilerParams(vmem_limit_bytes=16 << 20)


def held(value):
    return pltpu.with_memory_space_constraint(value, pltpu.HBM)


def halves(value):
    high = value.astype(jnp.bfloat16)
    return high, (value - high.astype(jnp.float32)).astype(jnp.bfloat16)


def dot(first, second):
    return jnp.dot(first, second, preferred_element_type=jnp.float32)


def product(first, high, low):
    top, rest = halves(first)
    return dot(top, high) + dot(top, low) + dot(rest, high)


def shifted(block, axis, distance):
    count = lax.axis_size(axis)
    route = [(i, i + distance) for i in range(count - distance)]
    return lax.ppermute(block, axis, route)


def in_squares():
    energies = lax.axis_size("energy")
    return energies % 2 == 0 and energies <= 16 and lax.axis_size("rep") == 2


def share_of(place):
    outer = lax.axis_size("energy") // 2
    return place % 2 * outer + place // 2 if in_squares() else place


def weight_rows(weight, first_row, width):
    weight = jnp.full((EXTRA, width), weight, jnp.float32)
    first = weight.astype(jnp.bfloat16).astype(jnp.float32)
    second = (weight - first).astype(jnp.bfloat16).astype(jnp.float32)
    third = weight - first - second
    row = lax.broadcasted_iota(jnp.int32, (EXTRA, width), 0) - first_row
    later = jnp.where(row == 1, second, jnp.where(row == 2, third, 0.0))
    return jnp.where(row == 0, first, later)


def prepare_kernel(weight_ref, block_ref, out_ref, arrived):
    half, width = out_ref.shape[0] - EXTRA, out_ref.shape[1]
    x = lax.axis_index("energy") % 2
    start = pl.multiple_of((1 - x) * half, half)
    copy = pltpu.make_async_copy(
        block_ref.at[pl.ds(start, half), :], out_ref.at[pl.ds(0, half), :], arrived
    )
    copy.start()
    out_ref[half:, :] = weight_rows(weight_ref[0], 3, width).astype(out_ref.dtype)
    copy.wait()


def arrange_kernel(weight_ref, block_ref, got_ref, *out_refs):
    outer = len(out_refs) + 1
    half, width = got_ref.shape[0] - EXTRA, got_ref.shape[1]
    share = half // outer
    x, z = lax.axis_index("energy") % 2, lax.axis_index("energy") // 2
    tail = weight_rows(weight_ref[0], 0, width) + got_ref[half:, :].astype(jnp.float32)
    tail = tail.astype(got_ref.dtype)
    for k, out_ref in enumerate(out_refs, 1):
        at = (z + k) % outer * share
        mine = pl.ds(pl.multiple_of(x * half + at, share), share)
        out_ref[:share, :] = block_ref[mine, :]
        out_ref[share:2 * share, :] = got_ref[pl.ds(pl.multiple_of(at, share), share), :]
        out_ref[2 * share:, :] = tail


def polar_kernel(received, weight_ref, offsets_ref, block_ref, got_ref, bare_ref, out_ref,
                 padded, weighted, bare_rows, arrived):
    _, share, width = out_ref.shape
    energies = weighted.shape[0]
    outer = energies // 2
    half = outer * share
    energy = lax.axis_index("energy")
    x, z = energy % 2, energy // 2
    start = pl.multiple_of(x * half + z * share, share)
    copy = pltpu.make_async_copy(bare_ref.at[pl.ds(start, share), :], bare_rows, arrived)
    copy.start()
    padded[:SHIFTS] = jnp.zeros((SHIFTS, share, width), jnp.float32)

    def place(at, rows, weight):
        rows = rows.astype(jnp.float32)
        padded[SHIFTS + at] = rows
        weighted[at] = rows * weight

    def total(tail, row):
        return tail[row:row + 1] + tail[row + 1:row + 2] + tail[row + 2:row + 3]

    place(energy, block_ref[pl.ds(start, share), :], weight_ref[0])
    place(
        z * 2 + 1 - x,
        got_ref[pl.ds(pl.multiple_of(z * share, share), share), :],
        total(got_ref[half:, :].astype(jnp.float32), 3),
    )
    for k, ref in enumerate(received, 1):
        behind = (z + outer - k) % outer * 2
        tail = ref[2 * share:, :].astype(jnp.float32)
        place(behind + x, ref[:share, :], total(tail, 0))
        place(behind + 1 - x, ref[share:2 * share, :], total(tail, 3))
    totals = [jnp.zeros((share, width), jnp.float32) for _ in range(FREQS)]
    for e in range(energies):
        own = weighted[e]
        for f in range(FREQS):
            totals[f] += own * padded[SHIFTS + e - offsets_ref[f]]
    copy.wait()
    factor = -(width ** -0.5) * energies ** -0.5
    for f in range(FREQS):
        out_ref[f] = totals[f] * (factor * bare_rows[...])


def polar_share(green, weight, offsets, bare, scalars):
    energies = lax.axis_size("energy")
    rows, width = green.shape
    outer = energies // 2
    share = rows // energies
    half = rows // 2
    sent = pl.pallas_call(
        prepare_kernel,
        out_shape=jax.ShapeDtypeStruct((half + EXTRA, width), green.dtype),
        in_specs=[in_smem, in_hbm],
        out_specs=in_vmem,
        scratch_shapes=[pltpu.SemaphoreType.DMA],
        compiler_params=small,
        name="prepare",
    )(weight, held(green))
    got = lax.ppermute(sent, "energy", [(e, e ^ 1) for e in range(energies)])
    shares = pl.pallas_call(
        arrange_kernel,
        out_shape=(jax.ShapeDtypeStruct((2 * share + EXTRA, width), green.dtype),) * (outer - 1),
        in_specs=[in_smem, in_vmem, in_vmem],
        out_specs=(in_vmem,) * (outer - 1),
        compiler_params=small,
        name="arrange",
    )(weight, green, got)
    received = [None] * (outer - 1)
    for k in range(outer - 1, 0, -1):
        route = [(z * 2 + x, (z + k) % outer * 2 + x) for z in range(outer) for x in range(2)]
        received[k - 1] = lax.ppermute(shares[k - 1], "energy", route)

    def kernel(*refs):
        count = outer - 1
        polar_kernel(refs[:count], *refs[count:count + 2], *refs[count + 5:])

    return pl.pallas_call(
        kernel,
        out_shape=jax.ShapeDtypeStruct((FREQS, share, width), jnp.float32),
        in_specs=[in_vmem] * (outer - 1) + [in_smem] * 5 + [in_vmem, in_vmem, in_place],
        out_specs=in_vmem,
        scratch_shapes=[
            VMEM((SHIFTS + energies, share, width), jnp.float32),
            VMEM((energies, share, width), jnp.float32),
            VMEM((share, width), jnp.float32),
            pltpu.SemaphoreType.DMA,
        ],
        compiler_params=small,
        name="polar",
    )(*received, weight, offsets, *scalars, green, got, bare)


def polar_share_plain(green, weight, offsets, bare, scalars):
    energies = lax.axis_size("energy")
    rows, width = green.shape
    share = rows // energies
    weights = lax.all_gather(weight, "energy", axis=0, tiled=True)
    parts = green.reshape(energies, share, width)
    parts = jnp.stack([parts[share_of(k)] for k in range(energies)]) if in_squares() else parts
    got = lax.all_to_all(parts, "energy", 0, 0, tiled=True)
    wide = got.astype(jnp.float32)
    weighted = wide * weights[:, None, None]
    padded = jnp.concatenate([jnp.zeros((SHIFTS,) + wide.shape[1:], wide.dtype), wide], axis=0)
    own = lax.dynamic_slice_in_dim(bare, share_of(lax.axis_index("energy")) * share, share, 0)
    factor = -(width ** -0.5) * energies ** -0.5
    chunks = []
    for f in range(FREQS):
        low = lax.dynamic_slice_in_dim(padded, SHIFTS - offsets[f], energies, 0)
        chunks.append(factor * own * jnp.sum(weighted * low, axis=0))
    return jnp.stack(chunks)


def gather_energy(chunk):
    outer = lax.axis_size("energy") // 2
    here = lax.axis_index("energy") // 2
    wholes = [
        lax.dynamic_update_index_in_dim(jnp.zeros((outer,) + part.shape, part.dtype), part, here, 0)
        for part in chunk
    ]
    for k in range(outer - 1, 0, -1):
        route = [(z * 2 + x, (z + k) % outer * 2 + x) for z in range(outer) for x in range(2)]
        got = lax.ppermute(chunk, "energy", route)
        wholes = [
            lax.dynamic_update_index_in_dim(whole, part, (here - k) % outer, 0)
            for whole, part in zip(wholes, got)
        ]
    return wholes


def gather_square(parts):
    energies = lax.axis_size("energy")

    def along_x(part):
        return lax.ppermute(part, "energy", [(e, e ^ 1) for e in range(energies)])

    def along_rep(part):
        return lax.ppermute(part, "rep", [(0, 1), (1, 0)])

    beside = [along_x(part) for part in parts]
    above = [along_rep(part) for part in parts]
    apart = [along_rep(part) for part in beside]
    return [*parts, *beside, *above, *apart]


def gathered(chunk):
    chunk = chunk.astype(coded)
    if in_squares():
        pieces = gather_square(gather_energy(chunk))
    else:
        pieces = [lax.all_gather(chunk, ("rep", "energy"), axis=1, tiled=True)]
    return [piece.astype(jnp.float32) for piece in pieces]


def parts_of(value):
    size = jnp.abs(value)
    exponent = jnp.where(size > 0.0, jnp.floor(jnp.log2(jnp.where(size > 0.0, size, 1.0))), 0.0)
    exponent = jnp.clip(exponent, -120.0, 120.0)
    mantissa = value * jnp.exp2(-exponent)
    first = mantissa.astype(jnp.bfloat16).astype(jnp.float32)
    second = (mantissa - first).astype(jnp.bfloat16).astype(jnp.float32)
    return exponent, first, second


def whole_of(exponent, first, second):
    return (first + second) * jnp.exp2(exponent)


def corner_start(place, block, rows):
    x, rep = lax.axis_index("energy") % 2, lax.axis_index("rep")
    at_x = 1 - x if place % 2 else x
    at_rep = 1 - rep if place >= 2 else rep
    return pl.multiple_of(at_rep * rows + at_x * block, block)


def early_kernel(pieces, bare_ref, once_ref, high, low):
    rows, width = bare_ref.shape
    if len(pieces) == 1:
        for f in range(FREQS):
            high[f], low[f] = halves(pieces[0][f])
    else:
        outer, share, _ = pieces[0].shape
        block = outer * share
        empty = jnp.zeros((block, width), jnp.bfloat16)
        for f in range(FREQS):
            for place in range(4):
                at = pl.ds(corner_start(place, block, rows), block)
                if place == 3:
                    high[f, at, :], low[f, at, :] = empty, empty
                else:
                    upper, lower = halves(pieces[place * FREQS + f][...].reshape(block, width))
                    high[f, at, :], low[f, at, :] = upper, lower
    bare = bare_ref[...]
    for f in range(FREQS):
        once_ref[f] = bare + product(bare, high[f], low[f])


def twice_kernel(apart, once_ref, high_ref, low_ref, steps_ref, bare_ref, made_ref, high, low):
    rows, width = bare_ref.shape
    bare = bare_ref[...]
    once = [once_ref[f] for f in range(FREQS)]
    at = jnp.where(steps_ref[1] > steps_ref[0], 1, 0)
    high[...], low[...] = high_ref[at], low_ref[at]
    if apart:
        outer, share, _ = apart[0].shape
        block = outer * share
        start = corner_start(3, block, rows)
        beyond = bare_ref[:, pl.ds(start, block)]
        parts = [halves(ref[...].reshape(block, width)) for ref in apart]
        once = [once[f] + product(beyond, *parts[f]) for f in range(FREQS)]
        high[pl.ds(start, block), :] = jnp.where(at == 0, parts[0][0], parts[1][0])
        low[pl.ds(start, block), :] = jnp.where(at == 0, parts[0][1], parts[1][1])
    last = jnp.where(at == 0, once[0], once[1])
    upper, lower = high[...], low[...]
    twice = last + product(product(last, upper, lower), upper, lower)
    for f in range(FREQS):
        count = steps_ref[f]
        value = jnp.where(count == 0, bare, jnp.where(count == 1, once[f], twice))
        made_ref[f] = value.astype(jnp.bfloat16)


def dyson_kernel(made_ref, offsets_ref, level_ref, hamiltonian_ref, two_ref, four_ref, odd_ref,
                 beside_refs, screened_ref, packed_ref, step_ref, own_ref,
                 hamiltonian_rows, made_sem, hamiltonian_sem):
    rows, width = step_ref.shape
    entry_scale = width ** -0.5
    read = pltpu.make_async_copy(hamiltonian_ref, hamiltonian_rows, hamiltonian_sem)
    read.start()
    write = pltpu.make_async_copy(made_ref, screened_ref, made_sem)
    write.start()
    rep = lax.axis_index("rep")
    other = jnp.minimum(offsets_ref[0], offsets_ref[1])
    less = jnp.where(other == 2, two_ref[...], odd_ref[...])
    four = four_ref[...]
    energy_terms = jnp.zeros((rows, width), jnp.float32)
    for f in range(FREQS):
        lowered = jnp.where(offsets_ref[f] == SHIFTS, four, less).astype(jnp.float32)
        energy_terms += lowered * made_ref[f].astype(jnp.float32)
    beside = sum(ref[...].astype(jnp.float32) for ref in beside_refs)
    read.wait()
    rest = hamiltonian_rows[...] - entry_scale * energy_terms - (0.5 * entry_scale) * beside
    col = lax.broadcasted_iota(jnp.int32, (rows, width), 1)
    row = lax.broadcasted_iota(jnp.int32, (rows, width), 0) + rep * rows
    on = col == row
    diagonal = level_ref[0] + jnp.sum(jnp.where(on, rest, 0.0), axis=1, keepdims=True)
    off = jnp.where(on, 0.0, rest)
    largest = jnp.max(jnp.abs(off), axis=1, keepdims=True)
    largest = jnp.where(largest > 0.0, largest, 1.0)
    unit = off * (1.0 / largest)
    inverse = 1.0 / diagonal
    factor = -largest * inverse
    step_ref[...] = unit * factor
    factor_row = jnp.sum(jnp.where(on, factor, 0.0), axis=0, keepdims=True)
    inverse_row = jnp.sum(jnp.where(on, inverse, 0.0), axis=0, keepdims=True)
    blank = jnp.zeros((1, width), jnp.float32)
    packed_ref[:rows, :] = unit
    packed_ref[rows:, :] = jnp.concatenate(
        [*parts_of(factor_row), *parts_of(inverse_row), blank, blank], axis=0
    )
    own_ref[...] = jnp.concatenate([factor_row, inverse_row] + [blank] * 6, axis=0)
    write.wait()


def dyson_rows(pieces, offsets, steps, level, bare, hamiltonian, two, four, odd, beside):
    rows, width = bare.shape
    sides = len(beside)
    known, apart = (pieces, []) if len(pieces) == 1 else (pieces[:-FREQS], pieces[-FREQS:])
    count = len(known)

    def first_kernel(*refs):
        early_kernel(refs[:count], *refs[count:])

    early = pl.pallas_call(
        first_kernel,
        out_shape=(jax.ShapeDtypeStruct((FREQS, rows, width), jnp.float32),)
        + (jax.ShapeDtypeStruct((FREQS, width, width), jnp.bfloat16),) * 2,
        in_specs=[in_vmem] * (count + 1),
        out_specs=(in_vmem,) * 3,
        compiler_params=large,
        name="early",
    )(*known, bare)

    def second_kernel(*refs):
        far, rest = refs[:len(apart)], refs[len(apart):]
        twice_kernel(far, *rest)

    made = pl.pallas_call(
        second_kernel,
        out_shape=jax.ShapeDtypeStruct((FREQS, rows, width), jnp.bfloat16),
        in_specs=[in_vmem] * (len(apart) + 3) + [in_smem, in_vmem],
        out_specs=in_vmem,
        scratch_shapes=[VMEM((width, width), jnp.bfloat16)] * 2,
        compiler_params=large,
        name="twice",
    )(*apart, *early, steps, bare)

    def kernel(*refs):
        dyson_kernel(*refs[:7], refs[7:7 + sides], *refs[7 + sides:])

    return pl.pallas_call(
        kernel,
        out_shape=(
            jax.ShapeDtypeStruct((FREQS, rows, width), jnp.bfloat16),
            jax.ShapeDtypeStruct((rows + EXTRA, width), jnp.float32),
            jax.ShapeDtypeStruct((rows, width), jnp.float32),
            jax.ShapeDtypeStruct((EXTRA, width), jnp.float32),
        ),
        in_specs=[in_vmem] + [in_smem] * 2 + [in_hbm] + [in_vmem] * (3 + sides),
        out_specs=(in_hbm,) + (in_vmem,) * 3,
        scratch_shapes=[VMEM((rows, width), jnp.float32)] + [pltpu.SemaphoreType.DMA] * 2,
        compiler_params=large,
        name="dyson",
    )(made, offsets, level, held(hamiltonian), two, four, odd, *beside)


def columns(value, first):
    rows = value.shape[0]
    left, right = value[:, :rows], value[:, rows:]
    return jnp.where(first, left, right), jnp.where(first, right, left)


def begin_kernel(step_ref, packed_ref, own_ref, square_ref, high_ref, low_ref):
    rows, _ = step_ref.shape
    high, low = halves(packed_ref[:rows, :])
    high_ref[...], low_ref[...] = high, low
    near, _ = columns(step_ref[...] * own_ref[0:1], lax.axis_index("rep") == 0)
    square_ref[...] = product(near, high, low)


def finish_kernel(steps_ref, step_ref, square_ref, high_ref, low_ref, theirs_ref, own_ref, out_ref,
                  made, sems):
    rows, _ = step_ref.shape
    rep = lax.axis_index("rep")
    first = rep == 0
    tail = theirs_ref[rows:, :]
    factors = own_ref[0:1] + whole_of(tail[0:1], tail[1:2], tail[2:3])
    inverses = own_ref[1:2] + whole_of(tail[3:4], tail[4:5], tail[5:6])
    theirs = halves(theirs_ref[:rows, :])
    step = step_ref[...]
    _, far = columns(step * factors, first)
    square = square_ref[...] + product(far, *theirs)
    near, far = columns(square * factors, first)
    writes = []
    for half in range(2):
        at = slice(half * rows, (half + 1) * rows)
        cube = product(near, high_ref[:, at], low_ref[:, at]) + product(
            far, theirs[0][:, at], theirs[1][:, at]
        )
        col = lax.broadcasted_iota(jnp.int32, (rows, rows), 1) + half * rows
        row = lax.broadcasted_iota(jnp.int32, (rows, rows), 0) + rep * rows
        total = jnp.where(col == row, 1.0, step[:, at])
        total = total + jnp.where(steps_ref[0] >= 2, square[:, at] + cube, 0.0)
        made[:, at] = total * inverses[:, at]
        writes.append(pltpu.make_async_copy(made.at[:, at], out_ref.at[:, at], sems.at[half]))
        writes[-1].start()
    for write in writes:
        write.wait()


def body(
    green_blocks, occupation, offsets, coulomb, hamiltonian, onsite_level, green_steps, screen_steps
):
    green = green_blocks[0, 0]
    bare = coulomb[0]
    rows, width = green.shape
    share = rows // lax.axis_size("energy")
    make = polar_share if in_squares() and share % 16 == 0 else polar_share_plain
    scalars = (screen_steps, green_steps, onsite_level)
    pieces = gathered(make(green, occupation, offsets, bare, scalars))

    two = shifted(green, "energy", 2)
    four = shifted(two, "energy", 2)
    odd = shifted(chosen(offsets, two, green), "energy", 1)

    slabs = lax.axis_size("slab")
    if slabs == 2:
        beside = [lax.ppermute(green, "slab", [(0, 1), (1, 0)])]
    else:
        up = [(i, i + 1) for i in range(slabs - 1)]
        down = [(j, i) for i, j in up]
        beside = [lax.ppermute(green, "slab", up), lax.ppermute(green, "slab", down)]

    screened, packed, step, own = dyson_rows(
        pieces, offsets, screen_steps, onsite_level, bare, hamiltonian[0], two, four, odd, beside
    )
    theirs = lax.ppermute(packed.astype(coded), "rep", [(0, 1), (1, 0)]).astype(jnp.float32)
    wide = jax.ShapeDtypeStruct((rows, width), jnp.float32)
    thin = jax.ShapeDtypeStruct((rows, width), jnp.bfloat16)
    square, high, low = pl.pallas_call(
        begin_kernel,
        out_shape=(wide, thin, thin),
        in_specs=[in_vmem] * 3,
        out_specs=(in_vmem,) * 3,
        compiler_params=small,
        name="begin",
    )(step, packed, own)
    green_next = pl.pallas_call(
        finish_kernel,
        out_shape=wide,
        in_specs=[in_smem] + [in_vmem] * 6,
        out_specs=in_hbm,
        scratch_shapes=[VMEM((rows, width), jnp.float32), pltpu.SemaphoreType.DMA((2,))],
        compiler_params=large,
        name="finish",
    )(green_steps, step, square, high, low, theirs, own)
    return green_next[None, None], screened[:, None]


def chosen_kernel(offsets_ref, two_ref, green_ref, out_ref):
    three = jnp.minimum(offsets_ref[0], offsets_ref[1]) == 3

    @pl.when(three)
    def _():
        out_ref[...] = two_ref[...]

    @pl.when(jnp.logical_not(three))
    def _():
        out_ref[...] = green_ref[...]


def chosen(offsets, two, green):
    return pl.pallas_call(
        chosen_kernel,
        out_shape=jax.ShapeDtypeStruct(green.shape, green.dtype),
        in_specs=[in_smem, in_vmem, in_vmem],
        out_specs=in_vmem,
        compiler_params=small,
        name="chosen",
    )(offsets, two, green)


def solution(mesh):
    return jax.shard_map(
        body,
        mesh=mesh,
        in_specs=(
            P("energy", "slab", "rep", None),
            P("energy"),
            P(),
            P("slab", "rep", None),
            P("slab", "rep", None),
            P("energy"),
            P("energy"),
            P(),
        ),
        out_specs=(P("energy", "slab", "rep", None), P(None, "slab", "rep", None)),
        check_vma=False,
    )
```

```python
import jax
import jax.numpy as jnp
from jax import lax
from jax.experimental import pallas as pl
from jax.experimental.pallas import tpu as pltpu
from jax.sharding import PartitionSpec as P


SHIFTS = 4
FREQS = 2
EXTRA = 8

coded = jnp.float16
VMEM = pltpu.VMEM
in_vmem = pl.BlockSpec(memory_space=pltpu.VMEM)
in_smem = pl.BlockSpec(memory_space=pltpu.SMEM)
in_place = pl.BlockSpec(memory_space=pl.ANY)
in_hbm = pl.BlockSpec(memory_space=pltpu.HBM)
small = pltpu.CompilerParams(vmem_limit_bytes=6 << 20)
large = pltpu.CompilerParams(vmem_limit_bytes=16 << 20)


def held(value):
    return pltpu.with_memory_space_constraint(value, pltpu.HBM)


def halves(value):
    high = value.astype(jnp.bfloat16)
    return high, (value - high.astype(jnp.float32)).astype(jnp.bfloat16)


def dot(first, second):
    return jnp.dot(first, second, preferred_element_type=jnp.float32)


def product(first, high, low):
    top, rest = halves(first)
    return dot(top, high) + dot(top, low) + dot(rest, high)


def shifted(block, axis, distance):
    count = lax.axis_size(axis)
    route = [(i, i + distance) for i in range(count - distance)]
    return lax.ppermute(block, axis, route)


def partner(z, k, outer):
    return z ^ k if outer & (outer - 1) == 0 else (z + k) % outer


def origin(z, k, outer):
    return z ^ k if outer & (outer - 1) == 0 else (z + outer - k) % outer


def in_squares():
    energies = lax.axis_size("energy")
    return energies % 2 == 0 and energies <= 16 and lax.axis_size("rep") == 2


def share_of(place):
    outer = lax.axis_size("energy") // 2
    return place % 2 * outer + place // 2 if in_squares() else place


def weight_rows(weight, first_row, width):
    weight = jnp.full((EXTRA, width), weight, jnp.float32)
    first = weight.astype(jnp.bfloat16).astype(jnp.float32)
    second = (weight - first).astype(jnp.bfloat16).astype(jnp.float32)
    third = weight - first - second
    row = lax.broadcasted_iota(jnp.int32, (EXTRA, width), 0) - first_row
    later = jnp.where(row == 1, second, jnp.where(row == 2, third, 0.0))
    return jnp.where(row == 0, first, later)


def prepare_kernel(weight_ref, block_ref, out_ref, arrived):
    half, width = out_ref.shape[0] - EXTRA, out_ref.shape[1]
    x = lax.axis_index("energy") % 2
    start = pl.multiple_of((1 - x) * half, half)
    copy = pltpu.make_async_copy(
        block_ref.at[pl.ds(start, half), :], out_ref.at[pl.ds(0, half), :], arrived
    )
    copy.start()
    out_ref[half:, :] = weight_rows(weight_ref[0], 3, width).astype(out_ref.dtype)
    copy.wait()


def arrange_kernel(weight_ref, block_ref, got_ref, *out_refs):
    outer = len(out_refs) + 1
    half, width = got_ref.shape[0] - EXTRA, got_ref.shape[1]
    share = half // outer
    x, z = lax.axis_index("energy") % 2, lax.axis_index("energy") // 2
    tail = weight_rows(weight_ref[0], 0, width) + got_ref[half:, :].astype(jnp.float32)
    tail = tail.astype(got_ref.dtype)
    for k, out_ref in enumerate(out_refs, 1):
        at = partner(z, k, outer) * share
        mine = pl.ds(pl.multiple_of(x * half + at, share), share)
        out_ref[:share, :] = block_ref[mine, :]
        out_ref[share:2 * share, :] = got_ref[pl.ds(pl.multiple_of(at, share), share), :]
        out_ref[2 * share:, :] = tail


def polar_kernel(received, weight_ref, offsets_ref, block_ref, got_ref, bare_ref, out_ref,
                 padded, weighted, bare_rows, arrived):
    _, share, width = out_ref.shape
    energies = weighted.shape[0]
    outer = energies // 2
    half = outer * share
    energy = lax.axis_index("energy")
    x, z = energy % 2, energy // 2
    start = pl.multiple_of(x * half + z * share, share)
    copy = pltpu.make_async_copy(bare_ref.at[pl.ds(start, share), :], bare_rows, arrived)
    copy.start()
    padded[:SHIFTS] = jnp.zeros((SHIFTS, share, width), jnp.float32)

    def place(at, rows, weight):
        rows = rows.astype(jnp.float32)
        padded[SHIFTS + at] = rows
        weighted[at] = rows * weight

    def total(tail, row):
        return tail[row:row + 1] + tail[row + 1:row + 2] + tail[row + 2:row + 3]

    place(energy, block_ref[pl.ds(start, share), :], weight_ref[0])
    place(
        z * 2 + 1 - x,
        got_ref[pl.ds(pl.multiple_of(z * share, share), share), :],
        total(got_ref[half:, :].astype(jnp.float32), 3),
    )
    for k, ref in enumerate(received, 1):
        behind = origin(z, k, outer) * 2
        tail = ref[2 * share:, :].astype(jnp.float32)
        place(behind + x, ref[:share, :], total(tail, 0))
        place(behind + 1 - x, ref[share:2 * share, :], total(tail, 3))
    totals = [jnp.zeros((share, width), jnp.float32) for _ in range(FREQS)]
    for e in range(energies):
        own = weighted[e]
        for f in range(FREQS):
            totals[f] += own * padded[SHIFTS + e - offsets_ref[f]]
    copy.wait()
    factor = -(width ** -0.5) * energies ** -0.5
    for f in range(FREQS):
        out_ref[f] = totals[f] * (factor * bare_rows[...])


def polar_share(green, weight, offsets, bare, scalars):
    energies = lax.axis_size("energy")
    rows, width = green.shape
    outer = energies // 2
    share = rows // energies
    half = rows // 2
    sent = pl.pallas_call(
        prepare_kernel,
        out_shape=jax.ShapeDtypeStruct((half + EXTRA, width), green.dtype),
        in_specs=[in_smem, in_hbm],
        out_specs=in_vmem,
        scratch_shapes=[pltpu.SemaphoreType.DMA],
        compiler_params=small,
        name="prepare",
    )(weight, held(green))
    got = lax.ppermute(sent, "energy", [(e, e ^ 1) for e in range(energies)])
    shares = pl.pallas_call(
        arrange_kernel,
        out_shape=(jax.ShapeDtypeStruct((2 * share + EXTRA, width), green.dtype),) * (outer - 1),
        in_specs=[in_smem, in_vmem, in_vmem],
        out_specs=(in_vmem,) * (outer - 1),
        compiler_params=small,
        name="arrange",
    )(weight, green, got)
    received = [None] * (outer - 1)
    for k in range(1, outer):
        route = [(z * 2 + x, partner(z, k, outer) * 2 + x) for z in range(outer) for x in range(2)]
        received[k - 1] = lax.ppermute(shares[k - 1], "energy", route)

    def kernel(*refs):
        count = outer - 1
        polar_kernel(refs[:count], *refs[count:count + 2], *refs[count + 5:])

    return pl.pallas_call(
        kernel,
        out_shape=jax.ShapeDtypeStruct((FREQS, share, width), jnp.float32),
        in_specs=[in_vmem] * (outer - 1) + [in_smem] * 5 + [in_vmem, in_vmem, in_place],
        out_specs=in_vmem,
        scratch_shapes=[
            VMEM((SHIFTS + energies, share, width), jnp.float32),
            VMEM((energies, share, width), jnp.float32),
            VMEM((share, width), jnp.float32),
            pltpu.SemaphoreType.DMA,
        ],
        compiler_params=small,
        name="polar",
    )(*received, weight, offsets, *scalars, green, got, bare)


def polar_share_plain(green, weight, offsets, bare, scalars):
    energies = lax.axis_size("energy")
    rows, width = green.shape
    share = rows // energies
    weights = lax.all_gather(weight, "energy", axis=0, tiled=True)
    parts = green.reshape(energies, share, width)
    parts = jnp.stack([parts[share_of(k)] for k in range(energies)]) if in_squares() else parts
    got = lax.all_to_all(parts, "energy", 0, 0, tiled=True)
    wide = got.astype(jnp.float32)
    weighted = wide * weights[:, None, None]
    padded = jnp.concatenate([jnp.zeros((SHIFTS,) + wide.shape[1:], wide.dtype), wide], axis=0)
    own = lax.dynamic_slice_in_dim(bare, share_of(lax.axis_index("energy")) * share, share, 0)
    factor = -(width ** -0.5) * energies ** -0.5
    chunks = []
    for f in range(FREQS):
        low = lax.dynamic_slice_in_dim(padded, SHIFTS - offsets[f], energies, 0)
        chunks.append(factor * own * jnp.sum(weighted * low, axis=0))
    return jnp.stack(chunks)


def gather_energy(chunk):
    outer = lax.axis_size("energy") // 2
    here = lax.axis_index("energy") // 2
    wholes = [
        lax.dynamic_update_index_in_dim(jnp.zeros((outer,) + part.shape, part.dtype), part, here, 0)
        for part in chunk
    ]
    for k in range(1, outer):
        route = [(z * 2 + x, partner(z, k, outer) * 2 + x) for z in range(outer) for x in range(2)]
        got = lax.ppermute(chunk, "energy", route)
        wholes = [
            lax.dynamic_update_index_in_dim(whole, part, origin(here, k, outer), 0)
            for whole, part in zip(wholes, got)
        ]
    return wholes


def gather_square(parts):
    energies = lax.axis_size("energy")

    def along_x(part):
        return lax.ppermute(part, "energy", [(e, e ^ 1) for e in range(energies)])

    def along_rep(part):
        return lax.ppermute(part, "rep", [(0, 1), (1, 0)])

    beside = [along_x(part) for part in parts]
    above = [along_rep(part) for part in parts]
    apart = [along_rep(beside[0]), along_x(above[1])]
    return [*parts, *beside, *above, *apart]


def gathered(chunk):
    chunk = chunk.astype(coded)
    if in_squares():
        pieces = gather_square(gather_energy(chunk))
    else:
        pieces = [lax.all_gather(chunk, ("rep", "energy"), axis=1, tiled=True)]
    return [piece.astype(jnp.float32) for piece in pieces]


def parts_of(value):
    size = jnp.abs(value)
    exponent = jnp.where(size > 0.0, jnp.floor(jnp.log2(jnp.where(size > 0.0, size, 1.0))), 0.0)
    exponent = jnp.clip(exponent, -120.0, 120.0)
    mantissa = value * jnp.exp2(-exponent)
    first = mantissa.astype(jnp.bfloat16).astype(jnp.float32)
    second = (mantissa - first).astype(jnp.bfloat16).astype(jnp.float32)
    return exponent, first, second


def whole_of(exponent, first, second):
    return (first + second) * jnp.exp2(exponent)


def corner_start(place, block, rows):
    x, rep = lax.axis_index("energy") % 2, lax.axis_index("rep")
    at_x = 1 - x if place % 2 else x
    at_rep = 1 - rep if place >= 2 else rep
    return pl.multiple_of(at_rep * rows + at_x * block, block)


def early_kernel(pieces, bare_ref, once_ref, high, low):
    rows, width = bare_ref.shape
    if len(pieces) == 1:
        for f in range(FREQS):
            high[f], low[f] = halves(pieces[0][f])
    else:
        outer, share, _ = pieces[0].shape
        block = outer * share
        empty = jnp.zeros((block, width), jnp.bfloat16)
        for f in range(FREQS):
            for place in range(4):
                at = pl.ds(corner_start(place, block, rows), block)
                if place == 3:
                    high[f, at, :], low[f, at, :] = empty, empty
                else:
                    upper, lower = halves(pieces[place * FREQS + f][...].reshape(block, width))
                    high[f, at, :], low[f, at, :] = upper, lower
    bare = bare_ref[...]
    for f in range(FREQS):
        once_ref[f] = bare + product(bare, high[f], low[f])


def dyson_kernel(apart, early, offsets_ref, steps_ref, level_ref, bare_ref, hamiltonian_ref, two_ref,
                 four_ref, odd_ref, beside_refs, screened_ref, packed_ref, step_ref, own_ref,
                 high, low, made, hamiltonian_rows, made_sem, hamiltonian_sem):
    once_ref, high_ref, low_ref = early
    rows, width = bare_ref.shape
    entry_scale = width ** -0.5
    read = pltpu.make_async_copy(hamiltonian_ref, hamiltonian_rows, hamiltonian_sem)
    read.start()
    rep = lax.axis_index("rep")
    bare = bare_ref[...]
    once = [once_ref[f] for f in range(FREQS)]
    at = jnp.where(steps_ref[1] > steps_ref[0], 1, 0)
    high[...], low[...] = high_ref[at], low_ref[at]
    if apart:
        outer, share, _ = apart[0].shape
        block = outer * share
        start = corner_start(3, block, rows)
        beyond = bare_ref[:, pl.ds(start, block)]
        parts = [halves(ref[...].reshape(block, width)) for ref in apart]
        once = [once[f] + product(beyond, *parts[f]) for f in range(FREQS)]
        high[pl.ds(start, block), :] = jnp.where(at == 0, parts[0][0], parts[1][0])
        low[pl.ds(start, block), :] = jnp.where(at == 0, parts[0][1], parts[1][1])
    last = jnp.where(at == 0, once[0], once[1])
    upper, lower = high[...], low[...]
    twice = last + product(product(last, upper, lower), upper, lower)
    other = jnp.minimum(offsets_ref[0], offsets_ref[1])
    less = jnp.where(other == 2, two_ref[...], odd_ref[...])
    four = four_ref[...]
    energy_terms = jnp.zeros((rows, width), jnp.float32)
    for f in range(FREQS):
        count = steps_ref[f]
        value = jnp.where(count == 0, bare, jnp.where(count == 1, once[f], twice))
        value = value.astype(jnp.bfloat16)
        made[f] = value
        lowered = jnp.where(offsets_ref[f] == SHIFTS, four, less).astype(jnp.float32)
        energy_terms += lowered * value.astype(jnp.float32)
    write = pltpu.make_async_copy(made, screened_ref, made_sem)
    write.start()
    read.wait()
    beside = sum(ref[...].astype(jnp.float32) for ref in beside_refs)
    rest = hamiltonian_rows[...] - entry_scale * energy_terms - (0.5 * entry_scale) * beside
    col = lax.broadcasted_iota(jnp.int32, (rows, width), 1)
    row = lax.broadcasted_iota(jnp.int32, (rows, width), 0) + rep * rows
    on = col == row
    diagonal = level_ref[0] + jnp.sum(jnp.where(on, rest, 0.0), axis=1, keepdims=True)
    off = jnp.where(on, 0.0, rest)
    largest = jnp.max(jnp.abs(off), axis=1, keepdims=True)
    largest = jnp.where(largest > 0.0, largest, 1.0)
    unit = off * (1.0 / largest)
    inverse = 1.0 / diagonal
    factor = -largest * inverse
    step_ref[...] = unit * factor
    factor_row = jnp.sum(jnp.where(on, factor, 0.0), axis=0, keepdims=True)
    inverse_row = jnp.sum(jnp.where(on, inverse, 0.0), axis=0, keepdims=True)
    blank = jnp.zeros((1, width), jnp.float32)
    packed_ref[:rows, :] = unit
    packed_ref[rows:, :] = jnp.concatenate(
        [*parts_of(factor_row), *parts_of(inverse_row), blank, blank], axis=0
    )
    own_ref[...] = jnp.concatenate([factor_row, inverse_row] + [blank] * 6, axis=0)
    write.wait()


def dyson_rows(pieces, offsets, steps, level, bare, hamiltonian, two, four, odd, beside):
    rows, width = bare.shape
    sides = len(beside)
    known, apart = (pieces, []) if len(pieces) == 1 else (pieces[:-FREQS], pieces[-FREQS:])
    count = len(known)

    def first_kernel(*refs):
        early_kernel(refs[:count], *refs[count:])

    early = pl.pallas_call(
        first_kernel,
        out_shape=(jax.ShapeDtypeStruct((FREQS, rows, width), jnp.float32),)
        + (jax.ShapeDtypeStruct((FREQS, width, width), jnp.bfloat16),) * 2,
        in_specs=[in_vmem] * (count + 1),
        out_specs=(in_vmem,) * 3,
        compiler_params=large,
        name="early",
    )(*known, bare)

    def kernel(*refs):
        far, rest = refs[:len(apart)], refs[len(apart):]
        done, rest = rest[:3], rest[3:]
        named, rest = rest[:8], rest[8:]
        dyson_kernel(far, done, *named, rest[:sides], *rest[sides:])

    return pl.pallas_call(
        kernel,
        out_shape=(
            jax.ShapeDtypeStruct((FREQS, rows, width), jnp.bfloat16),
            jax.ShapeDtypeStruct((rows + EXTRA, width), jnp.float32),
            jax.ShapeDtypeStruct((rows, width), jnp.float32),
            jax.ShapeDtypeStruct((EXTRA, width), jnp.float32),
        ),
        in_specs=[in_vmem] * (len(apart) + 3) + [in_smem] * 3 + [in_vmem, in_hbm]
        + [in_vmem] * (3 + sides),
        out_specs=(in_hbm,) + (in_vmem,) * 3,
        scratch_shapes=[VMEM((width, width), jnp.bfloat16)] * 2
        + [VMEM((FREQS, rows, width), jnp.bfloat16), VMEM((rows, width), jnp.float32)]
        + [pltpu.SemaphoreType.DMA] * 2,
        compiler_params=large,
        name="dyson",
    )(*apart, *early, offsets, steps, level, bare, held(hamiltonian), two, four, odd, *beside)


def columns(value, first):
    rows = value.shape[0]
    left, right = value[:, :rows], value[:, rows:]
    return jnp.where(first, left, right), jnp.where(first, right, left)


def begin_kernel(step_ref, packed_ref, own_ref, square_ref, high_ref, low_ref):
    rows, _ = step_ref.shape
    high, low = halves(packed_ref[:rows, :])
    high_ref[...], low_ref[...] = high, low
    near, _ = columns(step_ref[...] * own_ref[0:1], lax.axis_index("rep") == 0)
    square_ref[...] = product(near, high, low)


def finish_kernel(steps_ref, step_ref, square_ref, high_ref, low_ref, theirs_ref, own_ref, out_ref,
                  made, sems):
    rows, _ = step_ref.shape
    rep = lax.axis_index("rep")
    first = rep == 0
    tail = theirs_ref[rows:, :]
    factors = own_ref[0:1] + whole_of(tail[0:1], tail[1:2], tail[2:3])
    inverses = own_ref[1:2] + whole_of(tail[3:4], tail[4:5], tail[5:6])
    theirs = halves(theirs_ref[:rows, :])
    step = step_ref[...]
    _, far = columns(step * factors, first)
    square = square_ref[...] + product(far, *theirs)
    near, far = columns(square * factors, first)
    writes = []
    for half in range(2):
        at = slice(half * rows, (half + 1) * rows)
        cube = product(near, high_ref[:, at], low_ref[:, at]) + product(
            far, theirs[0][:, at], theirs[1][:, at]
        )
        col = lax.broadcasted_iota(jnp.int32, (rows, rows), 1) + half * rows
        row = lax.broadcasted_iota(jnp.int32, (rows, rows), 0) + rep * rows
        total = jnp.where(col == row, 1.0, step[:, at])
        total = total + jnp.where(steps_ref[0] >= 2, square[:, at] + cube, 0.0)
        made[:, at] = total * inverses[:, at]
        writes.append(pltpu.make_async_copy(made.at[:, at], out_ref.at[:, at], sems.at[half]))
        writes[-1].start()
    for write in writes:
        write.wait()


def body(
    green_blocks, occupation, offsets, coulomb, hamiltonian, onsite_level, green_steps, screen_steps
):
    green = green_blocks[0, 0]
    bare = coulomb[0]
    rows, width = green.shape
    share = rows // lax.axis_size("energy")
    make = polar_share if in_squares() and share % 16 == 0 else polar_share_plain
    scalars = (screen_steps, green_steps, onsite_level)
    pieces = gathered(make(green, occupation, offsets, bare, scalars))

    two = shifted(green, "energy", 2)
    four = shifted(two, "energy", 2)
    odd = shifted(chosen(offsets, two, green), "energy", 1)

    slabs = lax.axis_size("slab")
    if slabs == 2:
        beside = [lax.ppermute(green, "slab", [(0, 1), (1, 0)])]
    else:
        up = [(i, i + 1) for i in range(slabs - 1)]
        down = [(j, i) for i, j in up]
        beside = [lax.ppermute(green, "slab", up), lax.ppermute(green, "slab", down)]

    screened, packed, step, own = dyson_rows(
        pieces, offsets, screen_steps, onsite_level, bare, hamiltonian[0], two, four, odd, beside
    )
    theirs = lax.ppermute(packed.astype(coded), "rep", [(0, 1), (1, 0)]).astype(jnp.float32)
    wide = jax.ShapeDtypeStruct((rows, width), jnp.float32)
    thin = jax.ShapeDtypeStruct((rows, width), jnp.bfloat16)
    square, high, low = pl.pallas_call(
        begin_kernel,
        out_shape=(wide, thin, thin),
        in_specs=[in_vmem] * 3,
        out_specs=(in_vmem,) * 3,
        compiler_params=small,
        name="begin",
    )(step, packed, own)
    green_next = pl.pallas_call(
        finish_kernel,
        out_shape=wide,
        in_specs=[in_smem] + [in_vmem] * 6,
        out_specs=in_hbm,
        scratch_shapes=[VMEM((rows, width), jnp.float32), pltpu.SemaphoreType.DMA((2,))],
        compiler_params=large,
        name="finish",
    )(green_steps, step, square, high, low, theirs, own)
    return green_next[None, None], screened[:, None]


def chosen_kernel(offsets_ref, two_ref, green_ref, out_ref):
    three = jnp.minimum(offsets_ref[0], offsets_ref[1]) == 3

    @pl.when(three)
    def _():
        out_ref[...] = two_ref[...]

    @pl.when(jnp.logical_not(three))
    def _():
        out_ref[...] = green_ref[...]


def chosen(offsets, two, green):
    return pl.pallas_call(
        chosen_kernel,
        out_shape=jax.ShapeDtypeStruct(green.shape, green.dtype),
        in_specs=[in_smem, in_vmem, in_vmem],
        out_specs=in_vmem,
        compiler_params=small,
        name="chosen",
    )(offsets, two, green)


def solution(mesh):
    return jax.shard_map(
        body,
        mesh=mesh,
        in_specs=(
            P("energy", "slab", "rep", None),
            P("energy"),
            P(),
            P("slab", "rep", None),
            P("slab", "rep", None),
            P("energy"),
            P("energy"),
            P(),
        ),
        out_specs=(P("energy", "slab", "rep", None), P(None, "slab", "rep", None)),
        check_vma=False,
    )
```

```python
import jax
import jax.numpy as jnp
from jax import lax
from jax.experimental import pallas as pl
from jax.experimental.pallas import tpu as pltpu
from jax.sharding import PartitionSpec as P


SHIFTS = 4
FREQS = 2
EXTRA = 8

coded = jnp.float16
VMEM = pltpu.VMEM
in_vmem = pl.BlockSpec(memory_space=pltpu.VMEM)
in_smem = pl.BlockSpec(memory_space=pltpu.SMEM)
in_place = pl.BlockSpec(memory_space=pl.ANY)
in_hbm = pl.BlockSpec(memory_space=pltpu.HBM)
small = pltpu.CompilerParams(vmem_limit_bytes=6 << 20)
large = pltpu.CompilerParams(vmem_limit_bytes=16 << 20)


def held(value):
    return pltpu.with_memory_space_constraint(value, pltpu.HBM)


def halves(value):
    high = value.astype(jnp.bfloat16)
    return high, (value - high.astype(jnp.float32)).astype(jnp.bfloat16)


def dot(first, second):
    return jnp.dot(first, second, preferred_element_type=jnp.float32)


def product(first, high, low):
    top, rest = halves(first)
    return dot(top, high) + dot(top, low) + dot(rest, high)


def shifted(block, axis, distance):
    count = lax.axis_size(axis)
    route = [(i, i + distance) for i in range(count - distance)]
    return lax.ppermute(block, axis, route)


def partner(z, k, outer):
    return z ^ k if outer & (outer - 1) == 0 else (z + k) % outer


def origin(z, k, outer):
    return z ^ k if outer & (outer - 1) == 0 else (z + outer - k) % outer


def in_squares():
    energies = lax.axis_size("energy")
    return energies % 2 == 0 and energies <= 10 and lax.axis_size("rep") == 2


def share_of(place):
    outer = lax.axis_size("energy") // 2
    return place % 2 * outer + place // 2 if in_squares() else place


def weight_parts(weight):
    first = weight.astype(jnp.bfloat16).astype(jnp.float32)
    second = (weight - first).astype(jnp.bfloat16).astype(jnp.float32)
    return first, second, weight - first - second


def in_rows(parts, first_row, rows, width):
    row = lax.broadcasted_iota(jnp.int32, (rows, width), 0) - first_row
    total = jnp.zeros((rows, width), jnp.float32)
    for k, part in enumerate(parts):
        total = total + jnp.where(row == k, part, 0.0)
    return total


def split_kernel(weight_ref, block_ref, *refs):
    out_refs, arrived = refs[:-1], refs[-1]
    outer = len(out_refs) + 1
    tall, width = out_refs[0].shape
    share = (tall - EXTRA) // 2
    z = lax.axis_index("energy") // 2
    copies = []
    for k, out_ref in enumerate(out_refs, 1):
        for x in range(2):
            at = pl.multiple_of((x * outer + partner(z, k, outer)) * share, share)
            copies.append(pltpu.make_async_copy(
                block_ref.at[pl.ds(at, share), :], out_ref.at[pl.ds(x * share, share), :],
                arrived.at[len(copies)],
            ))
            copies[-1].start()
    weight = jnp.full((EXTRA, width), weight_ref[0], jnp.float32)
    tail = in_rows(weight_parts(weight), 0, EXTRA, width).astype(out_refs[0].dtype)
    for out_ref in out_refs:
        out_ref[2 * share:, :] = tail
    for copy in copies:
        copy.wait()


def collect_kernel(received, weight_ref, block_ref, out_ref):
    outer = len(received) + 1
    tall, width = out_ref.shape
    share = (tall - 2 * EXTRA) // outer
    x, z = lax.axis_index("energy") % 2, lax.axis_index("energy") // 2
    at = pl.multiple_of(((1 - x) * outer + z) * share, share)
    out_ref[:share, :] = block_ref[pl.ds(at, share), :]
    weight = jnp.full((1, width), weight_ref[0], jnp.float32)
    tail = in_rows(weight_parts(weight), 0, 2 * EXTRA, width)
    for k, ref in enumerate(received, 1):
        at = pl.multiple_of((1 - x) * share, share)
        out_ref[k * share:(k + 1) * share, :] = ref[pl.ds(at, share), :]
        parts = ref[2 * share:, :].astype(jnp.float32)
        tail = tail + in_rows([parts[i:i + 1] for i in range(3)], 3 * k, 2 * EXTRA, width)
    out_ref[outer * share:, :] = tail.astype(out_ref.dtype)


def polar_kernel(received, weight_ref, offsets_ref, block_ref, got_ref, bare_ref, out_ref,
                 padded, weighted, bare_rows, arrived):
    _, share, width = out_ref.shape
    energies = weighted.shape[0]
    outer = energies // 2
    energy = lax.axis_index("energy")
    x, z = energy % 2, energy // 2
    start = pl.multiple_of((x * outer + z) * share, share)
    copy = pltpu.make_async_copy(bare_ref.at[pl.ds(start, share), :], bare_rows, arrived)
    copy.start()
    padded[:SHIFTS] = jnp.zeros((SHIFTS, share, width), jnp.float32)

    def place(at, rows, weight):
        rows = rows.astype(jnp.float32)
        padded[SHIFTS + at] = rows
        weighted[at] = rows * weight

    def total(tail, row):
        return tail[row:row + 1] + tail[row + 1:row + 2] + tail[row + 2:row + 3]

    place(energy, block_ref[pl.ds(start, share), :], weight_ref[0])
    for k, ref in enumerate(received, 1):
        rows = ref[pl.ds(pl.multiple_of(x * share, share), share), :]
        place(origin(z, k, outer) * 2 + x, rows, total(ref[2 * share:, :].astype(jnp.float32), 0))
    tail = got_ref[outer * share:, :].astype(jnp.float32)
    for k in range(outer):
        rows = got_ref[k * share:(k + 1) * share, :]
        place((origin(z, k, outer) if k else z) * 2 + 1 - x, rows, total(tail, 3 * k))
    totals = [jnp.zeros((share, width), jnp.float32) for _ in range(FREQS)]
    for e in range(energies):
        own = weighted[e]
        for f in range(FREQS):
            totals[f] += own * padded[SHIFTS + e - offsets_ref[f]]
    copy.wait()
    factor = -(width ** -0.5) * energies ** -0.5
    for f in range(FREQS):
        out_ref[f] = totals[f] * (factor * bare_rows[...])


def polar_share(green, weight, offsets, bare, scalars):
    energies = lax.axis_size("energy")
    rows, width = green.shape
    outer = energies // 2
    share = rows // energies
    count = outer - 1
    shares = pl.pallas_call(
        split_kernel,
        out_shape=(jax.ShapeDtypeStruct((2 * share + EXTRA, width), green.dtype),) * count,
        in_specs=[in_smem, in_hbm],
        out_specs=(in_vmem,) * count,
        scratch_shapes=[pltpu.SemaphoreType.DMA((2 * count,))],
        compiler_params=small,
        name="split",
    )(weight, held(green))
    received = [None] * count
    for k in range(count, 0, -1):
        route = [(z * 2 + x, partner(z, k, outer) * 2 + x) for z in range(outer) for x in range(2)]
        received[k - 1] = lax.ppermute(shares[k - 1], "energy", route)

    def second_kernel(*refs):
        collect_kernel(refs[:count], refs[count], *refs[count + 4:])

    sent = pl.pallas_call(
        second_kernel,
        out_shape=jax.ShapeDtypeStruct((outer * share + 2 * EXTRA, width), green.dtype),
        in_specs=[in_vmem] * count + [in_smem] * 4 + [in_vmem],
        out_specs=in_vmem,
        compiler_params=small,
        name="collect",
    )(*received, weight, *scalars, green)
    got = lax.ppermute(sent, "energy", [(e, e ^ 1) for e in range(energies)])

    def kernel(*refs):
        polar_kernel(refs[:count], *refs[count:])

    return pl.pallas_call(
        kernel,
        out_shape=jax.ShapeDtypeStruct((FREQS, share, width), jnp.float32),
        in_specs=[in_vmem] * count + [in_smem] * 2 + [in_vmem, in_vmem, in_place],
        out_specs=in_vmem,
        scratch_shapes=[
            VMEM((SHIFTS + energies, share, width), jnp.float32),
            VMEM((energies, share, width), jnp.float32),
            VMEM((share, width), jnp.float32),
            pltpu.SemaphoreType.DMA,
        ],
        compiler_params=small,
        name="polar",
    )(*received, weight, offsets, green, got, bare)


def polar_share_plain(green, weight, offsets, bare, scalars):
    energies = lax.axis_size("energy")
    rows, width = green.shape
    share = rows // energies
    weights = lax.all_gather(weight, "energy", axis=0, tiled=True)
    parts = green.reshape(energies, share, width)
    parts = jnp.stack([parts[share_of(k)] for k in range(energies)]) if in_squares() else parts
    got = lax.all_to_all(parts, "energy", 0, 0, tiled=True)
    wide = got.astype(jnp.float32)
    weighted = wide * weights[:, None, None]
    padded = jnp.concatenate([jnp.zeros((SHIFTS,) + wide.shape[1:], wide.dtype), wide], axis=0)
    own = lax.dynamic_slice_in_dim(bare, share_of(lax.axis_index("energy")) * share, share, 0)
    factor = -(width ** -0.5) * energies ** -0.5
    chunks = []
    for f in range(FREQS):
        low = lax.dynamic_slice_in_dim(padded, SHIFTS - offsets[f], energies, 0)
        chunks.append(factor * own * jnp.sum(weighted * low, axis=0))
    return jnp.stack(chunks)


def gather_energy(chunk):
    outer = lax.axis_size("energy") // 2
    here = lax.axis_index("energy") // 2
    wholes = [
        lax.dynamic_update_index_in_dim(jnp.zeros((outer,) + part.shape, part.dtype), part, here, 0)
        for part in chunk
    ]
    for k in range(outer - 1, 0, -1):
        route = [(z * 2 + x, partner(z, k, outer) * 2 + x) for z in range(outer) for x in range(2)]
        got = lax.ppermute(chunk, "energy", route)
        wholes = [
            lax.dynamic_update_index_in_dim(whole, part, origin(here, k, outer), 0)
            for whole, part in zip(wholes, got)
        ]
    return wholes


def gather_square(parts):
    energies = lax.axis_size("energy")

    def along_x(part):
        return lax.ppermute(part, "energy", [(e, e ^ 1) for e in range(energies)])

    def along_rep(part):
        return lax.ppermute(part, "rep", [(0, 1), (1, 0)])

    beside = [along_x(part) for part in parts]
    above = [along_rep(part) for part in parts]
    apart = [along_rep(beside[0]), along_x(above[1])]
    return [*parts, *beside, *above, *apart]


def gathered(chunk):
    chunk = chunk.astype(coded)
    if in_squares():
        pieces = gather_square(gather_energy(chunk))
    else:
        pieces = [lax.all_gather(chunk, ("rep", "energy"), axis=1, tiled=True)]
    return [piece.astype(jnp.float32) for piece in pieces]


def parts_of(value):
    size = jnp.abs(value)
    exponent = jnp.where(size > 0.0, jnp.floor(jnp.log2(jnp.where(size > 0.0, size, 1.0))), 0.0)
    exponent = jnp.clip(exponent, -120.0, 120.0)
    mantissa = value * jnp.exp2(-exponent)
    first = mantissa.astype(jnp.bfloat16).astype(jnp.float32)
    second = (mantissa - first).astype(jnp.bfloat16).astype(jnp.float32)
    return exponent, first, second


def whole_of(exponent, first, second):
    return (first + second) * jnp.exp2(exponent)


def corner_start(place, block, rows):
    x, rep = lax.axis_index("energy") % 2, lax.axis_index("rep")
    at_x = 1 - x if place % 2 else x
    at_rep = 1 - rep if place >= 2 else rep
    return pl.multiple_of(at_rep * rows + at_x * block, block)


def early_kernel(pieces, bare_ref, once_ref, high, low):
    rows, width = bare_ref.shape
    if len(pieces) == 1:
        for f in range(FREQS):
            high[f], low[f] = halves(pieces[0][f])
    else:
        outer, share, _ = pieces[0].shape
        block = outer * share
        empty = jnp.zeros((block, width), jnp.bfloat16)
        for f in range(FREQS):
            for place in range(4):
                at = pl.ds(corner_start(place, block, rows), block)
                if place == 3:
                    high[f, at, :], low[f, at, :] = empty, empty
                else:
                    upper, lower = halves(pieces[place * FREQS + f][...].reshape(block, width))
                    high[f, at, :], low[f, at, :] = upper, lower
    bare = bare_ref[...]
    for f in range(FREQS):
        once_ref[f] = bare + product(bare, high[f], low[f])


def dyson_kernel(apart, early, offsets_ref, steps_ref, level_ref, bare_ref, hamiltonian_ref, two_ref,
                 four_ref, odd_ref, beside_refs, screened_ref, packed_ref, step_ref, own_ref,
                 high, low, made, hamiltonian_rows, made_sem, hamiltonian_sem):
    once_ref, high_ref, low_ref = early
    rows, width = bare_ref.shape
    entry_scale = width ** -0.5
    read = pltpu.make_async_copy(hamiltonian_ref, hamiltonian_rows, hamiltonian_sem)
    read.start()
    rep = lax.axis_index("rep")
    bare = bare_ref[...]
    once = [once_ref[f] for f in range(FREQS)]
    at = jnp.where(steps_ref[1] > steps_ref[0], 1, 0)
    high[...], low[...] = high_ref[at], low_ref[at]
    if apart:
        outer, share, _ = apart[0].shape
        block = outer * share
        start = corner_start(3, block, rows)
        beyond = bare_ref[:, pl.ds(start, block)]
        parts = [halves(ref[...].reshape(block, width)) for ref in apart]
        once = [once[f] + product(beyond, *parts[f]) for f in range(FREQS)]
        high[pl.ds(start, block), :] = jnp.where(at == 0, parts[0][0], parts[1][0])
        low[pl.ds(start, block), :] = jnp.where(at == 0, parts[0][1], parts[1][1])
    last = jnp.where(at == 0, once[0], once[1])
    upper, lower = high[...], low[...]
    twice = last + product(product(last, upper, lower), upper, lower)
    other = jnp.minimum(offsets_ref[0], offsets_ref[1])
    less = jnp.where(other == 2, two_ref[...], odd_ref[...])
    four = four_ref[...]
    energy_terms = jnp.zeros((rows, width), jnp.float32)
    for f in range(FREQS):
        count = steps_ref[f]
        value = jnp.where(count == 0, bare, jnp.where(count == 1, once[f], twice))
        value = value.astype(jnp.bfloat16)
        made[f] = value
        lowered = jnp.where(offsets_ref[f] == SHIFTS, four, less).astype(jnp.float32)
        energy_terms += lowered * value.astype(jnp.float32)
    write = pltpu.make_async_copy(made, screened_ref, made_sem)
    write.start()
    read.wait()
    beside = sum(ref[...].astype(jnp.float32) for ref in beside_refs)
    rest = hamiltonian_rows[...] - entry_scale * energy_terms - (0.5 * entry_scale) * beside
    col = lax.broadcasted_iota(jnp.int32, (rows, width), 1)
    row = lax.broadcasted_iota(jnp.int32, (rows, width), 0) + rep * rows
    on = col == row
    diagonal = level_ref[0] + jnp.sum(jnp.where(on, rest, 0.0), axis=1, keepdims=True)
    off = jnp.where(on, 0.0, rest)
    largest = jnp.max(jnp.abs(off), axis=1, keepdims=True)
    largest = jnp.where(largest > 0.0, largest, 1.0)
    unit = off * (1.0 / largest)
    inverse = 1.0 / diagonal
    factor = -largest * inverse
    step_ref[...] = unit * factor
    factor_row = jnp.sum(jnp.where(on, factor, 0.0), axis=0, keepdims=True)
    inverse_row = jnp.sum(jnp.where(on, inverse, 0.0), axis=0, keepdims=True)
    blank = jnp.zeros((1, width), jnp.float32)
    packed_ref[:rows, :] = unit
    packed_ref[rows:, :] = jnp.concatenate(
        [*parts_of(factor_row), *parts_of(inverse_row), blank, blank], axis=0
    )
    own_ref[...] = jnp.concatenate([factor_row, inverse_row] + [blank] * 6, axis=0)
    write.wait()


def dyson_rows(pieces, offsets, steps, level, bare, hamiltonian, two, four, odd, beside):
    rows, width = bare.shape
    sides = len(beside)
    known, apart = (pieces, []) if len(pieces) == 1 else (pieces[:-FREQS], pieces[-FREQS:])
    count = len(known)

    def first_kernel(*refs):
        early_kernel(refs[:count], *refs[count:])

    early = pl.pallas_call(
        first_kernel,
        out_shape=(jax.ShapeDtypeStruct((FREQS, rows, width), jnp.float32),)
        + (jax.ShapeDtypeStruct((FREQS, width, width), jnp.bfloat16),) * 2,
        in_specs=[in_vmem] * (count + 1),
        out_specs=(in_vmem,) * 3,
        compiler_params=large,
        name="early",
    )(*known, bare)

    def kernel(*refs):
        far, rest = refs[:len(apart)], refs[len(apart):]
        done, rest = rest[:3], rest[3:]
        named, rest = rest[:8], rest[8:]
        dyson_kernel(far, done, *named, rest[:sides], *rest[sides:])

    return pl.pallas_call(
        kernel,
        out_shape=(
            jax.ShapeDtypeStruct((FREQS, rows, width), jnp.bfloat16),
            jax.ShapeDtypeStruct((rows + EXTRA, width), jnp.float32),
            jax.ShapeDtypeStruct((rows, width), jnp.float32),
            jax.ShapeDtypeStruct((EXTRA, width), jnp.float32),
        ),
        in_specs=[in_vmem] * (len(apart) + 3) + [in_smem] * 3 + [in_vmem, in_hbm]
        + [in_vmem] * (3 + sides),
        out_specs=(in_hbm,) + (in_vmem,) * 3,
        scratch_shapes=[VMEM((width, width), jnp.bfloat16)] * 2
        + [VMEM((FREQS, rows, width), jnp.bfloat16), VMEM((rows, width), jnp.float32)]
        + [pltpu.SemaphoreType.DMA] * 2,
        compiler_params=large,
        name="dyson",
    )(*apart, *early, offsets, steps, level, bare, held(hamiltonian), two, four, odd, *beside)


def columns(value, first):
    rows = value.shape[0]
    left, right = value[:, :rows], value[:, rows:]
    return jnp.where(first, left, right), jnp.where(first, right, left)


def begin_kernel(step_ref, packed_ref, own_ref, square_ref, high_ref, low_ref):
    rows, _ = step_ref.shape
    high, low = halves(packed_ref[:rows, :])
    high_ref[...], low_ref[...] = high, low
    near, _ = columns(step_ref[...] * own_ref[0:1], lax.axis_index("rep") == 0)
    square_ref[...] = product(near, high, low)


def finish_kernel(steps_ref, step_ref, square_ref, high_ref, low_ref, theirs_ref, own_ref, out_ref,
                  made, sems):
    rows, _ = step_ref.shape
    rep = lax.axis_index("rep")
    first = rep == 0
    tail = theirs_ref[rows:, :]
    factors = own_ref[0:1] + whole_of(tail[0:1], tail[1:2], tail[2:3])
    inverses = own_ref[1:2] + whole_of(tail[3:4], tail[4:5], tail[5:6])
    theirs = halves(theirs_ref[:rows, :])
    step = step_ref[...]
    _, far = columns(step * factors, first)
    square = square_ref[...] + product(far, *theirs)
    near, far = columns(square * factors, first)
    writes = []
    for half in range(2):
        at = slice(half * rows, (half + 1) * rows)
        cube = product(near, high_ref[:, at], low_ref[:, at]) + product(
            far, theirs[0][:, at], theirs[1][:, at]
        )
        col = lax.broadcasted_iota(jnp.int32, (rows, rows), 1) + half * rows
        row = lax.broadcasted_iota(jnp.int32, (rows, rows), 0) + rep * rows
        total = jnp.where(col == row, 1.0, step[:, at])
        total = total + jnp.where(steps_ref[0] >= 2, square[:, at] + cube, 0.0)
        made[:, at] = total * inverses[:, at]
        writes.append(pltpu.make_async_copy(made.at[:, at], out_ref.at[:, at], sems.at[half]))
        writes[-1].start()
    for write in writes:
        write.wait()


def body(
    green_blocks, occupation, offsets, coulomb, hamiltonian, onsite_level, green_steps, screen_steps
):
    green = green_blocks[0, 0]
    bare = coulomb[0]
    rows, width = green.shape
    share = rows // lax.axis_size("energy")
    make = polar_share if in_squares() and share % 16 == 0 else polar_share_plain
    scalars = (screen_steps, green_steps, onsite_level)
    pieces = gathered(make(green, occupation, offsets, bare, scalars))

    two = shifted(green, "energy", 2)
    four = shifted(two, "energy", 2)
    odd = shifted(chosen(offsets, two, green), "energy", 1)

    slabs = lax.axis_size("slab")
    if slabs == 2:
        beside = [lax.ppermute(green, "slab", [(0, 1), (1, 0)])]
    else:
        up = [(i, i + 1) for i in range(slabs - 1)]
        down = [(j, i) for i, j in up]
        beside = [lax.ppermute(green, "slab", up), lax.ppermute(green, "slab", down)]

    screened, packed, step, own = dyson_rows(
        pieces, offsets, screen_steps, onsite_level, bare, hamiltonian[0], two, four, odd, beside
    )
    theirs = lax.ppermute(packed.astype(coded), "rep", [(0, 1), (1, 0)]).astype(jnp.float32)
    wide = jax.ShapeDtypeStruct((rows, width), jnp.float32)
    thin = jax.ShapeDtypeStruct((rows, width), jnp.bfloat16)
    square, high, low = pl.pallas_call(
        begin_kernel,
        out_shape=(wide, thin, thin),
        in_specs=[in_vmem] * 3,
        out_specs=(in_vmem,) * 3,
        compiler_params=small,
        name="begin",
    )(step, packed, own)
    green_next = pl.pallas_call(
        finish_kernel,
        out_shape=wide,
        in_specs=[in_smem] + [in_vmem] * 6,
        out_specs=in_hbm,
        scratch_shapes=[VMEM((rows, width), jnp.float32), pltpu.SemaphoreType.DMA((2,))],
        compiler_params=large,
        name="finish",
    )(green_steps, step, square, high, low, theirs, own)
    return green_next[None, None], screened[:, None]


def chosen_kernel(offsets_ref, two_ref, green_ref, out_ref):
    three = jnp.minimum(offsets_ref[0], offsets_ref[1]) == 3

    @pl.when(three)
    def _():
        out_ref[...] = two_ref[...]

    @pl.when(jnp.logical_not(three))
    def _():
        out_ref[...] = green_ref[...]


def chosen(offsets, two, green):
    return pl.pallas_call(
        chosen_kernel,
        out_shape=jax.ShapeDtypeStruct(green.shape, green.dtype),
        in_specs=[in_smem, in_vmem, in_vmem],
        out_specs=in_vmem,
        compiler_params=small,
        name="chosen",
    )(offsets, two, green)


def solution(mesh):
    return jax.shard_map(
        body,
        mesh=mesh,
        in_specs=(
            P("energy", "slab", "rep", None),
            P("energy"),
            P(),
            P("slab", "rep", None),
            P("slab", "rep", None),
            P("energy"),
            P("energy"),
            P(),
        ),
        out_specs=(P("energy", "slab", "rep", None), P(None, "slab", "rep", None)),
        check_vma=False,
    )
```

```python
import jax
import jax.numpy as jnp
from jax import lax
from jax.experimental import pallas as pl
from jax.experimental.pallas import tpu as pltpu
from jax.sharding import PartitionSpec as P


SHIFTS = 4
FREQS = 2
EXTRA = 8

coded = jnp.float16
VMEM = pltpu.VMEM
in_vmem = pl.BlockSpec(memory_space=pltpu.VMEM)
in_smem = pl.BlockSpec(memory_space=pltpu.SMEM)
in_place = pl.BlockSpec(memory_space=pl.ANY)
in_hbm = pl.BlockSpec(memory_space=pltpu.HBM)
small = pltpu.CompilerParams(vmem_limit_bytes=6 << 20)
large = pltpu.CompilerParams(vmem_limit_bytes=16 << 20)


def held(value):
    return pltpu.with_memory_space_constraint(value, pltpu.HBM)


def halves(value):
    high = value.astype(jnp.bfloat16)
    return high, (value - high.astype(jnp.float32)).astype(jnp.bfloat16)


def dot(first, second):
    return jnp.dot(first, second, preferred_element_type=jnp.float32)


def product(first, high, low):
    top, rest = halves(first)
    return dot(top, high) + dot(top, low) + dot(rest, high)


def shifted(block, axis, distance):
    count = lax.axis_size(axis)
    route = [(i, i + distance) for i in range(count - distance)]
    return lax.ppermute(block, axis, route)


def partner(z, k, outer):
    return z ^ k if outer & (outer - 1) == 0 else (z + k) % outer


def origin(z, k, outer):
    return z ^ k if outer & (outer - 1) == 0 else (z + outer - k) % outer


def in_squares():
    energies = lax.axis_size("energy")
    return energies % 2 == 0 and energies <= 16 and lax.axis_size("rep") == 2


def share_of(place):
    outer = lax.axis_size("energy") // 2
    return place % 2 * outer + place // 2 if in_squares() else place


def weight_rows(weight, first_row, width):
    weight = jnp.full((EXTRA, width), weight, jnp.float32)
    first = weight.astype(jnp.bfloat16).astype(jnp.float32)
    second = (weight - first).astype(jnp.bfloat16).astype(jnp.float32)
    third = weight - first - second
    row = lax.broadcasted_iota(jnp.int32, (EXTRA, width), 0) - first_row
    later = jnp.where(row == 1, second, jnp.where(row == 2, third, 0.0))
    return jnp.where(row == 0, first, later)


def prepare_kernel(weight_ref, block_ref, out_ref):
    half, width = out_ref.shape[0] - EXTRA, out_ref.shape[1]
    x = lax.axis_index("energy") % 2
    out_ref[:half, :] = block_ref[pl.ds(pl.multiple_of((1 - x) * half, half), half), :]
    out_ref[half:, :] = weight_rows(weight_ref[0], 3, width).astype(out_ref.dtype)


def arrange_kernel(weight_ref, block_ref, got_ref, *out_refs):
    outer = len(out_refs) + 1
    half, width = got_ref.shape[0] - EXTRA, got_ref.shape[1]
    share = half // outer
    x, z = lax.axis_index("energy") % 2, lax.axis_index("energy") // 2
    tail = weight_rows(weight_ref[0], 0, width) + got_ref[half:, :].astype(jnp.float32)
    tail = tail.astype(got_ref.dtype)
    for k, out_ref in enumerate(out_refs, 1):
        at = partner(z, k, outer) * share
        mine = pl.ds(pl.multiple_of(x * half + at, share), share)
        out_ref[:share, :] = block_ref[mine, :]
        out_ref[share:2 * share, :] = got_ref[pl.ds(pl.multiple_of(at, share), share), :]
        out_ref[2 * share:, :] = tail


def polar_kernel(received, weight_ref, offsets_ref, block_ref, got_ref, bare_ref, out_ref,
                 padded, weighted, bare_rows, arrived):
    _, share, width = out_ref.shape
    energies = weighted.shape[0]
    outer = energies // 2
    half = outer * share
    energy = lax.axis_index("energy")
    x, z = energy % 2, energy // 2
    start = pl.multiple_of(x * half + z * share, share)
    copy = pltpu.make_async_copy(bare_ref.at[pl.ds(start, share), :], bare_rows, arrived)
    copy.start()
    padded[:SHIFTS] = jnp.zeros((SHIFTS, share, width), jnp.float32)

    def place(at, rows, weight):
        rows = rows.astype(jnp.float32)
        padded[SHIFTS + at] = rows
        weighted[at] = rows * weight

    def total(tail, row):
        return tail[row:row + 1] + tail[row + 1:row + 2] + tail[row + 2:row + 3]

    place(energy, block_ref[pl.ds(start, share), :], weight_ref[0])
    place(
        z * 2 + 1 - x,
        got_ref[pl.ds(pl.multiple_of(z * share, share), share), :],
        total(got_ref[half:, :].astype(jnp.float32), 3),
    )
    for k, ref in enumerate(received, 1):
        behind = origin(z, k, outer) * 2
        tail = ref[2 * share:, :].astype(jnp.float32)
        place(behind + x, ref[:share, :], total(tail, 0))
        place(behind + 1 - x, ref[share:2 * share, :], total(tail, 3))
    totals = [jnp.zeros((share, width), jnp.float32) for _ in range(FREQS)]
    for e in range(energies):
        own = weighted[e]
        for f in range(FREQS):
            totals[f] += own * padded[SHIFTS + e - offsets_ref[f]]
    copy.wait()
    factor = -(width ** -0.5) * energies ** -0.5
    for f in range(FREQS):
        out_ref[f] = totals[f] * (factor * bare_rows[...])


def polar_share(green, weight, offsets, bare, scalars):
    energies = lax.axis_size("energy")
    rows, width = green.shape
    outer = energies // 2
    share = rows // energies
    half = rows // 2
    sent = pl.pallas_call(
        prepare_kernel,
        out_shape=jax.ShapeDtypeStruct((half + EXTRA, width), green.dtype),
        in_specs=[in_smem, in_vmem],
        out_specs=in_vmem,
        compiler_params=small,
        name="prepare",
    )(weight, green)
    got = lax.ppermute(sent, "energy", [(e, e ^ 1) for e in range(energies)])
    shares = pl.pallas_call(
        arrange_kernel,
        out_shape=(jax.ShapeDtypeStruct((2 * share + EXTRA, width), green.dtype),) * (outer - 1),
        in_specs=[in_smem, in_vmem, in_vmem],
        out_specs=(in_vmem,) * (outer - 1),
        compiler_params=small,
        name="arrange",
    )(weight, green, got)
    received = [None] * (outer - 1)
    for k in range(outer - 1, 0, -1):
        route = [(z * 2 + x, partner(z, k, outer) * 2 + x) for z in range(outer) for x in range(2)]
        received[k - 1] = lax.ppermute(shares[k - 1], "energy", route)

    def kernel(*refs):
        count = outer - 1
        polar_kernel(refs[:count], *refs[count:count + 2], *refs[count + 5:])

    return pl.pallas_call(
        kernel,
        out_shape=jax.ShapeDtypeStruct((FREQS, share, width), jnp.float32),
        in_specs=[in_vmem] * (outer - 1) + [in_smem] * 5 + [in_vmem, in_vmem, in_place],
        out_specs=in_vmem,
        scratch_shapes=[
            VMEM((SHIFTS + energies, share, width), jnp.float32),
            VMEM((energies, share, width), jnp.float32),
            VMEM((share, width), jnp.float32),
            pltpu.SemaphoreType.DMA,
        ],
        compiler_params=small,
        name="polar",
    )(*received, weight, offsets, *scalars, green, got, bare)


def polar_share_plain(green, weight, offsets, bare, scalars):
    energies = lax.axis_size("energy")
    rows, width = green.shape
    share = rows // energies
    weights = lax.all_gather(weight, "energy", axis=0, tiled=True)
    parts = green.reshape(energies, share, width)
    parts = jnp.stack([parts[share_of(k)] for k in range(energies)]) if in_squares() else parts
    got = lax.all_to_all(parts, "energy", 0, 0, tiled=True)
    wide = got.astype(jnp.float32)
    weighted = wide * weights[:, None, None]
    padded = jnp.concatenate([jnp.zeros((SHIFTS,) + wide.shape[1:], wide.dtype), wide], axis=0)
    own = lax.dynamic_slice_in_dim(bare, share_of(lax.axis_index("energy")) * share, share, 0)
    factor = -(width ** -0.5) * energies ** -0.5
    chunks = []
    for f in range(FREQS):
        low = lax.dynamic_slice_in_dim(padded, SHIFTS - offsets[f], energies, 0)
        chunks.append(factor * own * jnp.sum(weighted * low, axis=0))
    return jnp.stack(chunks)


def gather_energy(chunk):
    outer = lax.axis_size("energy") // 2
    here = lax.axis_index("energy") // 2
    wholes = [
        lax.dynamic_update_index_in_dim(jnp.zeros((outer,) + part.shape, part.dtype), part, here, 0)
        for part in chunk
    ]
    for k in range(outer - 1, 0, -1):
        route = [(z * 2 + x, partner(z, k, outer) * 2 + x) for z in range(outer) for x in range(2)]
        got = lax.ppermute(chunk, "energy", route)
        wholes = [
            lax.dynamic_update_index_in_dim(whole, part, origin(here, k, outer), 0)
            for whole, part in zip(wholes, got)
        ]
    return wholes


def gather_square(parts):
    energies = lax.axis_size("energy")

    def along_x(part):
        return lax.ppermute(part, "energy", [(e, e ^ 1) for e in range(energies)])

    def along_rep(part):
        return lax.ppermute(part, "rep", [(0, 1), (1, 0)])

    beside = [along_x(part) for part in parts]
    above = [along_rep(part) for part in parts]
    apart = [along_rep(beside[0]), along_x(above[1])]
    return [*parts, *beside, *above, *apart]


def gathered(chunk):
    chunk = chunk.astype(coded)
    if in_squares():
        pieces = gather_square(gather_energy(chunk))
    else:
        pieces = [lax.all_gather(chunk, ("rep", "energy"), axis=1, tiled=True)]
    return [piece.astype(jnp.float32) for piece in pieces]


def parts_of(value):
    size = jnp.abs(value)
    exponent = jnp.where(size > 0.0, jnp.floor(jnp.log2(jnp.where(size > 0.0, size, 1.0))), 0.0)
    exponent = jnp.clip(exponent, -120.0, 120.0)
    mantissa = value * jnp.exp2(-exponent)
    first = mantissa.astype(jnp.bfloat16).astype(jnp.float32)
    second = (mantissa - first).astype(jnp.bfloat16).astype(jnp.float32)
    return exponent, first, second


def whole_of(exponent, first, second):
    return (first + second) * jnp.exp2(exponent)


def corner_start(place, block, rows):
    x, rep = lax.axis_index("energy") % 2, lax.axis_index("rep")
    at_x = 1 - x if place % 2 else x
    at_rep = 1 - rep if place >= 2 else rep
    return pl.multiple_of(at_rep * rows + at_x * block, block)


def early_kernel(pieces, bare_ref, once_ref, high, low):
    rows, width = bare_ref.shape
    if len(pieces) == 1:
        for f in range(FREQS):
            high[f], low[f] = halves(pieces[0][f])
    else:
        outer, share, _ = pieces[0].shape
        block = outer * share
        empty = jnp.zeros((block, width), jnp.bfloat16)
        for f in range(FREQS):
            for place in range(4):
                at = pl.ds(corner_start(place, block, rows), block)
                if place == 3:
                    high[f, at, :], low[f, at, :] = empty, empty
                else:
                    upper, lower = halves(pieces[place * FREQS + f][...].reshape(block, width))
                    high[f, at, :], low[f, at, :] = upper, lower
    bare = bare_ref[...]
    for f in range(FREQS):
        once_ref[f] = bare + product(bare, high[f], low[f])


def dyson_kernel(apart, early, offsets_ref, steps_ref, level_ref, bare_ref, hamiltonian_ref, two_ref,
                 four_ref, odd_ref, beside_refs, screened_ref, packed_ref, step_ref, own_ref,
                 high, low, made, hamiltonian_rows, made_sem, hamiltonian_sem):
    once_ref, high_ref, low_ref = early
    rows, width = bare_ref.shape
    entry_scale = width ** -0.5
    read = pltpu.make_async_copy(hamiltonian_ref, hamiltonian_rows, hamiltonian_sem)
    read.start()
    rep = lax.axis_index("rep")
    bare = bare_ref[...]
    once = [once_ref[f] for f in range(FREQS)]
    at = jnp.where(steps_ref[1] > steps_ref[0], 1, 0)
    high[...], low[...] = high_ref[at], low_ref[at]
    if apart:
        outer, share, _ = apart[0].shape
        block = outer * share
        start = corner_start(3, block, rows)
        beyond = bare_ref[:, pl.ds(start, block)]
        parts = [halves(ref[...].reshape(block, width)) for ref in apart]
        once = [once[f] + product(beyond, *parts[f]) for f in range(FREQS)]
        high[pl.ds(start, block), :] = jnp.where(at == 0, parts[0][0], parts[1][0])
        low[pl.ds(start, block), :] = jnp.where(at == 0, parts[0][1], parts[1][1])
    last = jnp.where(at == 0, once[0], once[1])
    upper, lower = high[...], low[...]
    twice = last + product(product(last, upper, lower), upper, lower)
    other = jnp.minimum(offsets_ref[0], offsets_ref[1])
    less = jnp.where(other == 2, two_ref[...], odd_ref[...])
    four = four_ref[...]
    energy_terms = jnp.zeros((rows, width), jnp.float32)
    for f in range(FREQS):
        count = steps_ref[f]
        value = jnp.where(count == 0, bare, jnp.where(count == 1, once[f], twice))
        value = value.astype(jnp.bfloat16)
        made[f] = value
        lowered = jnp.where(offsets_ref[f] == SHIFTS, four, less).astype(jnp.float32)
        energy_terms += lowered * value.astype(jnp.float32)
    write = pltpu.make_async_copy(made, screened_ref, made_sem)
    write.start()
    read.wait()
    beside = sum(ref[...].astype(jnp.float32) for ref in beside_refs)
    rest = hamiltonian_rows[...] - entry_scale * energy_terms - (0.5 * entry_scale) * beside
    col = lax.broadcasted_iota(jnp.int32, (rows, width), 1)
    row = lax.broadcasted_iota(jnp.int32, (rows, width), 0) + rep * rows
    off = jnp.where(col == row, 0.0, rest)
    first = rep == 0
    own = jnp.where(first, rest[:, :rows], rest[:, rows:])
    on = lax.broadcasted_iota(jnp.int32, (rows, rows), 0) == lax.broadcasted_iota(
        jnp.int32, (rows, rows), 1
    )
    diagonal = level_ref[0] + jnp.sum(jnp.where(on, own, 0.0), axis=1, keepdims=True)
    largest = jnp.max(jnp.max(jnp.abs(off), axis=0, keepdims=True), axis=1, keepdims=True)
    largest = jnp.where(largest > 0.0, largest, 1.0)
    unit = off * (1.0 / largest)
    inverse = 1.0 / diagonal
    factor = -largest * inverse
    step_ref[...] = unit * factor

    def in_own_columns(column):
        line = jnp.sum(jnp.where(on, column, 0.0), axis=0, keepdims=True)
        return jnp.concatenate([jnp.where(first, line, 0.0), jnp.where(first, 0.0, line)], axis=1)

    inverse_row = in_own_columns(inverse)
    factor_row = -largest * inverse_row
    blank = jnp.zeros((1, width), jnp.float32)
    packed_ref[:rows, :] = unit
    packed_ref[rows:, :] = jnp.concatenate(
        [*parts_of(factor_row), *parts_of(inverse_row), blank, blank], axis=0
    )
    own_ref[...] = jnp.concatenate([factor_row, inverse_row] + [blank] * 6, axis=0)
    write.wait()


def dyson_rows(pieces, offsets, steps, level, bare, hamiltonian, two, four, odd, beside):
    rows, width = bare.shape
    sides = len(beside)
    known, apart = (pieces, []) if len(pieces) == 1 else (pieces[:-FREQS], pieces[-FREQS:])
    count = len(known)

    def first_kernel(*refs):
        early_kernel(refs[:count], *refs[count:])

    early = pl.pallas_call(
        first_kernel,
        out_shape=(jax.ShapeDtypeStruct((FREQS, rows, width), jnp.float32),)
        + (jax.ShapeDtypeStruct((FREQS, width, width), jnp.bfloat16),) * 2,
        in_specs=[in_vmem] * (count + 1),
        out_specs=(in_vmem,) * 3,
        compiler_params=large,
        name="early",
    )(*known, bare)

    def kernel(*refs):
        far, rest = refs[:len(apart)], refs[len(apart):]
        done, rest = rest[:3], rest[3:]
        named, rest = rest[:8], rest[8:]
        dyson_kernel(far, done, *named, rest[:sides], *rest[sides:])

    return pl.pallas_call(
        kernel,
        out_shape=(
            jax.ShapeDtypeStruct((FREQS, rows, width), jnp.bfloat16),
            jax.ShapeDtypeStruct((rows + EXTRA, width), jnp.float32),
            jax.ShapeDtypeStruct((rows, width), jnp.float32),
            jax.ShapeDtypeStruct((EXTRA, width), jnp.float32),
        ),
        in_specs=[in_vmem] * (len(apart) + 3) + [in_smem] * 3 + [in_vmem, in_hbm]
        + [in_vmem] * (3 + sides),
        out_specs=(in_hbm,) + (in_vmem,) * 3,
        scratch_shapes=[VMEM((width, width), jnp.bfloat16)] * 2
        + [VMEM((FREQS, rows, width), jnp.bfloat16), VMEM((rows, width), jnp.float32)]
        + [pltpu.SemaphoreType.DMA] * 2,
        compiler_params=large,
        name="dyson",
    )(*apart, *early, offsets, steps, level, bare, held(hamiltonian), two, four, odd, *beside)


def columns(value, first):
    rows = value.shape[0]
    left, right = value[:, :rows], value[:, rows:]
    return jnp.where(first, left, right), jnp.where(first, right, left)


def begin_kernel(step_ref, packed_ref, own_ref, square_ref, high_ref, low_ref):
    rows, _ = step_ref.shape
    high, low = halves(packed_ref[:rows, :])
    high_ref[...], low_ref[...] = high, low
    near, _ = columns(step_ref[...] * own_ref[0:1], lax.axis_index("rep") == 0)
    square_ref[...] = product(near, high, low)


def finish_kernel(steps_ref, step_ref, square_ref, high_ref, low_ref, theirs_ref, own_ref, out_ref,
                  made, sems):
    rows, _ = step_ref.shape
    rep = lax.axis_index("rep")
    first = rep == 0
    tail = theirs_ref[rows:, :]
    factors = own_ref[0:1] + whole_of(tail[0:1], tail[1:2], tail[2:3])
    inverses = own_ref[1:2] + whole_of(tail[3:4], tail[4:5], tail[5:6])
    theirs = halves(theirs_ref[:rows, :])
    step = step_ref[...]
    _, far = columns(step * factors, first)
    square = square_ref[...] + product(far, *theirs)
    near, far = columns(square * factors, first)
    writes = []
    for half in range(2):
        at = slice(half * rows, (half + 1) * rows)
        cube = product(near, high_ref[:, at], low_ref[:, at]) + product(
            far, theirs[0][:, at], theirs[1][:, at]
        )
        col = lax.broadcasted_iota(jnp.int32, (rows, rows), 1) + half * rows
        row = lax.broadcasted_iota(jnp.int32, (rows, rows), 0) + rep * rows
        total = jnp.where(col == row, 1.0, step[:, at])
        total = total + jnp.where(steps_ref[0] >= 2, square[:, at] + cube, 0.0)
        made[:, at] = total * inverses[:, at]
        writes.append(pltpu.make_async_copy(made.at[:, at], out_ref.at[:, at], sems.at[half]))
        writes[-1].start()
    for write in writes:
        write.wait()


def body(
    green_blocks, occupation, offsets, coulomb, hamiltonian, onsite_level, green_steps, screen_steps
):
    green = green_blocks[0, 0]
    bare = coulomb[0]
    rows, width = green.shape
    share = rows // lax.axis_size("energy")
    make = polar_share if in_squares() and share % 16 == 0 else polar_share_plain
    scalars = (screen_steps, green_steps, onsite_level)
    pieces = gathered(make(green, occupation, offsets, bare, scalars))

    two = shifted(green, "energy", 2)
    four = shifted(two, "energy", 2)
    odd = shifted(chosen(offsets, two, green), "energy", 1)

    slabs = lax.axis_size("slab")
    if slabs == 2:
        beside = [lax.ppermute(green, "slab", [(0, 1), (1, 0)])]
    else:
        up = [(i, i + 1) for i in range(slabs - 1)]
        down = [(j, i) for i, j in up]
        beside = [lax.ppermute(green, "slab", up), lax.ppermute(green, "slab", down)]

    screened, packed, step, own = dyson_rows(
        pieces, offsets, screen_steps, onsite_level, bare, hamiltonian[0], two, four, odd, beside
    )
    theirs = lax.ppermute(packed.astype(coded), "rep", [(0, 1), (1, 0)]).astype(jnp.float32)
    wide = jax.ShapeDtypeStruct((rows, width), jnp.float32)
    thin = jax.ShapeDtypeStruct((rows, width), jnp.bfloat16)
    square, high, low = pl.pallas_call(
        begin_kernel,
        out_shape=(wide, thin, thin),
        in_specs=[in_vmem] * 3,
        out_specs=(in_vmem,) * 3,
        compiler_params=small,
        name="begin",
    )(step, packed, own)
    green_next = pl.pallas_call(
        finish_kernel,
        out_shape=wide,
        in_specs=[in_smem] + [in_vmem] * 6,
        out_specs=in_hbm,
        scratch_shapes=[VMEM((rows, width), jnp.float32), pltpu.SemaphoreType.DMA((2,))],
        compiler_params=large,
        name="finish",
    )(green_steps, step, square, high, low, theirs, own)
    return green_next[None, None], screened[:, None]


def chosen_kernel(offsets_ref, two_ref, green_ref, out_ref):
    three = jnp.minimum(offsets_ref[0], offsets_ref[1]) == 3

    @pl.when(three)
    def _():
        out_ref[...] = two_ref[...]

    @pl.when(jnp.logical_not(three))
    def _():
        out_ref[...] = green_ref[...]


def chosen(offsets, two, green):
    return pl.pallas_call(
        chosen_kernel,
        out_shape=jax.ShapeDtypeStruct(green.shape, green.dtype),
        in_specs=[in_smem, in_vmem, in_vmem],
        out_specs=in_vmem,
        compiler_params=small,
        name="chosen",
    )(offsets, two, green)


def solution(mesh):
    return jax.shard_map(
        body,
        mesh=mesh,
        in_specs=(
            P("energy", "slab", "rep", None),
            P("energy"),
            P(),
            P("slab", "rep", None),
            P("slab", "rep", None),
            P("energy"),
            P("energy"),
            P(),
        ),
        out_specs=(P("energy", "slab", "rep", None), P(None, "slab", "rep", None)),
        check_vma=False,
    )
```

```python
import jax
import jax.numpy as jnp
from jax import lax
from jax.experimental import pallas as pl
from jax.experimental.pallas import tpu as pltpu
from jax.sharding import PartitionSpec as P


SHIFTS = 4
FREQS = 2
EXTRA = 8

coded = jnp.float16
VMEM = pltpu.VMEM
in_vmem = pl.BlockSpec(memory_space=pltpu.VMEM)
in_smem = pl.BlockSpec(memory_space=pltpu.SMEM)
in_place = pl.BlockSpec(memory_space=pl.ANY)
in_hbm = pl.BlockSpec(memory_space=pltpu.HBM)
small = pltpu.CompilerParams(vmem_limit_bytes=6 << 20)
large = pltpu.CompilerParams(vmem_limit_bytes=16 << 20)


def held(value):
    return pltpu.with_memory_space_constraint(value, pltpu.HBM)


def halves(value):
    high = value.astype(jnp.bfloat16)
    return high, (value - high.astype(jnp.float32)).astype(jnp.bfloat16)


def dot(first, second):
    return jnp.dot(first, second, preferred_element_type=jnp.float32)


def product(first, high, low):
    top, rest = halves(first)
    return dot(top, high) + dot(top, low) + dot(rest, high)


def shifted(block, axis, distance):
    count = lax.axis_size(axis)
    route = [(i, i + distance) for i in range(count - distance)]
    return lax.ppermute(block, axis, route)


def partner(z, k, outer):
    return z ^ k if outer & (outer - 1) == 0 else (z + k) % outer


def origin(z, k, outer):
    return z ^ k if outer & (outer - 1) == 0 else (z + outer - k) % outer


def in_squares():
    energies = lax.axis_size("energy")
    return energies % 2 == 0 and energies <= 16 and lax.axis_size("rep") == 2


def share_of(place):
    outer = lax.axis_size("energy") // 2
    return place % 2 * outer + place // 2 if in_squares() else place


def weight_rows(weight, first_row, width):
    weight = jnp.full((EXTRA, width), weight, jnp.float32)
    first = weight.astype(jnp.bfloat16).astype(jnp.float32)
    second = (weight - first).astype(jnp.bfloat16).astype(jnp.float32)
    third = weight - first - second
    row = lax.broadcasted_iota(jnp.int32, (EXTRA, width), 0) - first_row
    later = jnp.where(row == 1, second, jnp.where(row == 2, third, 0.0))
    return jnp.where(row == 0, first, later)


def prepare_kernel(weight_ref, block_ref, out_ref, arrived):
    half, width = out_ref.shape[0] - EXTRA, out_ref.shape[1]
    x = lax.axis_index("energy") % 2
    start = pl.multiple_of((1 - x) * half, half)
    copy = pltpu.make_async_copy(
        block_ref.at[pl.ds(start, half), :], out_ref.at[pl.ds(0, half), :], arrived
    )
    copy.start()
    out_ref[half:, :] = weight_rows(weight_ref[0], 3, width).astype(out_ref.dtype)
    copy.wait()


def arrange_kernel(weight_ref, block_ref, got_ref, *out_refs):
    outer = len(out_refs) + 1
    half, width = got_ref.shape[0] - EXTRA, got_ref.shape[1]
    share = half // outer
    x, z = lax.axis_index("energy") % 2, lax.axis_index("energy") // 2
    tail = weight_rows(weight_ref[0], 0, width) + got_ref[half:, :].astype(jnp.float32)
    tail = tail.astype(got_ref.dtype)
    for k, out_ref in enumerate(out_refs, 1):
        at = partner(z, k, outer) * share
        mine = pl.ds(pl.multiple_of(x * half + at, share), share)
        out_ref[:share, :] = block_ref[mine, :]
        out_ref[share:2 * share, :] = got_ref[pl.ds(pl.multiple_of(at, share), share), :]
        out_ref[2 * share:, :] = tail


def polar_kernel(received, weight_ref, offsets_ref, block_ref, got_ref, bare_ref, out_ref,
                 padded, weighted, bare_rows, arrived):
    _, share, width = out_ref.shape
    energies = weighted.shape[0]
    outer = energies // 2
    half = outer * share
    energy = lax.axis_index("energy")
    x, z = energy % 2, energy // 2
    start = pl.multiple_of(x * half + z * share, share)
    copy = pltpu.make_async_copy(bare_ref.at[pl.ds(start, share), :], bare_rows, arrived)
    copy.start()
    padded[:SHIFTS] = jnp.zeros((SHIFTS, share, width), jnp.float32)

    def place(at, rows, weight):
        rows = rows.astype(jnp.float32)
        padded[SHIFTS + at] = rows
        weighted[at] = rows * weight

    def total(tail, row):
        return tail[row:row + 1] + tail[row + 1:row + 2] + tail[row + 2:row + 3]

    place(energy, block_ref[pl.ds(start, share), :], weight_ref[0])
    place(
        z * 2 + 1 - x,
        got_ref[pl.ds(pl.multiple_of(z * share, share), share), :],
        total(got_ref[half:, :].astype(jnp.float32), 3),
    )
    for k, ref in enumerate(received, 1):
        behind = origin(z, k, outer) * 2
        tail = ref[2 * share:, :].astype(jnp.float32)
        place(behind + x, ref[:share, :], total(tail, 0))
        place(behind + 1 - x, ref[share:2 * share, :], total(tail, 3))
    totals = [jnp.zeros((share, width), jnp.float32) for _ in range(FREQS)]
    for e in range(energies):
        own = weighted[e]
        for f in range(FREQS):
            totals[f] += own * padded[SHIFTS + e - offsets_ref[f]]
    copy.wait()
    factor = -(width ** -0.5) * energies ** -0.5
    for f in range(FREQS):
        out_ref[f] = totals[f] * (factor * bare_rows[...])


def polar_share(green, weight, offsets, bare, scalars):
    energies = lax.axis_size("energy")
    rows, width = green.shape
    outer = energies // 2
    share = rows // energies
    half = rows // 2
    sent = pl.pallas_call(
        prepare_kernel,
        out_shape=jax.ShapeDtypeStruct((half + EXTRA, width), green.dtype),
        in_specs=[in_smem, in_hbm],
        out_specs=in_vmem,
        scratch_shapes=[pltpu.SemaphoreType.DMA],
        compiler_params=small,
        name="prepare",
    )(weight, held(green))
    got = lax.ppermute(sent, "energy", [(e, e ^ 1) for e in range(energies)])
    shares = pl.pallas_call(
        arrange_kernel,
        out_shape=(jax.ShapeDtypeStruct((2 * share + EXTRA, width), green.dtype),) * (outer - 1),
        in_specs=[in_smem, in_vmem, in_vmem],
        out_specs=(in_vmem,) * (outer - 1),
        compiler_params=small,
        name="arrange",
    )(weight, green, got)
    received = [None] * (outer - 1)
    for k in range(outer - 1, 0, -1):
        route = [(z * 2 + x, partner(z, k, outer) * 2 + x) for z in range(outer) for x in range(2)]
        received[k - 1] = lax.ppermute(shares[k - 1], "energy", route)

    def kernel(*refs):
        count = outer - 1
        polar_kernel(refs[:count], *refs[count:count + 2], *refs[count + 5:])

    return pl.pallas_call(
        kernel,
        out_shape=jax.ShapeDtypeStruct((FREQS, share, width), jnp.float32),
        in_specs=[in_vmem] * (outer - 1) + [in_smem] * 5 + [in_vmem, in_vmem, in_place],
        out_specs=in_vmem,
        scratch_shapes=[
            VMEM((SHIFTS + energies, share, width), jnp.float32),
            VMEM((energies, share, width), jnp.float32),
            VMEM((share, width), jnp.float32),
            pltpu.SemaphoreType.DMA,
        ],
        compiler_params=small,
        name="polar",
    )(*received, weight, offsets, *scalars, green, got, bare)


def polar_share_plain(green, weight, offsets, bare, scalars):
    energies = lax.axis_size("energy")
    rows, width = green.shape
    share = rows // energies
    weights = lax.all_gather(weight, "energy", axis=0, tiled=True)
    parts = green.reshape(energies, share, width)
    parts = jnp.stack([parts[share_of(k)] for k in range(energies)]) if in_squares() else parts
    got = lax.all_to_all(parts, "energy", 0, 0, tiled=True)
    wide = got.astype(jnp.float32)
    weighted = wide * weights[:, None, None]
    padded = jnp.concatenate([jnp.zeros((SHIFTS,) + wide.shape[1:], wide.dtype), wide], axis=0)
    own = lax.dynamic_slice_in_dim(bare, share_of(lax.axis_index("energy")) * share, share, 0)
    factor = -(width ** -0.5) * energies ** -0.5
    chunks = []
    for f in range(FREQS):
        low = lax.dynamic_slice_in_dim(padded, SHIFTS - offsets[f], energies, 0)
        chunks.append(factor * own * jnp.sum(weighted * low, axis=0))
    return jnp.stack(chunks)


def gather_energy(chunk):
    outer = lax.axis_size("energy") // 2
    here = lax.axis_index("energy") // 2
    freqs, share, width = chunk.shape
    whole = jnp.zeros((freqs, outer, share, width), chunk.dtype)
    whole = lax.dynamic_update_slice_in_dim(whole, chunk[:, None], here, 1)
    for k in range(outer - 1, 0, -1):
        route = [(z * 2 + x, partner(z, k, outer) * 2 + x) for z in range(outer) for x in range(2)]
        got = lax.ppermute(chunk, "energy", route)
        whole = lax.dynamic_update_slice_in_dim(whole, got[:, None], origin(here, k, outer), 1)
    return whole


def gather_square(part):
    energies = lax.axis_size("energy")

    def along_x(part):
        return lax.ppermute(part, "energy", [(e, e ^ 1) for e in range(energies)])

    def along_rep(part):
        return lax.ppermute(part, "rep", [(0, 1), (1, 0)])

    beside = along_x(part)
    above = along_rep(part)
    apart = [along_rep(beside[0]), along_x(above[1])]
    return [*part, *beside, *above, *apart]


def gathered(chunk):
    chunk = chunk.astype(coded)
    if in_squares():
        pieces = gather_square(gather_energy(chunk))
    else:
        pieces = [lax.all_gather(chunk, ("rep", "energy"), axis=1, tiled=True)]
    return [piece.astype(jnp.float32) for piece in pieces]


def parts_of(value):
    size = jnp.abs(value)
    exponent = jnp.where(size > 0.0, jnp.floor(jnp.log2(jnp.where(size > 0.0, size, 1.0))), 0.0)
    exponent = jnp.clip(exponent, -120.0, 120.0)
    mantissa = value * jnp.exp2(-exponent)
    first = mantissa.astype(jnp.bfloat16).astype(jnp.float32)
    second = (mantissa - first).astype(jnp.bfloat16).astype(jnp.float32)
    return exponent, first, second


def whole_of(exponent, first, second):
    return (first + second) * jnp.exp2(exponent)


def corner_start(place, block, rows):
    x, rep = lax.axis_index("energy") % 2, lax.axis_index("rep")
    at_x = 1 - x if place % 2 else x
    at_rep = 1 - rep if place >= 2 else rep
    return pl.multiple_of(at_rep * rows + at_x * block, block)


def early_kernel(pieces, bare_ref, once_ref, high, low):
    rows, width = bare_ref.shape
    if len(pieces) == 1:
        for f in range(FREQS):
            high[f], low[f] = halves(pieces[0][f])
    else:
        outer, share, _ = pieces[0].shape
        block = outer * share
        empty = jnp.zeros((block, width), jnp.bfloat16)
        for f in range(FREQS):
            for place in range(4):
                at = pl.ds(corner_start(place, block, rows), block)
                if place == 3:
                    high[f, at, :], low[f, at, :] = empty, empty
                else:
                    upper, lower = halves(pieces[place * FREQS + f][...].reshape(block, width))
                    high[f, at, :], low[f, at, :] = upper, lower
    bare = bare_ref[...]
    for f in range(FREQS):
        once_ref[f] = bare + product(bare, high[f], low[f])


def dyson_kernel(apart, early, offsets_ref, steps_ref, level_ref, bare_ref, hamiltonian_ref, two_ref,
                 four_ref, odd_ref, beside_refs, screened_ref, packed_ref, step_ref, own_ref,
                 high, low, made, hamiltonian_rows, made_sem, hamiltonian_sem):
    once_ref, high_ref, low_ref = early
    rows, width = bare_ref.shape
    entry_scale = width ** -0.5
    read = pltpu.make_async_copy(hamiltonian_ref, hamiltonian_rows, hamiltonian_sem)
    read.start()
    rep = lax.axis_index("rep")
    bare = bare_ref[...]
    once = [once_ref[f] for f in range(FREQS)]
    at = jnp.where(steps_ref[1] > steps_ref[0], 1, 0)
    high[...], low[...] = high_ref[at], low_ref[at]
    if apart:
        outer, share, _ = apart[0].shape
        block = outer * share
        start = corner_start(3, block, rows)
        beyond = bare_ref[:, pl.ds(start, block)]
        parts = [halves(ref[...].reshape(block, width)) for ref in apart]
        once = [once[f] + product(beyond, *parts[f]) for f in range(FREQS)]
        high[pl.ds(start, block), :] = jnp.where(at == 0, parts[0][0], parts[1][0])
        low[pl.ds(start, block), :] = jnp.where(at == 0, parts[0][1], parts[1][1])
    last = jnp.where(at == 0, once[0], once[1])
    upper, lower = high[...], low[...]
    twice = last + product(product(last, upper, lower), upper, lower)
    other = jnp.minimum(offsets_ref[0], offsets_ref[1])
    less = jnp.where(other == 2, two_ref[...], odd_ref[...])
    four = four_ref[...]
    energy_terms = jnp.zeros((rows, width), jnp.float32)
    for f in range(FREQS):
        count = steps_ref[f]
        value = jnp.where(count == 0, bare, jnp.where(count == 1, once[f], twice))
        value = value.astype(jnp.bfloat16)
        made[f] = value
        lowered = jnp.where(offsets_ref[f] == SHIFTS, four, less).astype(jnp.float32)
        energy_terms += lowered * value.astype(jnp.float32)
    write = pltpu.make_async_copy(made, screened_ref, made_sem)
    write.start()
    read.wait()
    beside = sum(ref[...].astype(jnp.float32) for ref in beside_refs)
    rest = hamiltonian_rows[...] - entry_scale * energy_terms - (0.5 * entry_scale) * beside
    col = lax.broadcasted_iota(jnp.int32, (rows, width), 1)
    row = lax.broadcasted_iota(jnp.int32, (rows, width), 0) + rep * rows
    on = col == row
    diagonal = level_ref[0] + jnp.sum(jnp.where(on, rest, 0.0), axis=1, keepdims=True)
    off = jnp.where(on, 0.0, rest)
    largest = jnp.max(jnp.abs(off), axis=1, keepdims=True)
    largest = jnp.where(largest > 0.0, largest, 1.0)
    unit = off * (1.0 / largest)
    inverse = 1.0 / diagonal
    factor = -largest * inverse
    step_ref[...] = unit * factor
    factor_row = jnp.sum(jnp.where(on, factor, 0.0), axis=0, keepdims=True)
    inverse_row = jnp.sum(jnp.where(on, inverse, 0.0), axis=0, keepdims=True)
    blank = jnp.zeros((1, width), jnp.float32)
    packed_ref[:rows, :] = unit
    packed_ref[rows:, :] = jnp.concatenate(
        [*parts_of(factor_row), *parts_of(inverse_row), blank, blank], axis=0
    )
    own_ref[...] = jnp.concatenate([factor_row, inverse_row] + [blank] * 6, axis=0)
    write.wait()


def dyson_rows(pieces, offsets, steps, level, bare, hamiltonian, two, four, odd, beside):
    rows, width = bare.shape
    sides = len(beside)
    known, apart = (pieces, []) if len(pieces) == 1 else (pieces[:-FREQS], pieces[-FREQS:])
    count = len(known)

    def first_kernel(*refs):
        early_kernel(refs[:count], *refs[count:])

    early = pl.pallas_call(
        first_kernel,
        out_shape=(jax.ShapeDtypeStruct((FREQS, rows, width), jnp.float32),)
        + (jax.ShapeDtypeStruct((FREQS, width, width), jnp.bfloat16),) * 2,
        in_specs=[in_vmem] * (count + 1),
        out_specs=(in_vmem,) * 3,
        compiler_params=large,
        name="early",
    )(*known, bare)

    def kernel(*refs):
        far, rest = refs[:len(apart)], refs[len(apart):]
        done, rest = rest[:3], rest[3:]
        named, rest = rest[:8], rest[8:]
        dyson_kernel(far, done, *named, rest[:sides], *rest[sides:])

    return pl.pallas_call(
        kernel,
        out_shape=(
            jax.ShapeDtypeStruct((FREQS, rows, width), jnp.bfloat16),
            jax.ShapeDtypeStruct((rows + EXTRA, width), jnp.float32),
            jax.ShapeDtypeStruct((rows, width), jnp.float32),
            jax.ShapeDtypeStruct((EXTRA, width), jnp.float32),
        ),
        in_specs=[in_vmem] * (len(apart) + 3) + [in_smem] * 3 + [in_vmem, in_hbm]
        + [in_vmem] * (3 + sides),
        out_specs=(in_hbm,) + (in_vmem,) * 3,
        scratch_shapes=[VMEM((width, width), jnp.bfloat16)] * 2
        + [VMEM((FREQS, rows, width), jnp.bfloat16), VMEM((rows, width), jnp.float32)]
        + [pltpu.SemaphoreType.DMA] * 2,
        compiler_params=large,
        name="dyson",
    )(*apart, *early, offsets, steps, level, bare, held(hamiltonian), two, four, odd, *beside)


def columns(value, first):
    rows = value.shape[0]
    left, right = value[:, :rows], value[:, rows:]
    return jnp.where(first, left, right), jnp.where(first, right, left)


def begin_kernel(step_ref, packed_ref, own_ref, square_ref, high_ref, low_ref):
    rows, _ = step_ref.shape
    high, low = halves(packed_ref[:rows, :])
    high_ref[...], low_ref[...] = high, low
    near, _ = columns(step_ref[...] * own_ref[0:1], lax.axis_index("rep") == 0)
    square_ref[...] = product(near, high, low)


def finish_kernel(steps_ref, step_ref, square_ref, high_ref, low_ref, theirs_ref, own_ref, out_ref,
                  made, sems):
    rows, _ = step_ref.shape
    rep = lax.axis_index("rep")
    first = rep == 0
    tail = theirs_ref[rows:, :]
    factors = own_ref[0:1] + whole_of(tail[0:1], tail[1:2], tail[2:3])
    inverses = own_ref[1:2] + whole_of(tail[3:4], tail[4:5], tail[5:6])
    theirs = halves(theirs_ref[:rows, :])
    step = step_ref[...]
    _, far = columns(step * factors, first)
    square = square_ref[...] + product(far, *theirs)
    near, far = columns(square * factors, first)
    writes = []
    for half in range(2):
        at = slice(half * rows, (half + 1) * rows)
        cube = product(near, high_ref[:, at], low_ref[:, at]) + product(
            far, theirs[0][:, at], theirs[1][:, at]
        )
        col = lax.broadcasted_iota(jnp.int32, (rows, rows), 1) + half * rows
        row = lax.broadcasted_iota(jnp.int32, (rows, rows), 0) + rep * rows
        total = jnp.where(col == row, 1.0, step[:, at])
        total = total + jnp.where(steps_ref[0] >= 2, square[:, at] + cube, 0.0)
        made[:, at] = total * inverses[:, at]
        writes.append(pltpu.make_async_copy(made.at[:, at], out_ref.at[:, at], sems.at[half]))
        writes[-1].start()
    for write in writes:
        write.wait()


def body(
    green_blocks, occupation, offsets, coulomb, hamiltonian, onsite_level, green_steps, screen_steps
):
    green = green_blocks[0, 0]
    bare = coulomb[0]
    rows, width = green.shape
    share = rows // lax.axis_size("energy")
    make = polar_share if in_squares() and share % 16 == 0 else polar_share_plain
    scalars = (screen_steps, green_steps, onsite_level)
    pieces = gathered(make(green, occupation, offsets, bare, scalars))

    two = shifted(green, "energy", 2)
    four = shifted(two, "energy", 2)
    odd = shifted(chosen(offsets, two, green), "energy", 1)

    slabs = lax.axis_size("slab")
    if slabs == 2:
        beside = [lax.ppermute(green, "slab", [(0, 1), (1, 0)])]
    else:
        up = [(i, i + 1) for i in range(slabs - 1)]
        down = [(j, i) for i, j in up]
        beside = [lax.ppermute(green, "slab", up), lax.ppermute(green, "slab", down)]

    screened, packed, step, own = dyson_rows(
        pieces, offsets, screen_steps, onsite_level, bare, hamiltonian[0], two, four, odd, beside
    )
    theirs = lax.ppermute(packed.astype(coded), "rep", [(0, 1), (1, 0)]).astype(jnp.float32)
    wide = jax.ShapeDtypeStruct((rows, width), jnp.float32)
    thin = jax.ShapeDtypeStruct((rows, width), jnp.bfloat16)
    square, high, low = pl.pallas_call(
        begin_kernel,
        out_shape=(wide, thin, thin),
        in_specs=[in_vmem] * 3,
        out_specs=(in_vmem,) * 3,
        compiler_params=small,
        name="begin",
    )(step, packed, own)
    green_next = pl.pallas_call(
        finish_kernel,
        out_shape=wide,
        in_specs=[in_smem] + [in_vmem] * 6,
        out_specs=in_hbm,
        scratch_shapes=[VMEM((rows, width), jnp.float32), pltpu.SemaphoreType.DMA((2,))],
        compiler_params=large,
        name="finish",
    )(green_steps, step, square, high, low, theirs, own)
    return green_next[None, None], screened[:, None]


def chosen_kernel(offsets_ref, two_ref, green_ref, out_ref):
    three = jnp.minimum(offsets_ref[0], offsets_ref[1]) == 3

    @pl.when(three)
    def _():
        out_ref[...] = two_ref[...]

    @pl.when(jnp.logical_not(three))
    def _():
        out_ref[...] = green_ref[...]


def chosen(offsets, two, green):
    return pl.pallas_call(
        chosen_kernel,
        out_shape=jax.ShapeDtypeStruct(green.shape, green.dtype),
        in_specs=[in_smem, in_vmem, in_vmem],
        out_specs=in_vmem,
        compiler_params=small,
        name="chosen",
    )(offsets, two, green)


def solution(mesh):
    return jax.shard_map(
        body,
        mesh=mesh,
        in_specs=(
            P("energy", "slab", "rep", None),
            P("energy"),
            P(),
            P("slab", "rep", None),
            P("slab", "rep", None),
            P("energy"),
            P("energy"),
            P(),
        ),
        out_specs=(P("energy", "slab", "rep", None), P(None, "slab", "rep", None)),
        check_vma=False,
    )
```

```python
import jax
import jax.numpy as jnp
from jax import lax
from jax.experimental import pallas as pl
from jax.experimental.pallas import tpu as pltpu
from jax.sharding import PartitionSpec as P


SHIFTS = 4
FREQS = 2
EXTRA = 8

coded = jnp.float16
VMEM = pltpu.VMEM
in_vmem = pl.BlockSpec(memory_space=pltpu.VMEM)
in_smem = pl.BlockSpec(memory_space=pltpu.SMEM)
in_place = pl.BlockSpec(memory_space=pl.ANY)
in_hbm = pl.BlockSpec(memory_space=pltpu.HBM)
small = pltpu.CompilerParams(vmem_limit_bytes=6 << 20)
large = pltpu.CompilerParams(vmem_limit_bytes=16 << 20)


def held(value):
    return pltpu.with_memory_space_constraint(value, pltpu.HBM)


def halves(value):
    high = value.astype(jnp.bfloat16)
    return high, (value - high.astype(jnp.float32)).astype(jnp.bfloat16)


def dot(first, second):
    return jnp.dot(first, second, preferred_element_type=jnp.float32)


def product(first, high, low):
    top, rest = halves(first)
    return dot(top, high) + dot(top, low) + dot(rest, high)


def shifted(block, axis, distance):
    count = lax.axis_size(axis)
    route = [(i, i + distance) for i in range(count - distance)]
    return lax.ppermute(block, axis, route)


def partner(z, k, outer):
    return z ^ k if outer & (outer - 1) == 0 else (z + k) % outer


def origin(z, k, outer):
    return z ^ k if outer & (outer - 1) == 0 else (z + outer - k) % outer


def in_squares():
    energies = lax.axis_size("energy")
    return energies % 2 == 0 and energies <= 16 and lax.axis_size("rep") == 2


def share_of(place):
    outer = lax.axis_size("energy") // 2
    return place % 2 * outer + place // 2 if in_squares() else place


def weight_rows(weight, first_row, width):
    weight = jnp.full((EXTRA, width), weight, jnp.float32)
    first = weight.astype(jnp.bfloat16).astype(jnp.float32)
    second = (weight - first).astype(jnp.bfloat16).astype(jnp.float32)
    third = weight - first - second
    row = lax.broadcasted_iota(jnp.int32, (EXTRA, width), 0) - first_row
    later = jnp.where(row == 1, second, jnp.where(row == 2, third, 0.0))
    return jnp.where(row == 0, first, later)


def prepare_kernel(weight_ref, block_ref, out_ref, arrived):
    half, width = out_ref.shape[0] - EXTRA, out_ref.shape[1]
    x = lax.axis_index("energy") % 2
    start = pl.multiple_of((1 - x) * half, half)
    copy = pltpu.make_async_copy(
        block_ref.at[pl.ds(start, half), :], out_ref.at[pl.ds(0, half), :], arrived
    )
    copy.start()
    out_ref[half:, :] = weight_rows(weight_ref[0], 3, width).astype(out_ref.dtype)
    copy.wait()


def arrange_kernel(weight_ref, block_ref, got_ref, *out_refs):
    outer = len(out_refs) + 1
    half, width = got_ref.shape[0] - EXTRA, got_ref.shape[1]
    share = half // outer
    x, z = lax.axis_index("energy") % 2, lax.axis_index("energy") // 2
    tail = weight_rows(weight_ref[0], 0, width) + got_ref[half:, :].astype(jnp.float32)
    tail = tail.astype(got_ref.dtype)
    for k, out_ref in enumerate(out_refs, 1):
        at = partner(z, k, outer) * share
        mine = pl.ds(pl.multiple_of(x * half + at, share), share)
        out_ref[:share, :] = block_ref[mine, :]
        out_ref[share:2 * share, :] = got_ref[pl.ds(pl.multiple_of(at, share), share), :]
        out_ref[2 * share:, :] = tail


def polar_kernel(received, weight_ref, offsets_ref, block_ref, got_ref, bare_ref, out_ref,
                 padded, weighted, bare_rows, arrived):
    _, share, width = out_ref.shape
    energies = weighted.shape[0]
    outer = energies // 2
    half = outer * share
    energy = lax.axis_index("energy")
    x, z = energy % 2, energy // 2
    start = pl.multiple_of(x * half + z * share, share)
    copy = pltpu.make_async_copy(bare_ref.at[pl.ds(start, share), :], bare_rows, arrived)
    copy.start()
    padded[:SHIFTS] = jnp.zeros((SHIFTS, share, width), jnp.float32)

    def place(at, rows, weight):
        rows = rows.astype(jnp.float32)
        padded[SHIFTS + at] = rows
        weighted[at] = rows * weight

    def total(tail, row):
        return tail[row:row + 1] + tail[row + 1:row + 2] + tail[row + 2:row + 3]

    place(energy, block_ref[pl.ds(start, share), :], weight_ref[0])
    place(
        z * 2 + 1 - x,
        got_ref[pl.ds(pl.multiple_of(z * share, share), share), :],
        total(got_ref[half:, :].astype(jnp.float32), 3),
    )
    for k, ref in enumerate(received, 1):
        behind = origin(z, k, outer) * 2
        tail = ref[2 * share:, :].astype(jnp.float32)
        place(behind + x, ref[:share, :], total(tail, 0))
        place(behind + 1 - x, ref[share:2 * share, :], total(tail, 3))
    totals = [jnp.zeros((share, width), jnp.float32) for _ in range(FREQS)]
    for e in range(energies):
        own = weighted[e]
        for f in range(FREQS):
            totals[f] += own * padded[SHIFTS + e - offsets_ref[f]]
    copy.wait()
    factor = -(width ** -0.5) * energies ** -0.5
    for f in range(FREQS):
        out_ref[f] = totals[f] * (factor * bare_rows[...])


def polar_share(green, weight, offsets, bare, scalars):
    energies = lax.axis_size("energy")
    rows, width = green.shape
    outer = energies // 2
    share = rows // energies
    half = rows // 2
    sent = pl.pallas_call(
        prepare_kernel,
        out_shape=jax.ShapeDtypeStruct((half + EXTRA, width), green.dtype),
        in_specs=[in_smem, in_hbm],
        out_specs=in_vmem,
        scratch_shapes=[pltpu.SemaphoreType.DMA],
        compiler_params=small,
        name="prepare",
    )(weight, held(green))
    got = lax.ppermute(sent, "energy", [(e, e ^ 1) for e in range(energies)])
    shares = pl.pallas_call(
        arrange_kernel,
        out_shape=(jax.ShapeDtypeStruct((2 * share + EXTRA, width), green.dtype),) * (outer - 1),
        in_specs=[in_smem, in_vmem, in_vmem],
        out_specs=(in_vmem,) * (outer - 1),
        compiler_params=small,
        name="arrange",
    )(weight, green, got)
    received = [None] * (outer - 1)
    for k in range(outer - 1, 0, -1):
        route = [(z * 2 + x, partner(z, k, outer) * 2 + x) for z in range(outer) for x in range(2)]
        received[k - 1] = lax.ppermute(shares[k - 1], "energy", route)

    def kernel(*refs):
        count = outer - 1
        polar_kernel(refs[:count], *refs[count:count + 2], *refs[count + 5:])

    return pl.pallas_call(
        kernel,
        out_shape=jax.ShapeDtypeStruct((FREQS, share, width), jnp.float32),
        in_specs=[in_vmem] * (outer - 1) + [in_smem] * 5 + [in_vmem, in_vmem, in_place],
        out_specs=in_vmem,
        scratch_shapes=[
            VMEM((SHIFTS + energies, share, width), jnp.float32),
            VMEM((energies, share, width), jnp.float32),
            VMEM((share, width), jnp.float32),
            pltpu.SemaphoreType.DMA,
        ],
        compiler_params=small,
        name="polar",
    )(*received, weight, offsets, *scalars, green, got, bare)


def polar_share_plain(green, weight, offsets, bare, scalars):
    energies = lax.axis_size("energy")
    rows, width = green.shape
    share = rows // energies
    weights = lax.all_gather(weight, "energy", axis=0, tiled=True)
    parts = green.reshape(energies, share, width)
    parts = jnp.stack([parts[share_of(k)] for k in range(energies)]) if in_squares() else parts
    got = lax.all_to_all(parts, "energy", 0, 0, tiled=True)
    wide = got.astype(jnp.float32)
    weighted = wide * weights[:, None, None]
    padded = jnp.concatenate([jnp.zeros((SHIFTS,) + wide.shape[1:], wide.dtype), wide], axis=0)
    own = lax.dynamic_slice_in_dim(bare, share_of(lax.axis_index("energy")) * share, share, 0)
    factor = -(width ** -0.5) * energies ** -0.5
    chunks = []
    for f in range(FREQS):
        low = lax.dynamic_slice_in_dim(padded, SHIFTS - offsets[f], energies, 0)
        chunks.append(factor * own * jnp.sum(weighted * low, axis=0))
    return jnp.stack(chunks)


def gather_energy(chunk):
    outer = lax.axis_size("energy") // 2
    here = lax.axis_index("energy") // 2
    wholes = [
        lax.dynamic_update_index_in_dim(jnp.zeros((outer,) + part.shape, part.dtype), part, here, 0)
        for part in chunk
    ]
    for k in range(outer - 1, 0, -1):
        route = [(z * 2 + x, partner(z, k, outer) * 2 + x) for z in range(outer) for x in range(2)]
        got = lax.ppermute(chunk, "energy", route)
        wholes = [
            lax.dynamic_update_index_in_dim(whole, part, origin(here, k, outer), 0)
            for whole, part in zip(wholes, got)
        ]
    return wholes


def gather_square(parts):
    energies = lax.axis_size("energy")

    def along_x(part):
        return lax.ppermute(part, "energy", [(e, e ^ 1) for e in range(energies)])

    def along_rep(part):
        return lax.ppermute(part, "rep", [(0, 1), (1, 0)])

    beside = [along_x(part) for part in parts]
    above = [along_rep(part) for part in parts]
    apart = [along_rep(part) for part in beside]
    return [*parts, *beside, *above, *apart]


def gathered(chunk):
    chunk = chunk.astype(coded)
    if in_squares():
        pieces = gather_square(gather_energy(chunk))
    else:
        pieces = [lax.all_gather(chunk, ("rep", "energy"), axis=1, tiled=True)]
    return [piece.astype(jnp.float32) for piece in pieces]


def parts_of(value):
    size = jnp.abs(value)
    exponent = jnp.where(size > 0.0, jnp.floor(jnp.log2(jnp.where(size > 0.0, size, 1.0))), 0.0)
    exponent = jnp.clip(exponent, -120.0, 120.0)
    mantissa = value * jnp.exp2(-exponent)
    first = mantissa.astype(jnp.bfloat16).astype(jnp.float32)
    second = (mantissa - first).astype(jnp.bfloat16).astype(jnp.float32)
    return exponent, first, second


def whole_of(exponent, first, second):
    return (first + second) * jnp.exp2(exponent)


def corner_start(place, block, rows):
    x, rep = lax.axis_index("energy") % 2, lax.axis_index("rep")
    at_x = 1 - x if place % 2 else x
    at_rep = 1 - rep if place >= 2 else rep
    return pl.multiple_of(at_rep * rows + at_x * block, block)


def early_kernel(pieces, bare_ref, once_ref, high, low):
    rows, width = bare_ref.shape
    if len(pieces) == 1:
        for f in range(FREQS):
            high[f], low[f] = halves(pieces[0][f])
    else:
        outer, share, _ = pieces[0].shape
        block = outer * share
        empty = jnp.zeros((block, width), jnp.bfloat16)
        for f in range(FREQS):
            for place in range(4):
                at = pl.ds(corner_start(place, block, rows), block)
                if place == 3:
                    high[f, at, :], low[f, at, :] = empty, empty
                else:
                    upper, lower = halves(pieces[place * FREQS + f][...].reshape(block, width))
                    high[f, at, :], low[f, at, :] = upper, lower
    bare = bare_ref[...]
    for f in range(FREQS):
        once_ref[f] = bare + product(bare, high[f], low[f])


def dyson_kernel(apart, early, offsets_ref, steps_ref, level_ref, bare_ref, hamiltonian_ref, two_ref,
                 four_ref, odd_ref, beside_refs, screened_ref, packed_ref, step_ref, own_ref,
                 high, low, made, hamiltonian_rows, made_sem, hamiltonian_sem):
    once_ref, high_ref, low_ref = early
    rows, width = bare_ref.shape
    entry_scale = width ** -0.5
    read = pltpu.make_async_copy(hamiltonian_ref, hamiltonian_rows, hamiltonian_sem)
    read.start()
    rep = lax.axis_index("rep")
    bare = bare_ref[...]
    once = [once_ref[f] for f in range(FREQS)]
    at = jnp.where(steps_ref[1] > steps_ref[0], 1, 0)
    high[...], low[...] = high_ref[at], low_ref[at]
    if apart:
        outer, share, _ = apart[0].shape
        block = outer * share
        start = corner_start(3, block, rows)
        beyond = bare_ref[:, pl.ds(start, block)]
        parts = [halves(ref[...].reshape(block, width)) for ref in apart]
        once = [once[f] + product(beyond, *parts[f]) for f in range(FREQS)]
        high[pl.ds(start, block), :] = jnp.where(at == 0, parts[0][0], parts[1][0])
        low[pl.ds(start, block), :] = jnp.where(at == 0, parts[0][1], parts[1][1])
    last = jnp.where(at == 0, once[0], once[1])
    upper, lower = high[...], low[...]
    twice = last + product(product(last, upper, lower), upper, lower)
    other = jnp.minimum(offsets_ref[0], offsets_ref[1])
    less = jnp.where(other == 2, two_ref[...], odd_ref[...])
    four = four_ref[...]
    energy_terms = jnp.zeros((rows, width), jnp.float32)
    for f in range(FREQS):
        count = steps_ref[f]
        value = jnp.where(count == 0, bare, jnp.where(count == 1, once[f], twice))
        value = value.astype(jnp.bfloat16)
        made[f] = value
        lowered = jnp.where(offsets_ref[f] == SHIFTS, four, less).astype(jnp.float32)
        energy_terms += lowered * value.astype(jnp.float32)
    write = pltpu.make_async_copy(made, screened_ref, made_sem)
    write.start()
    read.wait()
    beside = sum(ref[...].astype(jnp.float32) for ref in beside_refs)
    rest = hamiltonian_rows[...] - entry_scale * energy_terms - (0.5 * entry_scale) * beside
    col = lax.broadcasted_iota(jnp.int32, (rows, width), 1)
    row = lax.broadcasted_iota(jnp.int32, (rows, width), 0) + rep * rows
    on = col == row
    diagonal = level_ref[0] + jnp.sum(jnp.where(on, rest, 0.0), axis=1, keepdims=True)
    off = jnp.where(on, 0.0, rest)
    largest = jnp.max(jnp.abs(off), axis=1, keepdims=True)
    largest = jnp.where(largest > 0.0, largest, 1.0)
    unit = off * (1.0 / largest)
    inverse = 1.0 / diagonal
    factor = -largest * inverse
    step_ref[...] = unit * factor
    factor_row = jnp.sum(jnp.where(on, factor, 0.0), axis=0, keepdims=True)
    inverse_row = jnp.sum(jnp.where(on, inverse, 0.0), axis=0, keepdims=True)
    blank = jnp.zeros((1, width), jnp.float32)
    packed_ref[:rows, :] = unit
    packed_ref[rows:, :] = jnp.concatenate(
        [*parts_of(factor_row), *parts_of(inverse_row), blank, blank], axis=0
    )
    own_ref[...] = jnp.concatenate([factor_row, inverse_row] + [blank] * 6, axis=0)
    write.wait()


def dyson_rows(pieces, offsets, steps, level, bare, hamiltonian, two, four, odd, beside):
    rows, width = bare.shape
    sides = len(beside)
    known, apart = (pieces, []) if len(pieces) == 1 else (pieces[:-FREQS], pieces[-FREQS:])
    count = len(known)

    def first_kernel(*refs):
        early_kernel(refs[:count], *refs[count:])

    early = pl.pallas_call(
        first_kernel,
        out_shape=(jax.ShapeDtypeStruct((FREQS, rows, width), jnp.float32),)
        + (jax.ShapeDtypeStruct((FREQS, width, width), jnp.bfloat16),) * 2,
        in_specs=[in_vmem] * (count + 1),
        out_specs=(in_vmem,) * 3,
        compiler_params=large,
        name="early",
    )(*known, bare)

    def kernel(*refs):
        far, rest = refs[:len(apart)], refs[len(apart):]
        done, rest = rest[:3], rest[3:]
        named, rest = rest[:8], rest[8:]
        dyson_kernel(far, done, *named, rest[:sides], *rest[sides:])

    return pl.pallas_call(
        kernel,
        out_shape=(
            jax.ShapeDtypeStruct((FREQS, rows, width), jnp.bfloat16),
            jax.ShapeDtypeStruct((rows + EXTRA, width), jnp.float32),
            jax.ShapeDtypeStruct((rows, width), jnp.float32),
            jax.ShapeDtypeStruct((EXTRA, width), jnp.float32),
        ),
        in_specs=[in_vmem] * (len(apart) + 3) + [in_smem] * 3 + [in_vmem, in_hbm]
        + [in_vmem] * (3 + sides),
        out_specs=(in_hbm,) + (in_vmem,) * 3,
        scratch_shapes=[VMEM((width, width), jnp.bfloat16)] * 2
        + [VMEM((FREQS, rows, width), jnp.bfloat16), VMEM((rows, width), jnp.float32)]
        + [pltpu.SemaphoreType.DMA] * 2,
        compiler_params=large,
        name="dyson",
    )(*apart, *early, offsets, steps, level, bare, held(hamiltonian), two, four, odd, *beside)


def columns(value, first):
    rows = value.shape[0]
    left, right = value[:, :rows], value[:, rows:]
    return jnp.where(first, left, right), jnp.where(first, right, left)


def begin_kernel(step_ref, packed_ref, own_ref, square_ref, high_ref, low_ref):
    rows, _ = step_ref.shape
    high, low = halves(packed_ref[:rows, :])
    high_ref[...], low_ref[...] = high, low
    near, _ = columns(step_ref[...] * own_ref[0:1], lax.axis_index("rep") == 0)
    square_ref[...] = product(near, high, low)


def finish_kernel(steps_ref, step_ref, square_ref, high_ref, low_ref, theirs_ref, own_ref, out_ref,
                  made, sems):
    rows, _ = step_ref.shape
    rep = lax.axis_index("rep")
    first = rep == 0
    tail = theirs_ref[rows:, :]
    factors = own_ref[0:1] + whole_of(tail[0:1], tail[1:2], tail[2:3])
    inverses = own_ref[1:2] + whole_of(tail[3:4], tail[4:5], tail[5:6])
    theirs = halves(theirs_ref[:rows, :])
    step = step_ref[...]
    _, far = columns(step * factors, first)
    square = square_ref[...] + product(far, *theirs)
    near, far = columns(square * factors, first)
    writes = []
    for half in range(2):
        at = slice(half * rows, (half + 1) * rows)
        cube = product(near, high_ref[:, at], low_ref[:, at]) + product(
            far, theirs[0][:, at], theirs[1][:, at]
        )
        col = lax.broadcasted_iota(jnp.int32, (rows, rows), 1) + half * rows
        row = lax.broadcasted_iota(jnp.int32, (rows, rows), 0) + rep * rows
        total = jnp.where(col == row, 1.0, step[:, at])
        total = total + jnp.where(steps_ref[0] >= 2, square[:, at] + cube, 0.0)
        made[:, at] = total * inverses[:, at]
        writes.append(pltpu.make_async_copy(made.at[:, at], out_ref.at[:, at], sems.at[half]))
        writes[-1].start()
    for write in writes:
        write.wait()


def body(
    green_blocks, occupation, offsets, coulomb, hamiltonian, onsite_level, green_steps, screen_steps
):
    green = green_blocks[0, 0]
    bare = coulomb[0]
    rows, width = green.shape
    share = rows // lax.axis_size("energy")
    make = polar_share if in_squares() and share % 16 == 0 else polar_share_plain
    scalars = (screen_steps, green_steps, onsite_level)
    pieces = gathered(make(green, occupation, offsets, bare, scalars))

    two = shifted(green, "energy", 2)
    four = shifted(two, "energy", 2)
    odd = shifted(chosen(offsets, two, green), "energy", 1)

    slabs = lax.axis_size("slab")
    if slabs == 2:
        beside = [lax.ppermute(green, "slab", [(0, 1), (1, 0)])]
    else:
        up = [(i, i + 1) for i in range(slabs - 1)]
        down = [(j, i) for i, j in up]
        beside = [lax.ppermute(green, "slab", up), lax.ppermute(green, "slab", down)]

    screened, packed, step, own = dyson_rows(
        pieces, offsets, screen_steps, onsite_level, bare, hamiltonian[0], two, four, odd, beside
    )
    theirs = lax.ppermute(packed.astype(coded), "rep", [(0, 1), (1, 0)]).astype(jnp.float32)
    wide = jax.ShapeDtypeStruct((rows, width), jnp.float32)
    thin = jax.ShapeDtypeStruct((rows, width), jnp.bfloat16)
    square, high, low = pl.pallas_call(
        begin_kernel,
        out_shape=(wide, thin, thin),
        in_specs=[in_vmem] * 3,
        out_specs=(in_vmem,) * 3,
        compiler_params=small,
        name="begin",
    )(step, packed, own)
    green_next = pl.pallas_call(
        finish_kernel,
        out_shape=wide,
        in_specs=[in_smem] + [in_vmem] * 6,
        out_specs=in_hbm,
        scratch_shapes=[VMEM((rows, width), jnp.float32), pltpu.SemaphoreType.DMA((2,))],
        compiler_params=large,
        name="finish",
    )(green_steps, step, square, high, low, theirs, own)
    return green_next[None, None], screened[:, None]


def chosen_kernel(offsets_ref, two_ref, green_ref, out_ref):
    three = jnp.minimum(offsets_ref[0], offsets_ref[1]) == 3

    @pl.when(three)
    def _():
        out_ref[...] = two_ref[...]

    @pl.when(jnp.logical_not(three))
    def _():
        out_ref[...] = green_ref[...]


def chosen(offsets, two, green):
    return pl.pallas_call(
        chosen_kernel,
        out_shape=jax.ShapeDtypeStruct(green.shape, green.dtype),
        in_specs=[in_smem, in_vmem, in_vmem],
        out_specs=in_vmem,
        compiler_params=small,
        name="chosen",
    )(offsets, two, green)


def solution(mesh):
    return jax.shard_map(
        body,
        mesh=mesh,
        in_specs=(
            P("energy", "slab", "rep", None),
            P("energy"),
            P(),
            P("slab", "rep", None),
            P("slab", "rep", None),
            P("energy"),
            P("energy"),
            P(),
        ),
        out_specs=(P("energy", "slab", "rep", None), P(None, "slab", "rep", None)),
        check_vma=False,
    )
```
